32 devices in a mesh: dp: 8 (over y, x, core), mp: 4 (over z).
Axes of the slice: x: 2, y: 2, z: 4, core: 2. Of those that a mesh axis runs over, the one named last changes fastest.
Arguments:
- latents: float32 [3, 8192, 1024], P(None, ('dp', 'mp')), may hold values from -6 to 6
- group_ids: int32 [3, 8, 1024], P(None, 'dp'), may hold values from 0 to 15, never falling along the last dimension, each value on 1 to 128 neighbouring positions
- pad_mask: int32 [3, 8, 1024], P(None, 'dp'), may hold values 0 or 1
- w_qkv: bfloat16 [3, 1024, 1024], P(None, 'dp', 'mp'), may hold values from -0.1875 to 0.1875
- w_out: bfloat16 [1024, 1024], P('dp', 'mp'), may hold values from -0.5 to 0.5
- w_up: bfloat16 [1024, 4096], P('dp', 'mp'), may hold values from -0.1875 to 0.1875
- w_down: bfloat16 [1024, 4096], P('dp', 'mp'), may hold values from -0.09375 to 0.09375
- norm_gain: bfloat16 [2, 1024], P(None, 'dp'), may hold values from 0.099609375 to 1.8984375
- norm_bias: bfloat16 [2, 1024], P(None, 'dp'), may hold values from -3 to 3
- out_grad: float32 [3, 8192, 1024], P(None, ('dp', 'mp')), may hold values from -6 to 6
Outputs:
- latents_out: float32 [3, 8192, 1024], P(None, ('dp', 'mp'))
- latents_grad: float32 [3, 8192, 1024], P(None, ('dp', 'mp'))
- grad_qkv: float32 [3, 1024, 1024], P(None, 'dp', 'mp')
- grad_out: float32 [1024, 1024], P('dp', 'mp')
- grad_up: float32 [1024, 4096], P('dp', 'mp')
- grad_down: float32 [1024, 4096], P('dp', 'mp')
- grad_gain: float32 [2, 1024], P(None, 'dp')
- grad_bias: float32 [2, 1024], P(None, 'dp')
The draws below stay inside these ranges and needn't reach their ends.
Inputs may be any that keep to these rules, and one draw needn't show every extreme that they name: `group_ids`: group numbers along one clip never fall; each group of a clip holds 1 to 128 latents and one holds exactly 128.
All inputs are finite; a program needn't handle non-finite values. No bound on the sum of `pad_mask` on one device may be relied on, other than what follows from the above.
Results may differ from the reference program's by a relative error of at most 0.0095.
Values may be sent and summed in bfloat16 or wider, within the bound.
No kernel may reach another device: no remote copies, remote signals or barrier semaphores. Data moves between devices by JAX's collectives and lax.ppermute only.
A program may use at most 192 MiB of HBM per device.

```python
import math
import jax
import jax.numpy as jnp
import numpy as np
from jax import lax

D = 1024
HEADS = 8
HEAD_DIM = 128
FF = 4096
LEN = 1024
GROUPS = 16
GROUP_MAX = 128
MICRO = 3
SEQS = 8
TOKENS = 8192


def with_ends(array, rng, low, largest):
    longest = array.shape.index(max(array.shape))
    spots = []
    for shift in (0, 1):
        where = [jax.random.randint(jax.random.fold_in(rng, axis), (), 0, length) for axis, length in enumerate(array.shape)]
        where[longest] = (where[longest] + shift) % array.shape[longest]
        spots.append(tuple(where))
    return array.at[spots[0]].set(low).at[spots[1]].set(largest)


def levels(stream_key, dims, cuts, least, largest):
    gain, own = 1.0, jax.random.fold_in(stream_key, 6)
    for dim, parts in cuts:
        steps = jnp.exp(jax.random.uniform(jax.random.fold_in(own, dim), (parts,), jnp.float32, least / len(cuts), largest / len(cuts)))
        gain = gain * jnp.repeat(steps, dims[dim] // parts).reshape([-1 if axis == dim else 1 for axis in range(len(dims))])
    return gain


def profile(amount, total, most, slope):
    loads = [(1 << 20) // math.isqrt(standing ** slope) + 1 for standing in range(2, amount + 1)]
    spare, holding = total - most - (amount - 1), [1] * (amount - 1)
    while spare > 0:
        candidates = [i for i in range(amount - 1) if holding[i] < most]
        pool, left = sum([loads[i] for i in candidates]), spare
        for i in candidates:
            extra = min(most - holding[i], max(1, left * loads[i] // pool), spare)
            holding[i] = holding[i] + extra
            spare = spare - extra
    return np.array([most] + holding)


def uneven(rng, amount, total, bound, slope):
    if amount == 2:
        one = jax.random.randint(rng, (), max(1, total - bound), min(bound, total - 1) + 1)
        return jnp.stack([one, total - one])
    sizes = jnp.asarray(profile(amount, total, bound, slope), jnp.int32)
    pairs = (amount - 1) // 2
    donor, taker = sizes[1:1 + 2 * pairs:2], sizes[2:2 + 2 * pairs:2]
    room = jnp.minimum(donor - 1, bound - taker)
    moved = jax.random.randint(jax.random.fold_in(rng, 1), (pairs,), 0, 1 << 20) % (room + 1)
    sizes = sizes.at[1:1 + 2 * pairs:2].set(donor - moved).at[2:2 + 2 * pairs:2].set(taker + moved)
    return sizes[jax.random.permutation(jax.random.fold_in(rng, 2), amount)]


def normal_values(stream_key, dims, spread, reach, shards=(), kind=jnp.bfloat16):
    drawn = spread * jax.random.normal(stream_key, dims, jnp.float32)
    if shards:
        drawn = drawn * levels(stream_key, dims, shards, -0.22, 0.18)
    return jnp.clip(drawn, -reach, reach).astype(kind)


def setup_inputs(seed: int = 0) -> dict:
    arg_keys = jax.random.split(jax.random.key(seed), 11)
    latents = normal_values(arg_keys[0], (MICRO, TOKENS, D), 1.0, 6.0, ((1, 32),), jnp.float32)
    group_ids = jax.vmap(lambda own: jnp.searchsorted(jnp.cumsum(uneven(own, GROUPS, LEN, GROUP_MAX, 2)), jnp.arange(LEN), side="right"))(jax.random.split(arg_keys[1], MICRO * SEQS)).reshape((MICRO, SEQS, LEN)).astype(jnp.int32)
    pad_mask = with_ends((jax.random.randint(arg_keys[2], (MICRO, SEQS, LEN), 0, 4) < 3).astype(jnp.int32), jax.random.fold_in(arg_keys[2], 1), 0, 1)
    w_qkv = normal_values(arg_keys[3], (3, D, D), D ** -0.5, 0.1875, ((1, 8), (2, 4)))
    w_out = normal_values(arg_keys[4], (D, D), (D // 8) ** -0.5, 0.5, ((0, 8), (1, 4)))
    w_up = normal_values(arg_keys[5], (D, FF), D ** -0.5, 0.1875, ((0, 8), (1, 4)))
    w_down = normal_values(arg_keys[6], (D, FF), FF ** -0.5, 0.09375, ((0, 8), (1, 4)))
    norm_gain = jnp.clip(1.0 + 0.18 * jax.random.normal(arg_keys[7], (2, D), jnp.float32), 0.099609375, 1.8984375).astype(jnp.bfloat16)
    norm_bias = normal_values(arg_keys[8], (2, D), 0.5, 3.0, ((1, 8),))
    out_grad = normal_values(arg_keys[9], (MICRO, TOKENS, D), 1.0, 6.0, ((1, 32),), jnp.float32)
    return dict(latents=latents, group_ids=group_ids, pad_mask=pad_mask, w_qkv=w_qkv, w_out=w_out, w_up=w_up, w_down=w_down, norm_gain=norm_gain, norm_bias=norm_bias, out_grad=out_grad)


@jax.custom_vjp
def low(v):
    return lax.optimization_barrier(v.astype(jnp.bfloat16)).astype(jnp.float32)

@jax.custom_vjp
def low_back(v):
    return v

def low_keep(v):
    return (low(v), None)

def low_pass(kept, grad):
    return (grad,)

def back_keep(v):
    return (v, None)

def back_low(kept, grad):
    return (low(grad),)
low.defvjp(low_keep, low_pass)
low_back.defvjp(back_keep, back_low)
epsilon = 1e-05

def norm_rows(values, scaling, offset):
    row_mean = lax.optimization_barrier(jnp.mean(values, axis=-1, keepdims=True))
    centred = values - row_mean
    row_var = lax.optimization_barrier(jnp.mean(centred * centred, axis=-1, keepdims=True))
    return centred * lax.rsqrt(row_var + epsilon) * scaling + offset

def product(left, right):
    return jnp.dot(left, right, precision=lax.Precision.HIGHEST, preferred_element_type=jnp.float32)

def one_sequence(parameters, element):
    qkv_full, out_full, up_full, down_full, gains, offsets = parameters
    latent_rows, group_row, live_row = element
    inputs_a = low(norm_rows(latent_rows, gains[0], offsets[0]))
    queries = low(low_back(product(inputs_a, qkv_full[0]))).reshape(LEN, HEADS, HEAD_DIM)
    keys = low(low_back(product(inputs_a, qkv_full[1]))).reshape(LEN, HEADS, HEAD_DIM)
    values = low(low_back(product(inputs_a, qkv_full[2]))).reshape(LEN, HEADS, HEAD_DIM)
    positions = jnp.arange(LEN, dtype=jnp.int32)
    allowed = (group_row[:, None] == group_row[None, :]) & ((live_row[None, :] == 1) | (positions[:, None] == positions[None, :]))
    scores = low_back(jnp.einsum('qhd,khd->hqk', queries, keys, precision=lax.Precision.HIGHEST) * HEAD_DIM ** (-0.5))
    scores = jnp.where(allowed[None], scores, -1e+30)
    probabilities = low(jax.nn.softmax(scores, axis=-1))
    attended = jnp.einsum('hqk,khd->qhd', probabilities, values, precision=lax.Precision.HIGHEST).reshape(LEN, D)
    attended = low(low_back(attended))
    resid = latent_rows + low_back(product(attended, out_full.T))
    inputs_c = low(norm_rows(resid, gains[1], offsets[1]))
    upward = low_back(product(inputs_c, up_full))
    hidden = low(jax.nn.gelu(upward))
    return resid + low_back(product(hidden, down_full.T))

def reference(latents, group_ids, pad_mask, w_qkv, w_out, w_up, w_down, norm_gain, norm_bias, out_grad):
    parameters = (w_qkv.astype(jnp.float32), w_out.astype(jnp.float32), w_up.astype(jnp.float32), w_down.astype(jnp.float32), norm_gain.astype(jnp.float32), norm_bias.astype(jnp.float32))
    flat_rows = latents.reshape(-1, LEN, D)
    flat_groups = group_ids.reshape(-1, LEN)
    flat_live = pad_mask.reshape(-1, LEN)
    checked = jax.checkpoint(one_sequence)

    def forward(rows_all, params_all):
        return lax.map(lambda element: checked(params_all, element), (rows_all, flat_groups, flat_live))
    result, pullback = jax.vjp(forward, flat_rows, parameters)
    grad_rows, grad_params = pullback(out_grad.reshape(-1, LEN, D))
    return (result.reshape(latents.shape), grad_rows.reshape(latents.shape), grad_params[0], grad_params[1], grad_params[2], grad_params[3], grad_params[4], grad_params[5])
```

```python
import jax
import jax.numpy as jnp
from jax import lax
from jax.sharding import PartitionSpec as P

HEAD_DIM = 128
HALO = 128
EPSILON = 1e-05
LOW = jnp.bfloat16


def dot(left, right, dims, kind=jnp.float32):
    return lax.dot_general(
        left, right, ((dims[:1], dims[1:]), ((), ())), preferred_element_type=kind
    )


def swap(value, bit, count):
    return lax.ppermute(value, "dp", [(i, i ^ bit) for i in range(count)])


def shift(value, step, count):
    return lax.ppermute(value, "mp", [(i, (i + step) % count) for i in range(count)])


class Plan:
    def __init__(self, mesh):
        self.dp = mesh.shape["dp"]
        self.mp = mesh.shape["mp"]
        bits = [1 << i for i in range(self.dp.bit_length() - 1)]
        core, others = bits[:1], bits[1:]
        self.orders = (others + core, others[::-1] + core)
        self.major = core + others[::-1]
        relative = [0]
        for bit in self.major[::-1]:
            relative = relative + [r ^ bit for r in relative]
        self.relative = relative

    def own(self):
        return lax.axis_index("dp")

    def enter(self, value):
        width = value.shape[-1] // self.dp
        axis = value.ndim - 1
        return jnp.concatenate(
            [
                lax.dynamic_slice_in_dim(value, (self.own() ^ r) * width, width, axis)
                for r in self.relative
            ],
            axis=axis,
        )

    def leave(self, value):
        width = value.shape[-1] // self.dp
        axis = value.ndim - 1
        inverse = {r: p for p, r in enumerate(self.relative)}
        table = jnp.array([inverse[r] for r in range(self.dp)], jnp.int32)
        return jnp.concatenate(
            [
                lax.dynamic_slice_in_dim(value, table[self.own() ^ n] * width, width, axis)
                for n in range(self.dp)
            ],
            axis=axis,
        )

    def gather_rows(self, value, order):
        block = value.shape[0]
        known = [0]
        held = [value]
        for i, bit in enumerate(order):
            if i + 3 < len(order):
                held = [jnp.concatenate([held[0], swap(held[0], bit, self.dp)], axis=0)]
            else:
                held = held + [swap(part, bit, self.dp) for part in held]
            known = known + [r ^ bit for r in known]
        spans = held[0].shape[0] // block

        def piece(r):
            at, inner = divmod(known.index(r), spans)
            return held[at] if spans == 1 else held[at][inner * block : (inner + 1) * block]

        return jnp.concatenate([piece(r) for r in self.relative], axis=0)

    def gather(self, local):
        parts = [local] + [shift(local, -k, self.mp) for k in range(1, self.mp)]
        half = self.mp // 2
        return [
            self.gather_rows(jnp.concatenate(parts[i * half : (i + 1) * half], axis=1), order)
            for i, order in enumerate(self.orders)
        ]

    def scatter_rows(self, produce, order):
        first = order[-1]
        rest = order[:-1][::-1]
        sent = produce(1).astype(LOW)
        kept = produce(0) + swap(sent, first, self.dp).astype(jnp.float32)
        left = [bit for bit in self.major if bit != first]
        for bit in rest:
            place = left.index(bit)
            block = kept.shape[0] >> (place + 1)
            shaped = kept.reshape((1 << place), 2, block, kept.shape[1])
            sent = shaped[:, 1].reshape(-1, kept.shape[1]).astype(LOW)
            kept = shaped[:, 0].reshape(-1, kept.shape[1])
            kept = kept + swap(sent, bit, self.dp).astype(jnp.float32)
            left.remove(bit)
        return kept

    def scatter(self, produces):
        half = self.mp // 2
        blocks = []
        for produce, order in zip(produces, self.orders):
            rows = self.scatter_rows(produce, order)
            width = rows.shape[1] // half
            blocks += [rows[:, i * width : (i + 1) * width] for i in range(half)]
        total = blocks[0]
        for k in range(1, self.mp):
            total = total + shift(blocks[k].astype(LOW), k, self.mp).astype(jnp.float32)
        return total


def statistics(values):
    mean = jnp.mean(values, axis=-1, keepdims=True)
    centred = values - mean
    variance = jnp.mean(centred * centred, axis=-1, keepdims=True)
    return centred, lax.rsqrt(variance + EPSILON)


def norm_rows(values, gain, bias):
    centred, scale = statistics(values)
    return centred * scale * gain + bias


def norm_back(values, gain, grad):
    centred, scale = statistics(values)
    normed = centred * scale
    inner = grad * gain
    first = jnp.mean(inner, axis=-1, keepdims=True)
    second = jnp.mean(inner * normed, axis=-1, keepdims=True)
    return (
        (inner - first - normed * second) * scale,
        jnp.sum(grad * normed, axis=0),
        jnp.sum(grad, axis=0),
    )


def halo(value, count):
    before = lax.ppermute(value[:, -HALO:], "mp", [(i, i + 1) for i in range(count - 1)])
    after = lax.ppermute(value[:, :HALO], "mp", [(i + 1, i) for i in range(count - 1)])
    return jnp.concatenate([before, value, after], axis=1)


def solution(mesh):
    plan = Plan(mesh)

    def body(latents, group_ids, pad_mask, w_qkv, w_out, w_up, w_down, norm_gain, norm_bias, out_grad):
        micro, rows, width = latents.shape
        total = micro * rows
        mp = plan.mp
        factor = HEAD_DIM ** (-0.5)
        small = jnp.concatenate([norm_gain, norm_bias], axis=0).T
        small = plan.gather_rows(small, plan.orders[0]).T.astype(jnp.float32)
        gains, biases = small[:2], small[2:]

        local_qkv = jnp.concatenate([w_qkv[t] for t in range(3)], axis=1)
        qkv = plan.gather(local_qkv)
        out = plan.gather(w_out)
        up = plan.gather(w_up)
        down = plan.gather(w_down)

        entered = plan.enter(latents.reshape(total, width))
        grad_rows = plan.enter(out_grad.reshape(total, width))
        grad_z = grad_rows.astype(LOW)
        inputs_a = norm_rows(entered, gains[0], biases[0]).astype(LOW)
        window = halo(inputs_a.reshape(micro, rows, width), mp)
        span = rows + 2 * HALO
        first = lax.axis_index("mp") * rows - HALO
        pads = ((0, 0), (HALO, HALO))
        groups = lax.dynamic_slice_in_dim(
            jnp.pad(group_ids[:, 0], pads, constant_values=-1), first + HALO, span, 1
        )
        live = lax.dynamic_slice_in_dim(jnp.pad(pad_mask[:, 0], pads), first + HALO, span, 1)
        same = groups[:, :, None] == groups[:, None, :]
        diagonal = jnp.eye(span, dtype=bool)
        allowed = same & ((live[:, None, :] == 1) | diagonal[None])

        def heads(values):
            return values.reshape(micro, span, -1, HEAD_DIM)

        shaped = []
        attended = []
        flat_window = window.reshape(micro * span, width)
        for part in qkv:
            projected = dot(flat_window, part, (1, 0)).astype(LOW)
            projected = projected.reshape(micro, span, mp // 2, 3, -1)
            q, k, v = (heads(projected[:, :, :, t]) for t in range(3))
            scores = jnp.einsum(
                "bqhd,bkhd->bhqk", q, k, preferred_element_type=jnp.float32
            )
            scores = jnp.where(allowed[:, None], scores * factor, -1e30)
            peak = jnp.max(scores, axis=-1, keepdims=True)
            weights = jnp.exp(scores - peak)
            probabilities = weights / jnp.sum(weights, axis=-1, keepdims=True)
            mixture = jnp.einsum(
                "bhqk,bkhd->bqhd",
                probabilities[:, :, HALO : HALO + rows].astype(LOW),
                v,
                preferred_element_type=jnp.float32,
            )
            attended.append(mixture.reshape(total, -1).astype(LOW))
            shaped.append((q, k, v, probabilities))
        resid = entered + sum(dot(a, w, (1, 1)) for a, w in zip(attended, out))
        inputs_c = norm_rows(resid, gains[1], biases[1]).astype(LOW)
        hidden, slopes = [], []
        for part in up:
            upward = dot(inputs_c, part, (1, 0))
            value, pull = jax.vjp(jax.nn.gelu, upward)
            hidden.append(value.astype(LOW))
            slopes.append(pull(jnp.ones_like(upward))[0].astype(LOW))

        def rows_of(values, other):
            half = width // 2
            return lambda which: dot(values[:, which * half : (which + 1) * half], other, (0, 0))

        grad_down = plan.scatter([rows_of(grad_z, h) for h in hidden])
        latents_out = resid + sum(dot(h, w, (1, 1)) for h, w in zip(hidden, down))
        grad_upward = [
            (dot(grad_z, w, (1, 0)) * s.astype(jnp.float32)).astype(LOW)
            for w, s in zip(down, slopes)
        ]
        grad_up = plan.scatter([rows_of(inputs_c, g) for g in grad_upward])
        grad_norm_two = sum(dot(g, w, (1, 1)) for g, w in zip(grad_upward, up))
        part_two, gain_two, bias_two = norm_back(resid, gains[1], grad_norm_two)
        grad_resid = grad_rows + part_two
        grad_branch = grad_resid.astype(LOW)
        grad_out = plan.scatter([rows_of(grad_branch, a) for a in attended])
        branch_window = halo(grad_branch.reshape(micro, rows, width), mp)
        branch_window = branch_window.reshape(micro * span, width)
        grad_projected = []
        for (q, k, v, probabilities), w in zip(shaped, out):
            grad_att = heads(dot(branch_window, w, (1, 0)).astype(LOW))
            grad_probs = jnp.einsum(
                "bqhd,bkhd->bhqk", grad_att, v, preferred_element_type=jnp.float32
            )
            weighted = jnp.sum(probabilities * grad_probs, axis=-1, keepdims=True)
            grad_scores = (probabilities * (grad_probs - weighted)).astype(LOW)
            mine = slice(HALO, HALO + rows)
            grad_q = jnp.einsum(
                "bhqk,bkhd->bqhd", grad_scores[:, :, mine], k, preferred_element_type=jnp.float32
            )
            grad_k = jnp.einsum(
                "bhqk,bqhd->bkhd", grad_scores[:, :, :, mine], q, preferred_element_type=jnp.float32
            )
            grad_v = jnp.einsum(
                "bhqk,bqhd->bkhd",
                probabilities[:, :, :, mine].astype(LOW),
                grad_att,
                preferred_element_type=jnp.float32,
            )
            three = [
                (g * f).astype(LOW).reshape(total, mp // 2, -1)
                for g, f in ((grad_q, factor), (grad_k, factor), (grad_v, 1.0))
            ]
            grad_projected.append(jnp.stack(three, axis=2).reshape(total, -1))
        grad_qkv = plan.scatter([rows_of(inputs_a, g) for g in grad_projected])
        grad_qkv = jnp.stack(jnp.split(grad_qkv, 3, axis=1))
        grad_norm_one = sum(dot(g, w, (1, 1)) for g, w in zip(grad_projected, qkv))
        part_one, gain_one, bias_one = norm_back(entered, gains[0], grad_norm_one)
        latents_grad = grad_resid + part_one
        sums = jnp.stack([gain_one, gain_two, bias_one, bias_two]).T
        for bit in plan.major:
            half = sums.shape[0] // 2
            sums = sums[:half] + swap(sums[half:], bit, plan.dp)
        sums = lax.psum(sums, "mp").T
        shape = latents.shape
        return (
            plan.leave(latents_out).reshape(shape),
            plan.leave(latents_grad).reshape(shape),
            grad_qkv,
            grad_out,
            grad_up,
            grad_down,
            sums[:2],
            sums[2:],
        )

    return jax.shard_map(
        body,
        mesh=mesh,
        in_specs=(
            P(None, ("dp", "mp"), None),
            P(None, "dp", None),
            P(None, "dp", None),
            P(None, "dp", "mp"),
            P("dp", "mp"),
            P("dp", "mp"),
            P("dp", "mp"),
            P(None, "dp"),
            P(None, "dp"),
            P(None, ("dp", "mp"), None),
        ),
        out_specs=(
            P(None, ("dp", "mp"), None),
            P(None, ("dp", "mp"), None),
            P(None, "dp", "mp"),
            P("dp", "mp"),
            P("dp", "mp"),
            P("dp", "mp"),
            P(None, "dp"),
            P(None, "dp"),
        ),
        check_vma=False,
    )
```

```python
import jax
import jax.numpy as jnp
from jax import lax
from jax.experimental import pallas as pl
from jax.experimental.pallas import tpu as pltpu
from jax.sharding import PartitionSpec as P

HEAD_DIM = 128
HALO = 128
EPSILON = 1e-05
LOW = jnp.bfloat16


def dot(left, right, dims, kind=jnp.float32):
    return lax.dot_general(
        left, right, ((dims[:1], dims[1:]), ((), ())), preferred_element_type=kind
    )


def swap(value, bit, count):
    return lax.ppermute(value, "dp", [(i, i ^ bit) for i in range(count)])


def shift(value, step, count):
    return lax.ppermute(value, "mp", [(i, (i + step) % count) for i in range(count)])


class Plan:
    def __init__(self, mesh):
        self.dp = mesh.shape["dp"]
        self.mp = mesh.shape["mp"]
        bits = [1 << i for i in range(self.dp.bit_length() - 1)]
        core, others = bits[:1], bits[1:]
        self.orders = (others + core, others[::-1] + core)
        self.major = core + others[::-1]
        relative = [0]
        for bit in self.major[::-1]:
            relative = relative + [r ^ bit for r in relative]
        self.relative = relative

    def own(self):
        return lax.axis_index("dp")

    def enter(self, value):
        width = value.shape[-1] // self.dp
        axis = value.ndim - 1
        return jnp.concatenate(
            [
                lax.dynamic_slice_in_dim(value, (self.own() ^ r) * width, width, axis)
                for r in self.relative
            ],
            axis=axis,
        )

    def leave(self, value):
        width = value.shape[-1] // self.dp
        axis = value.ndim - 1
        inverse = {r: p for p, r in enumerate(self.relative)}
        table = jnp.array([inverse[r] for r in range(self.dp)], jnp.int32)
        return jnp.concatenate(
            [
                lax.dynamic_slice_in_dim(value, table[self.own() ^ n] * width, width, axis)
                for n in range(self.dp)
            ],
            axis=axis,
        )

    def gather_rows(self, value, order):
        block = value.shape[0]
        known = [0]
        held = [value]
        for i, bit in enumerate(order):
            if i + 3 < len(order):
                held = [jnp.concatenate([held[0], swap(held[0], bit, self.dp)], axis=0)]
            else:
                held = held + [swap(part, bit, self.dp) for part in held]
            known = known + [r ^ bit for r in known]
        spans = held[0].shape[0] // block

        def piece(r):
            at, inner = divmod(known.index(r), spans)
            return held[at] if spans == 1 else held[at][inner * block : (inner + 1) * block]

        return jnp.concatenate([piece(r) for r in self.relative], axis=0)

    def gather(self, local):
        parts = [local] + [shift(local, -k, self.mp) for k in range(1, self.mp)]
        half = self.mp // 2
        return [
            self.gather_rows(jnp.concatenate(parts[i * half : (i + 1) * half], axis=1), order)
            for i, order in enumerate(self.orders)
        ]

    def scatter_rows(self, produce, order):
        first = order[-1]
        rest = order[:-1][::-1]
        sent = produce(1).astype(LOW)
        kept = produce(0) + swap(sent, first, self.dp).astype(jnp.float32)
        left = [bit for bit in self.major if bit != first]
        for bit in rest:
            place = left.index(bit)
            block = kept.shape[0] >> (place + 1)
            shaped = kept.reshape((1 << place), 2, block, kept.shape[1])
            sent = shaped[:, 1].reshape(-1, kept.shape[1]).astype(LOW)
            kept = shaped[:, 0].reshape(-1, kept.shape[1])
            kept = kept + swap(sent, bit, self.dp).astype(jnp.float32)
            left.remove(bit)
        return kept

    def scatter(self, produces):
        half = self.mp // 2
        blocks = []
        for produce, order in zip(produces, self.orders):
            rows = self.scatter_rows(produce, order)
            width = rows.shape[1] // half
            blocks += [rows[:, i * width : (i + 1) * width] for i in range(half)]
        total = blocks[0]
        for k in range(1, self.mp):
            total = total + shift(blocks[k].astype(LOW), k, self.mp).astype(jnp.float32)
        return total


MEGA = 1 << 20
LOG2E = 1.4426950408889634


def params(limit=56):
    return pltpu.CompilerParams(vmem_limit_bytes=limit * MEGA)


def cost(flops, bytes_accessed, transcendentals=0):
    return pl.CostEstimate(
        flops=int(flops), bytes_accessed=int(bytes_accessed), transcendentals=int(transcendentals)
    )


def whole(*shape):
    return pl.BlockSpec(shape, lambda *_: (0,) * len(shape))


def statistics(values):
    mean = jnp.mean(values, axis=-1, keepdims=True)
    centred = values - mean
    variance = jnp.mean(centred * centred, axis=-1, keepdims=True)
    return centred, lax.rsqrt(variance + EPSILON)


def norm_rows(values, gain, bias):
    centred, scale = statistics(values)
    return centred * scale * gain + bias


def norm_back(values, gain, grad):
    centred, scale = statistics(values)
    normed = centred * scale
    inner = grad * gain
    first = jnp.mean(inner, axis=-1, keepdims=True)
    second = jnp.mean(inner * normed, axis=-1, keepdims=True)
    return (inner - first - normed * second) * scale, grad * normed, grad


def fold(rows):
    total = rows[:8]
    for i in range(1, rows.shape[0] // 8):
        total = total + rows[i * 8 : i * 8 + 8]
    return total


ROWS = 64


def store_blocks(ref, start, value, table, inverse=None):
    if table is None:
        ref[pl.ds(start, value.shape[0]), :] = value
        return
    count = table.shape[0]
    block = value.shape[1] // count
    for p in range(count):
        at = pl.multiple_of(table[p] * block, block)
        ref[pl.ds(start, value.shape[0]), pl.ds(at, block)] = value[:, p * block : (p + 1) * block]


def load_blocks(ref, start, size, table):
    if table is None:
        return ref[pl.ds(start, size), :]
    count = table.shape[0]
    block = ref.shape[1] // count
    parts = []
    for p in range(count):
        at = pl.multiple_of(table[p] * block, block)
        parts.append(ref[pl.ds(start, size), pl.ds(at, block)])
    return jnp.concatenate(parts, axis=1)


def enter_kernel(blocked):
    def kernel(table_ref, latents, grads, small, entered, entered_grads, grad_z, inputs_a):
        table = table_ref if blocked else None

        @pl.loop(0, latents.shape[0] // ROWS)
        def _(i):
            start = pl.multiple_of(i * ROWS, ROWS)
            at = pl.ds(start, ROWS)
            values = load_blocks(latents, start, ROWS, table)
            entered[at, :] = values
            inputs_a[at, :] = norm_rows(values, small[0:1], small[2:3]).astype(LOW)
            values = load_blocks(grads, start, ROWS, table)
            entered_grads[at, :] = values
            grad_z[at, :] = values.astype(LOW)

    return kernel


def enter_norm(table, blocked, latents, grads, small):
    total, width = latents.shape
    rows = 256
    spec = pl.BlockSpec((rows, width), lambda i, *_: (i, 0))
    shape = lambda kind: jax.ShapeDtypeStruct((total, width), kind)
    return pl.pallas_call(
        enter_kernel(blocked),
        name="enter",
        grid_spec=pltpu.PrefetchScalarGridSpec(
            num_scalar_prefetch=1,
            grid=(total // rows,),
            in_specs=[spec, spec, whole(4, width)],
            out_specs=[spec] * 4,
        ),
        out_shape=[shape(jnp.float32), shape(jnp.float32), shape(LOW), shape(LOW)],
        compiler_params=params(),
        cost_estimate=cost(total * width * 16, total * width * 20),
    )(table, latents, grads, small)


def attention_weights(q, k, bias, factor):
    scores = dot(q, k, (1, 1)) * factor + bias
    peak = jnp.max(scores, axis=-1, keepdims=True)
    weights = jnp.exp(scores - peak)
    return weights / jnp.sum(weights, axis=-1, keepdims=True)


def window_bias(group_column, key_row):
    span = group_column.shape[0]
    place = lax.broadcasted_iota(jnp.int32, (span, span), 0)
    other = lax.broadcasted_iota(jnp.int32, (span, span), 1)
    allowed = (group_column == key_row) | (place == other)
    return jnp.where(allowed, 0.0, -1e30)


def forward_kernel(rows, steps, local_heads, factor):
    def kernel(before, own, after, w_qkv, w_out, column, row, entered, small,
               saved, attended, resid, inputs_c, bias, total):
        step = pl.program_id(1)
        w = w_qkv[...]
        saved[0, 0:HALO] = dot(before[0], w, (1, 0)).astype(LOW)
        saved[0, HALO : HALO + rows] = dot(own[0], w, (1, 0)).astype(LOW)
        saved[0, HALO + rows :] = dot(after[0], w, (1, 0)).astype(LOW)

        @pl.when(step == 0)
        def _():
            bias[...] = window_bias(column[0], row[0])
            total[...] = entered[...]

        group = local_heads * HEAD_DIM
        mine = slice(HALO, HALO + rows)
        for h in range(local_heads):
            at = slice(h * HEAD_DIM, (h + 1) * HEAD_DIM)
            q = saved[0, mine, at]
            k = saved[0, :, group + h * HEAD_DIM : group + (h + 1) * HEAD_DIM]
            v = saved[0, :, 2 * group + h * HEAD_DIM : 2 * group + (h + 1) * HEAD_DIM]
            p = attention_weights(q, k, bias[mine, :], factor).astype(LOW)
            attended[:, at] = dot(p, v, (1, 0)).astype(LOW)
        total[...] += dot(attended[...], w_out[...], (1, 1))

        @pl.when(step == steps - 1)
        def _():
            @pl.loop(0, rows // ROWS)
            def _(i):
                at = pl.ds(pl.multiple_of(i * ROWS, ROWS), ROWS)
                values = total[at, :]
                resid[at, :] = values
                inputs_c[at, :] = norm_rows(values, small[1:2], small[3:4]).astype(LOW)

    return kernel


def forward_block(parts, w_qkv, w_out, column, row, entered, small, mp, factor):
    before, own, after = parts
    micro, rows, width = own.shape
    span = rows + 2 * HALO
    total = micro * rows
    c = w_qkv.shape[1] // mp
    g = w_out.shape[1] // mp
    per = lambda n: pl.BlockSpec((1, n, width), lambda i, k: (i, 0, 0))
    tall = pl.BlockSpec((rows, width), lambda i, k: (i, 0))
    return pl.pallas_call(
        forward_kernel(rows, mp, g // HEAD_DIM, factor),
        name="attention_forward",
        grid=(micro, mp),
        in_specs=[
            per(HALO), per(rows), per(HALO),
            pl.BlockSpec((width, c), lambda i, k: (0, k)),
            pl.BlockSpec((width, g), lambda i, k: (0, k)),
            pl.BlockSpec((1, span, 1), lambda i, k: (i, 0, 0)),
            pl.BlockSpec((1, 1, span), lambda i, k: (i, 0, 0)),
            tall,
            whole(4, width),
        ],
        out_specs=[
            pl.BlockSpec((1, span, c), lambda i, k: (i, 0, k)),
            pl.BlockSpec((rows, g), lambda i, k: (i, k)),
            tall,
            tall,
        ],
        out_shape=[
            jax.ShapeDtypeStruct((micro, span, c * mp), LOW),
            jax.ShapeDtypeStruct((total, g * mp), LOW),
            jax.ShapeDtypeStruct((total, width), jnp.float32),
            jax.ShapeDtypeStruct((total, width), LOW),
        ],
        scratch_shapes=[pltpu.VMEM((span, span), jnp.float32), pltpu.VMEM((rows, width), jnp.float32)],
        compiler_params=params(),
        cost_estimate=cost(
            2 * micro * (span * width * c * mp + total * width * width // micro + 2 * rows * span * width),
            40 * MEGA,
            micro * rows * span * mp * g // HEAD_DIM,
        ),
    )(before, own, after, w_qkv, w_out, column, row, entered, small)


def up_kernel(inputs, weight, hidden, slope):
    u = dot(inputs[...], weight[...], (1, 0))
    c = 0.7978845608028654
    square = u * u
    t = jnp.tanh(u * (c + c * 0.044715 * square))
    half = 0.5 + 0.5 * t
    hidden[...] = (u * half).astype(LOW)
    inner = 0.5 * c + 1.5 * c * 0.044715 * square
    slope[...] = (half + u * inner * (1.0 - t * t)).astype(LOW)


def feed_up(inputs, weight, tile=512):
    total, width = inputs.shape
    ff = weight.shape[1]
    block = pl.BlockSpec((total, tile), lambda j: (0, j))
    return pl.pallas_call(
        up_kernel,
        name="feed_up",
        grid=(ff // tile,),
        in_specs=[whole(total, width), pl.BlockSpec((width, tile), lambda j: (0, j))],
        out_specs=[block, block],
        out_shape=[jax.ShapeDtypeStruct((total, ff), LOW)] * 2,
        compiler_params=params(),
        cost_estimate=cost(2 * total * width * ff, 2 * (width * ff + 2 * total * ff), total * ff),
    )(inputs, weight)


def down_kernel(blocked, steps):
    def kernel(table_ref, hidden, weight, resid, out, total):
        step = pl.program_id(0)
        part = dot(hidden[...], weight[...], (1, 1))

        @pl.when(step == 0)
        def _():
            total[...] = resid[...] + part

        @pl.when(step > 0)
        def _():
            total[...] += part

        @pl.when(step == steps - 1)
        def _():
            @pl.loop(0, total.shape[0] // ROWS)
            def _(i):
                start = pl.multiple_of(i * ROWS, ROWS)
                store_blocks(out, start, total[pl.ds(start, ROWS), :], table_ref if blocked else None)

    return kernel


def feed_down(table, blocked, hidden, weight, resid, tile=512):
    total, width = resid.shape
    ff = weight.shape[1]
    return pl.pallas_call(
        down_kernel(blocked, ff // tile),
        name="feed_down",
        grid_spec=pltpu.PrefetchScalarGridSpec(
            num_scalar_prefetch=1,
            grid=(ff // tile,),
            in_specs=[
                pl.BlockSpec((total, tile), lambda j, *_: (0, j)),
                pl.BlockSpec((width, tile), lambda j, *_: (0, j)),
                whole(total, width),
            ],
            out_specs=whole(total, width),
            scratch_shapes=[pltpu.VMEM((total, width), jnp.float32)],
        ),
        out_shape=jax.ShapeDtypeStruct((total, width), jnp.float32),
        compiler_params=params(),
        cost_estimate=cost(2 * total * width * ff, 2 * (width * ff + total * ff) + 8 * total * width),
    )(table, hidden, weight, resid)


def feed_back_kernel(steps):
    def kernel(grad_z, down, up, slope, resid, grads, small, grad_upward, grad_resid, grad_branch, sums, total):
        step = pl.program_id(0)
        grad = dot(grad_z[...], down[...], (1, 0)) * slope[...].astype(jnp.float32)
        grad_upward[...] = grad.astype(LOW)
        part = dot(grad_upward[...], up[...], (1, 1))

        @pl.when(step == 0)
        def _():
            total[...] = part

        @pl.when(step > 0)
        def _():
            total[...] += part

        @pl.when(step == steps - 1)
        def _():
            sums[...] = jnp.zeros_like(sums)

            @pl.loop(0, total.shape[0] // ROWS)
            def _(i):
                at = pl.ds(pl.multiple_of(i * ROWS, ROWS), ROWS)
                back, by_gain, by_bias = norm_back(resid[at, :], small[1:2], total[at, :])
                back = back + grads[at, :]
                grad_resid[at, :] = back
                grad_branch[at, :] = back.astype(LOW)
                sums[0:8] += fold(by_gain)
                sums[8:16] += fold(by_bias)

    return kernel


def feed_back(grad_z, down, up, slope, resid, grads, small, tile=512):
    total, width = resid.shape
    ff = up.shape[1]
    wide = pl.BlockSpec((width, tile), lambda j: (0, j))
    block = pl.BlockSpec((total, tile), lambda j: (0, j))
    full = whole(total, width)
    return pl.pallas_call(
        feed_back_kernel(ff // tile),
        name="feed_back",
        grid=(ff // tile,),
        in_specs=[full, wide, wide, block, full, full, whole(4, width)],
        out_specs=[block, full, full, whole(16, width)],
        out_shape=[
            jax.ShapeDtypeStruct((total, ff), LOW),
            jax.ShapeDtypeStruct((total, width), jnp.float32),
            jax.ShapeDtypeStruct((total, width), LOW),
            jax.ShapeDtypeStruct((16, width), jnp.float32),
        ],
        scratch_shapes=[pltpu.VMEM((total, width), jnp.float32)],
        compiler_params=params(),
        cost_estimate=cost(4 * total * width * ff, 4 * (width * ff + total * ff) + 14 * total * width),
    )(grad_z, down, up, slope, resid, grads, small)


def backward_kernel(rows, steps, micro, local_heads, factor, blocked):
    def kernel(table_ref, before, own, after, w_qkv, w_out, column, row, saved, entered, grad_resid, small,
               grad_projected, latents_grad, sums, bias, total, grad_att):
        index, step = pl.program_id(0), pl.program_id(1)
        w = w_out[...]
        grad_att[0:HALO] = dot(before[0], w, (1, 0)).astype(LOW)
        grad_att[HALO : HALO + rows] = dot(own[0], w, (1, 0)).astype(LOW)
        grad_att[HALO + rows :] = dot(after[0], w, (1, 0)).astype(LOW)

        @pl.when(step == 0)
        def _():
            bias[...] = window_bias(column[0], row[0])

        group = local_heads * HEAD_DIM
        mine = slice(HALO, HALO + rows)
        for h in range(local_heads):
            at = slice(h * HEAD_DIM, (h + 1) * HEAD_DIM)
            at_k = slice(group + h * HEAD_DIM, group + (h + 1) * HEAD_DIM)
            at_v = slice(2 * group + h * HEAD_DIM, 2 * group + (h + 1) * HEAD_DIM)
            q, k, v = saved[0, :, at], saved[0, :, at_k], saved[0, :, at_v]
            grad_mix = grad_att[:, at]
            p = attention_weights(q, k, bias[...], factor)
            grad_p = dot(grad_mix, v, (1, 1))
            weighted = jnp.sum(p * grad_p, axis=-1, keepdims=True)
            grad_s = (p * (grad_p - weighted)).astype(LOW)
            grad_projected[:, at] = (dot(grad_s[mine], k, (1, 0)) * factor).astype(LOW)
            grad_projected[:, at_k] = (dot(grad_s[:, mine], q, (0, 0)) * factor).astype(LOW)
            grad_projected[:, at_v] = dot(p[:, mine].astype(LOW), grad_mix, (0, 0)).astype(LOW)
        part = dot(grad_projected[...], w_qkv[...], (1, 1))

        @pl.when(step == 0)
        def _():
            total[...] = part

        @pl.when(step > 0)
        def _():
            total[...] += part

        @pl.when((index == 0) & (step == 0))
        def _():
            sums[...] = jnp.zeros_like(sums)

        @pl.when(step == steps - 1)
        def _():
            @pl.loop(0, rows // ROWS)
            def _(i):
                start = pl.multiple_of(i * ROWS, ROWS)
                at = pl.ds(start, ROWS)
                back, by_gain, by_bias = norm_back(entered[at, :], small[0:1], total[at, :])
                store_blocks(latents_grad, start, back + grad_resid[at, :], table_ref if blocked else None)
                sums[0:8] += fold(by_gain)
                sums[8:16] += fold(by_bias)

    return kernel


def backward_block(table, blocked, parts, w_qkv, w_out, column, row, saved, entered, grad_resid, small, mp, factor):
    before, own, after = parts
    micro, rows, width = own.shape
    span = rows + 2 * HALO
    total = micro * rows
    c = w_qkv.shape[1] // mp
    g = w_out.shape[1] // mp
    per = lambda n: pl.BlockSpec((1, n, width), lambda i, k, *_: (i, 0, 0))
    tall = pl.BlockSpec((rows, width), lambda i, k, *_: (i, 0))
    return pl.pallas_call(
        backward_kernel(rows, mp, micro, g // HEAD_DIM, factor, blocked),
        name="attention_backward",
        grid_spec=pltpu.PrefetchScalarGridSpec(
            num_scalar_prefetch=1,
            grid=(micro, mp),
            in_specs=[
                per(HALO), per(rows), per(HALO),
                pl.BlockSpec((width, c), lambda i, k, *_: (0, k)),
                pl.BlockSpec((width, g), lambda i, k, *_: (0, k)),
                pl.BlockSpec((1, span, 1), lambda i, k, *_: (i, 0, 0)),
                pl.BlockSpec((1, 1, span), lambda i, k, *_: (i, 0, 0)),
                pl.BlockSpec((1, span, c), lambda i, k, *_: (i, 0, k)),
                tall,
                tall,
                whole(4, width),
            ],
            out_specs=[
                pl.BlockSpec((rows, c), lambda i, k, *_: (i, k)),
                tall,
                whole(16, width),
            ],
            scratch_shapes=[
                pltpu.VMEM((span, span), jnp.float32),
                pltpu.VMEM((rows, width), jnp.float32),
                pltpu.VMEM((span, g), LOW),
            ],
        ),
        out_shape=[
            jax.ShapeDtypeStruct((total, c * mp), LOW),
            jax.ShapeDtypeStruct((total, width), jnp.float32),
            jax.ShapeDtypeStruct((16, width), jnp.float32),
        ],
        compiler_params=params(),
        cost_estimate=cost(
            2 * micro * (span * width * width + rows * width * c * mp + 4 * span * span * width),
            50 * MEGA,
            micro * span * span * mp * g // HEAD_DIM,
        ),
    )(table, before, own, after, w_qkv, w_out, column, row, saved, entered, grad_resid, small)


def halo(value, count):
    before = lax.ppermute(value[:, -HALO:], "mp", [(i, i + 1) for i in range(count - 1)])
    after = lax.ppermute(value[:, :HALO], "mp", [(i + 1, i) for i in range(count - 1)])
    return before, value, after


def solution(mesh):
    plan = Plan(mesh)

    def body(latents, group_ids, pad_mask, w_qkv, w_out, w_up, w_down, norm_gain, norm_bias, out_grad):
        micro, rows, width = latents.shape
        total = micro * rows
        mp = plan.mp
        factor = HEAD_DIM ** (-0.5)
        small = jnp.concatenate([norm_gain, norm_bias], axis=0).T
        small = plan.gather_rows(small, plan.orders[0]).T.astype(jnp.float32)

        local_qkv = jnp.concatenate([w_qkv[t] for t in range(3)], axis=1)
        qkv = jnp.concatenate(plan.gather(local_qkv), axis=1)
        out = jnp.concatenate(plan.gather(w_out), axis=1)
        up = jnp.concatenate(plan.gather(w_up), axis=1)
        down = jnp.concatenate(plan.gather(w_down), axis=1)

        blocked = width // plan.dp % 128 == 0
        table = plan.own() ^ jnp.array(plan.relative, jnp.int32)
        rows_in = (latents.reshape(total, width), out_grad.reshape(total, width))
        if not blocked:
            rows_in = tuple(plan.enter(v) for v in rows_in)
        entered, grad_rows, grad_z, inputs_a = enter_norm(table, blocked, *rows_in, small)
        window = halo(inputs_a.reshape(micro, rows, width), mp)
        span = rows + 2 * HALO
        first = lax.axis_index("mp") * rows
        pads = ((0, 0), (HALO, HALO))
        groups = jnp.pad(group_ids[:, 0], pads, constant_values=-1)
        keys = jnp.where(jnp.pad(pad_mask[:, 0], pads) == 1, groups, -2)
        groups = lax.dynamic_slice_in_dim(groups, first, span, 1)
        keys = lax.dynamic_slice_in_dim(keys, first, span, 1)
        column, row = groups[:, :, None], keys[:, None, :]

        saved, attended, resid, inputs_c = forward_block(
            window, qkv, out, column, row, entered, small, mp, factor
        )
        hidden, slope = feed_up(inputs_c, up)

        def scatter(left, right):
            half, part = left.shape[1] // 2, right.shape[1] // 2

            def rows_of(i):
                other = right[:, i * part : (i + 1) * part]
                return lambda which: dot(left[:, which * half : (which + 1) * half], other, (0, 0))

            return plan.scatter([rows_of(0), rows_of(1)])

        grad_down = scatter(grad_z, hidden)
        latents_out = feed_down(table, blocked, hidden, down, resid)
        grad_upward, grad_resid, grad_branch, sums_two = feed_back(
            grad_z, down, up, slope, resid, grad_rows, small
        )
        grad_up = scatter(inputs_c, grad_upward)
        branch = halo(grad_branch.reshape(micro, rows, width), mp)
        grad_out = scatter(grad_branch, attended)
        grad_projected, latents_grad, sums_one = backward_block(
            table, blocked, branch, qkv, out, column, row, saved, entered, grad_resid, small, mp, factor
        )
        grad_qkv = scatter(inputs_a, grad_projected)
        grad_qkv = jnp.stack(jnp.split(grad_qkv, 3, axis=1))
        sums = jnp.stack([sums_one, sums_two], axis=0).reshape(2, 2, 8, width).sum(axis=2)
        sums = sums.transpose(1, 0, 2).reshape(4, width).T
        for bit in plan.major:
            half = sums.shape[0] // 2
            sums = sums[:half] + swap(sums[half:], bit, plan.dp)
        sums = lax.psum(sums, "mp").T
        if not blocked:
            latents_out, latents_grad = plan.leave(latents_out), plan.leave(latents_grad)
        shape = latents.shape
        return (
            latents_out.reshape(shape),
            latents_grad.reshape(shape),
            grad_qkv,
            grad_out,
            grad_up,
            grad_down,
            sums[:2],
            sums[2:],
        )

    return jax.shard_map(
        body,
        mesh=mesh,
        in_specs=(
            P(None, ("dp", "mp"), None),
            P(None, "dp", None),
            P(None, "dp", None),
            P(None, "dp", "mp"),
            P("dp", "mp"),
            P("dp", "mp"),
            P("dp", "mp"),
            P(None, "dp"),
            P(None, "dp"),
            P(None, ("dp", "mp"), None),
        ),
        out_specs=(
            P(None, ("dp", "mp"), None),
            P(None, ("dp", "mp"), None),
            P(None, "dp", "mp"),
            P("dp", "mp"),
            P("dp", "mp"),
            P("dp", "mp"),
            P(None, "dp"),
            P(None, "dp"),
        ),
        check_vma=False,
    )
```

```python
import jax
import jax.numpy as jnp
from jax import lax
from jax.experimental import pallas as pl
from jax.experimental.pallas import tpu as pltpu
from jax.sharding import PartitionSpec as P

HEAD_DIM = 128
HALO = 128
EPSILON = 1e-05
LOW = jnp.bfloat16


def dot(left, right, dims, kind=jnp.float32):
    return lax.dot_general(
        left, right, ((dims[:1], dims[1:]), ((), ())), preferred_element_type=kind
    )


class Links:
    def __init__(self, dp, mp):
        self.dp, self.mp = dp, mp
        self.last = {}

    def send(self, value, axis, pairs, link, depth):
        before = self.last.setdefault(link, [])
        if depth and len(before) >= depth:
            value, _ = lax.optimization_barrier((value, before[-depth]))
        result = lax.ppermute(value, axis, pairs)
        before.append(result)
        return result

    def swap(self, value, bit, depth=0):
        return self.send(value, "dp", [(i, i ^ bit) for i in range(self.dp)], bit, depth)

    def shift(self, value, step, depth=3):
        pairs = [(i, (i + step) % self.mp) for i in range(self.mp)]
        return self.send(value, "mp", pairs, "z", depth)

    def halo(self, value, depth=0):
        count = self.mp
        before = self.send(value[:, -HALO:], "mp", [(i, i + 1) for i in range(count - 1)], "z", depth)
        after = self.send(value[:, :HALO], "mp", [(i + 1, i) for i in range(count - 1)], "z", depth)
        return before, value, after


class Plan:
    def __init__(self, mesh):
        self.dp = mesh.shape["dp"]
        self.mp = mesh.shape["mp"]
        bits = [1 << i for i in range(self.dp.bit_length() - 1)]
        core, others = bits[:1], bits[1:]
        self.orders = (others + core, others[::-1] + core)
        self.major = core + others[::-1]
        relative = [0]
        for bit in self.major[::-1]:
            relative = relative + [r ^ bit for r in relative]
        self.relative = relative

    def own(self):
        return lax.axis_index("dp")

    def enter(self, value):
        width = value.shape[-1] // self.dp
        axis = value.ndim - 1
        return jnp.concatenate(
            [
                lax.dynamic_slice_in_dim(value, (self.own() ^ r) * width, width, axis)
                for r in self.relative
            ],
            axis=axis,
        )

    def leave(self, value):
        width = value.shape[-1] // self.dp
        axis = value.ndim - 1
        inverse = {r: p for p, r in enumerate(self.relative)}
        table = jnp.array([inverse[r] for r in range(self.dp)], jnp.int32)
        return jnp.concatenate(
            [
                lax.dynamic_slice_in_dim(value, table[self.own() ^ n] * width, width, axis)
                for n in range(self.dp)
            ],
            axis=axis,
        )

    def gather_small(self, links, value):
        for bit in self.major[::-1]:
            value = jnp.concatenate([value, links.swap(value, bit, 0)], axis=0)
        return value

    def spread_columns(self, links, local):
        parts = [local] + [links.shift(local, -k, 0) for k in range(1, self.mp)]
        return self.halves(parts)

    def halves(self, parts):
        half = self.mp // 2
        return [jnp.concatenate(parts[i * half : (i + 1) * half], axis=1) for i in range(2)]


class Gather:
    def __init__(self, plan, links, held):
        self.plan, self.links = plan, links
        self.block = held[0].shape[0]
        self.held = [[h] for h in held]
        self.known = [[0], [0]]
        self.steps = [list(order[:-1]) for order in plan.orders]

    def pieces(self, i, order):
        span = self.held[i][0].shape[0] // self.block
        at = [self.known[i].index(r) for r in order]
        pieces = []
        while at:
            n = at.pop(0)
            count = 1
            while at and at[0] == n + count and (n + count) % span:
                at.pop(0)
                count += 1
            held = self.held[i][n // span]
            first = n % span * self.block
            pieces.append(held if count == span else held[first : first + count * self.block])
        return pieces

    def join(self, i, order):
        pieces = self.pieces(i, order)
        return pieces[0] if len(pieces) == 1 else jnp.concatenate(pieces, axis=0)

    def step(self, tokens=()):
        for i in range(2):
            bit = self.steps[i][0]
            value = self.join(i, self.known[i])
            self.held[i] = [value, self.links.swap(after(value, *tokens), bit)]
            self.known[i] = self.known[i] + [r ^ bit for r in self.known[i]]
            self.steps[i] = self.steps[i][1:]
        return [h[1] for h in self.held]

    def steps_but_last(self, tokens=()):
        received = []
        while len(self.steps[0]) > 1:
            received = self.step(tokens)
        return received

    def hold(self, tokens):
        for i in range(2):
            self.held[i][1] = after(self.held[i][1], *tokens)

    def finish(self):
        order = self.plan.relative[: self.plan.dp // 2]
        mine = [self.join(i, order) for i in range(2)]
        return [(m, self.links.swap(m, self.plan.major[0])) for m in mine]


class Scatter:
    def __init__(self, plan, links, pairs):
        self.plan, self.links = plan, links
        self.pairs = pairs
        self.kept = [None, None]
        self.bits = [list(order[:-1][::-1]) for order in plan.orders]
        self.remain = [list(plan.major[1:]), list(plan.major[1:])]

    def core(self, i):
        self.kept[i] = []
        for left, rights in self.pairs:
            middle = left.shape[1] // 2
            sent = dot(left[:, middle:], rights[i], (0, 0)).astype(LOW)
            kept = dot(left[:, :middle], rights[i], (0, 0))
            self.kept[i].append((kept, self.links.swap(sent, self.plan.major[0])))

    def hold(self, i, tokens):
        self.kept[i] = [(k, after(r, *tokens)) for k, r in self.kept[i]]

    def add(self, i):
        self.kept[i] = [
            k[0] + k[1].astype(jnp.float32) if isinstance(k, tuple) else k for k in self.kept[i]
        ]
        return self.kept[i]

    def step(self, i, tokens=()):
        values = self.add(i)
        bit = self.bits[i].pop(0)
        block = values[0].shape[0] >> (self.remain[i].index(bit) + 1)
        shaped = [v.reshape(-1, 2, block, v.shape[1]) for v in values]
        out = [x[:, 1].reshape(-1, v.shape[1]).astype(LOW) for x, v in zip(shaped, values)]
        stay = [x[:, 0].reshape(-1, v.shape[1]) for x, v in zip(shaped, values)]
        out = out[0] if len(out) == 1 else jnp.concatenate(out, axis=1)
        received = self.links.swap(after(out, *tokens), bit)
        self.kept[i], at = [], 0
        for x in stay:
            self.kept[i].append((x, received[:, at : at + x.shape[1]]))
            at += x.shape[1]
        self.remain[i].remove(bit)
        return out

    def steps_but_last(self, i, tokens=()):
        out = None
        while len(self.bits[i]) > 1:
            out = self.step(i, tokens)
        return out

    def rows(self):
        half = self.plan.mp // 2
        result = []
        for pair in zip(*[self.add(i) for i in range(2)]):
            width = pair[0].shape[1] // half
            result.append([r[:, j * width : (j + 1) * width] for r in pair for j in range(half)])
        return result

    def shifts(self, natural, tokens=()):
        mp = self.plan.mp
        products = self.rows()
        own = lax.axis_index("mp")
        for n, rows in enumerate(products):
            if natural[n]:
                joined = jnp.stack(rows)
                products[n] = [
                    lax.dynamic_index_in_dim(joined, lax.rem(own + k, mp), 0, keepdims=False)
                    for k in range(mp)
                ]
        self.total = [rows[0] for rows in products]
        outs = []
        for k in range(1, mp):
            out = [rows[k].astype(LOW) for rows in products]
            outs.append(out[0] if len(out) == 1 else jnp.concatenate(out, axis=1))
        self.received = [
            self.links.shift(after(value, *tokens), k + 1, 0) for k, value in enumerate(outs)
        ]
        return outs

    def finish(self):
        result, at = [], 0
        for total in self.total:
            for part in self.received:
                total = total + part[:, at : at + total.shape[1]].astype(jnp.float32)
            result.append(total)
            at += total.shape[1]
        return result

    def reduce_columns(self):
        joined = jnp.stack(self.rows()[0])
        return lax.psum_scatter(joined, "mp", scatter_dimension=0, tiled=False)


def after(value, *tokens):
    if not tokens:
        return value
    return lax.optimization_barrier((value, *tokens))[0]


def split_dot(left, top, bottom):
    half = top.shape[0]
    return dot(left[:, :half], top, (1, 0)) + dot(left[:, half:], bottom, (1, 0))


MEGA = 1 << 20
LOG2E = 1.4426950408889634
VM_FWD = 36
VM_UP = 20
VM_DOWN = 20
VM_BACK = 32
VM_BWD = 36
VM_ENTER = 20


def params(limit=56):
    return pltpu.CompilerParams(vmem_limit_bytes=limit * MEGA)


def cost(flops, bytes_accessed, transcendentals=0):
    return pl.CostEstimate(
        flops=int(flops), bytes_accessed=int(bytes_accessed), transcendentals=int(transcendentals)
    )


def whole(*shape):
    return pl.BlockSpec(shape, lambda *_: (0,) * len(shape), pipeline_mode=pl.Buffered(1))


def statistics(values):
    mean = jnp.mean(values, axis=-1, keepdims=True)
    centred = values - mean
    variance = jnp.mean(centred * centred, axis=-1, keepdims=True)
    return centred, lax.rsqrt(variance + EPSILON)


def norm_rows(values, gain, bias):
    centred, scale = statistics(values)
    return centred * scale * gain + bias


def norm_back(values, gain, grad):
    centred, scale = statistics(values)
    normed = centred * scale
    inner = grad * gain
    first = jnp.mean(inner, axis=-1, keepdims=True)
    second = jnp.mean(inner * normed, axis=-1, keepdims=True)
    return (inner - first - normed * second) * scale, grad * normed, grad


def fold(rows):
    total = rows[:8]
    for i in range(1, rows.shape[0] // 8):
        total = total + rows[i * 8 : i * 8 + 8]
    return total


ROWS = 64


def store_blocks(ref, start, value, table, inverse=None):
    if table is None:
        ref[pl.ds(start, value.shape[0]), :] = value
        return
    count = table.shape[0]
    block = value.shape[1] // count
    for p in range(count):
        at = pl.multiple_of(table[p] * block, block)
        ref[pl.ds(start, value.shape[0]), pl.ds(at, block)] = value[:, p * block : (p + 1) * block]


def load_blocks(ref, start, size, table):
    if table is None:
        return ref[pl.ds(start, size), :]
    count = table.shape[0]
    block = ref.shape[1] // count
    parts = []
    for p in range(count):
        at = pl.multiple_of(table[p] * block, block)
        parts.append(ref[pl.ds(start, size), pl.ds(at, block)])
    return jnp.concatenate(parts, axis=1)


def enter_kernel(blocked):
    def kernel(table_ref, latents, grads, small, entered, entered_grads, grad_z, inputs_a):
        table = table_ref if blocked else None

        @pl.loop(0, latents.shape[0] // ROWS)
        def _(i):
            start = pl.multiple_of(i * ROWS, ROWS)
            at = pl.ds(start, ROWS)
            values = load_blocks(latents, start, ROWS, table)
            entered[at, :] = values
            inputs_a[at, :] = norm_rows(values, small[0:1], small[2:3]).astype(LOW)
            values = load_blocks(grads, start, ROWS, table)
            entered_grads[at, :] = values
            grad_z[at, :] = values.astype(LOW)

    return kernel


def enter_norm(table, blocked, latents, grads, small):
    total, width = latents.shape
    rows = 256
    spec = pl.BlockSpec((rows, width), lambda i, *_: (i, 0))
    shape = lambda kind: jax.ShapeDtypeStruct((total, width), kind)
    return pl.pallas_call(
        enter_kernel(blocked),
        name="enter",
        grid_spec=pltpu.PrefetchScalarGridSpec(
            num_scalar_prefetch=1,
            grid=(total // rows,),
            in_specs=[spec, spec, whole(4, width)],
            out_specs=[spec] * 4,
        ),
        out_shape=[shape(jnp.float32), shape(jnp.float32), shape(LOW), shape(LOW)],
        compiler_params=params(VM_ENTER),
        cost_estimate=cost(total * width * 16, total * width * 20),
    )(table, latents, grads, small)


def attention_weights(q, k, bias, factor):
    scores = dot(q, k, (1, 1)) * (factor * LOG2E) + bias
    peak = jnp.max(scores, axis=-1, keepdims=True)
    weights = jnp.exp2(scores - peak)
    return weights * (1.0 / jnp.sum(weights, axis=-1, keepdims=True))


def window_bias(group_column, key_row):
    span = group_column.shape[0]
    place = lax.broadcasted_iota(jnp.int32, (span, span), 0)
    other = lax.broadcasted_iota(jnp.int32, (span, span), 1)
    allowed = (group_column == key_row) | (place == other)
    return jnp.where(allowed, 0.0, -1e30)


def column_halves(rows, tile, count):
    return (
        pl.BlockSpec((rows, tile), lambda k, *_: (0, jnp.minimum(k, count - 1))),
        pl.BlockSpec((rows, tile), lambda k, *_: (0, jnp.clip(k - count, 0, count - 1))),
    )


def either(step, count, work, first, second):
    @pl.when(step < count)
    def _():
        work(*first)

    @pl.when((step >= count) & (step < 2 * count))
    def _():
        work(*second)


def project(window, w_top, w_bottom, target, index, rows):
    before, own, after = window
    target[0:HALO] = split_dot(before[index], w_top, w_bottom).astype(LOW)
    target[HALO : HALO + rows] = split_dot(own[index], w_top, w_bottom).astype(LOW)
    target[HALO + rows :] = split_dot(after[index], w_top, w_bottom).astype(LOW)


def forward_kernel(rows, steps, local_heads, factor):
    def kernel(before, own, after, top_a, bottom_a, top_b, bottom_b, column, row, start, small,
               saved, attended, resid, inputs_c, bias, total):
        step, index = pl.program_id(0), pl.program_id(1)
        group = local_heads * HEAD_DIM
        wide = 3 * group
        half = top_a.shape[0]
        target = saved.at[0]

        @pl.when(step == 0)
        def _():
            bias[index] = window_bias(column[index], row[index])
            total[index] = jnp.zeros((rows, 2 * half), jnp.float32)

        mine = slice(HALO, HALO + rows)

        def work(top, bottom):
            project((before, own, after), top[:, :wide], bottom[:, :wide], target, index, rows)
            for h in range(local_heads):
                at = slice(h * HEAD_DIM, (h + 1) * HEAD_DIM)
                q = target[mine, at]
                k = target[:, group + h * HEAD_DIM : group + (h + 1) * HEAD_DIM]
                v = target[:, 2 * group + h * HEAD_DIM : 2 * group + (h + 1) * HEAD_DIM]
                p = attention_weights(q, k, bias[index, mine, :], factor).astype(LOW)
                attended[0, :, at] = dot(p, v, (1, 0)).astype(LOW)
            total[index, :, :half] += dot(attended[0], top[:, wide:], (1, 1))
            total[index, :, half:] += dot(attended[0], bottom[:, wide:], (1, 1))

        @pl.when(step < steps // 2)
        def _():
            work(top_a, bottom_a)

        @pl.when(step >= steps // 2)
        def _():
            work(top_b, bottom_b)

        @pl.when(step == steps - 1)
        def _():
            @pl.loop(0, rows // ROWS)
            def _(i):
                at = pl.ds(pl.multiple_of(i * ROWS, ROWS), ROWS)
                values = total[index, at, :] + start[at, :]
                resid[at, :] = values
                inputs_c[at, :] = norm_rows(values, small[1:2], small[3:4]).astype(LOW)

    return kernel


def forward_block(window, weights, column, row, start, small, steps, factor):
    before, own, after = window
    micro, rows, width = own.shape
    span = rows + 2 * HALO
    total = micro * rows
    half = steps // 2
    c = weights[0][0].shape[1] // half
    g = c // 4
    late = pl.BlockSpec((rows, width), lambda k, i: (jnp.where(k == steps - 1, i, 0), 0))
    weight_a, weight_b = column_halves(width // 2, c, half)
    return pl.pallas_call(
        forward_kernel(rows, steps, g // HEAD_DIM, factor),
        name="attention_forward",
        grid=(steps, micro),
        in_specs=[
            whole(*before.shape), whole(*own.shape), whole(*after.shape),
            weight_a, weight_a, weight_b, weight_b,
            whole(*column.shape), whole(*row.shape),
            late,
            whole(4, width),
        ],
        out_specs=[
            pl.BlockSpec((1, span, 3 * g), lambda k, i: (i, 0, k)),
            pl.BlockSpec((1, rows, g), lambda k, i: (k // half, i, k % half)),
            late,
            late,
        ],
        out_shape=[
            jax.ShapeDtypeStruct((micro, span, 3 * g * steps), LOW),
            jax.ShapeDtypeStruct((2, total, g * half), LOW),
            jax.ShapeDtypeStruct((total, width), jnp.float32),
            jax.ShapeDtypeStruct((total, width), LOW),
        ],
        scratch_shapes=[
            pltpu.VMEM((micro, span, span), jnp.float32),
            pltpu.VMEM((micro, rows, width), jnp.float32),
        ],
        compiler_params=params(VM_FWD),
        cost_estimate=cost(
            2 * micro * steps * g * (span * width * 3 + rows * width + 2 * rows * span),
            30 * MEGA,
            micro * rows * span * steps * g // HEAD_DIM,
        ),
    )(before, own, after, *weights[0], *weights[1], column, row, start, small)


def up_kernel(count):
    def kernel(inputs, top_a, bottom_a, top_b, bottom_b, hidden, slope):
        def work(top, bottom):
            u = split_dot(inputs[...], top[...], bottom[...])
            c = 0.7978845608028654
            square = u * u
            t = jnp.tanh(u * (c + c * 0.044715 * square))
            half = 0.5 + 0.5 * t
            hidden[0] = (u * half).astype(LOW)
            inner = 0.5 * c + 1.5 * c * 0.044715 * square
            slope[0] = (half + u * inner * (1.0 - t * t)).astype(LOW)

        either(pl.program_id(0), count, work, (top_a, bottom_a), (top_b, bottom_b))

    return kernel


def feed_up(inputs, weights, tile=512):
    total, width = inputs.shape
    ff = 2 * weights[0][0].shape[1]
    count = ff // 2 // tile
    block = pl.BlockSpec((1, total, tile), lambda j: (j // count, 0, j % count))
    weight_a, weight_b = column_halves(width // 2, tile, count)
    return pl.pallas_call(
        up_kernel(count),
        name="feed_up",
        grid=(ff // tile,),
        in_specs=[whole(total, width), weight_a, weight_a, weight_b, weight_b],
        out_specs=[block, block],
        out_shape=[jax.ShapeDtypeStruct((2, total, ff // 2), LOW)] * 2,
        compiler_params=params(VM_UP),
        cost_estimate=cost(2 * total * width * ff, 2 * (width * ff + 2 * total * ff), total * ff),
    )(inputs, *weights[0], *weights[1])


LATE = 256


def down_kernel(blocked, steps):
    def kernel(table_ref, hidden, top_a, bottom_a, top_b, bottom_b, start_rows, out, total):
        step = pl.program_id(0)
        half = top_a.shape[0]

        @pl.when(step == 0)
        def _():
            total[...] = jnp.zeros_like(total)

        def work(top, bottom):
            total[:, :half] += dot(hidden[0], top[...], (1, 1))
            total[:, half:] += dot(hidden[0], bottom[...], (1, 1))

        either(step, steps // 2, work, (top_a, bottom_a), (top_b, bottom_b))

        @pl.when(step >= steps)
        def _():
            base = (step - steps) * LATE

            @pl.loop(0, LATE // ROWS)
            def _(i):
                start = pl.multiple_of(i * ROWS, ROWS)
                at = pl.ds(pl.multiple_of(base + start, ROWS), ROWS)
                values = total[at, :] + start_rows[pl.ds(start, ROWS), :]
                store_blocks(out, start, values, table_ref if blocked else None)

    return kernel


def feed_down(table, blocked, hidden, weights, start, tile=512):
    total, width = start.shape
    ff = 2 * hidden.shape[2]
    steps = ff // tile
    count = steps // 2
    clip = lambda j: jnp.minimum(j, steps - 1)
    late = pl.BlockSpec((LATE, width), lambda j, *_: (jnp.maximum(j - steps, 0), 0))
    weight_a, weight_b = column_halves(width // 2, tile, count)
    return pl.pallas_call(
        down_kernel(blocked, steps),
        name="feed_down",
        grid_spec=pltpu.PrefetchScalarGridSpec(
            num_scalar_prefetch=1,
            grid=(steps + total // LATE,),
            in_specs=[
                pl.BlockSpec((1, total, tile), lambda j, *_: (clip(j) // count, 0, clip(j) % count)),
                weight_a, weight_a, weight_b, weight_b,
                late,
            ],
            out_specs=late,
            scratch_shapes=[pltpu.VMEM((total, width), jnp.float32)],
        ),
        out_shape=jax.ShapeDtypeStruct((total, width), jnp.float32),
        compiler_params=params(VM_DOWN),
        cost_estimate=cost(2 * total * width * ff, 2 * (width * ff + total * ff) + 8 * total * width),
    )(table, hidden, *weights[0], *weights[1], start)


def feed_back_kernel(steps):
    def kernel(grad_z, down_top_a, down_bottom_a, down_top_b, down_bottom_b,
               up_top_a, up_bottom_a, up_top_b, up_bottom_b, slope, resid, grads, small,
               grad_upward, grad_resid, grad_branch, sums, total):
        step = pl.program_id(0)
        half = up_top_a.shape[0]

        @pl.when(step == 0)
        def _():
            total[...] = jnp.zeros_like(total)
            sums[...] = jnp.zeros_like(sums)

        def work(down_top, down_bottom, up_top, up_bottom):
            grad = split_dot(grad_z[...], down_top[...], down_bottom[...]) * slope[0].astype(jnp.float32)
            grad_upward[0] = grad.astype(LOW)
            total[:, :half] += dot(grad_upward[0], up_top[...], (1, 1))
            total[:, half:] += dot(grad_upward[0], up_bottom[...], (1, 1))

        either(
            step, steps // 2, work,
            (down_top_a, down_bottom_a, up_top_a, up_bottom_a),
            (down_top_b, down_bottom_b, up_top_b, up_bottom_b),
        )

        @pl.when(step >= steps)
        def _():
            base = (step - steps) * LATE

            @pl.loop(0, LATE // ROWS)
            def _(i):
                start = pl.multiple_of(i * ROWS, ROWS)
                at = pl.ds(start, ROWS)
                grad = total[pl.ds(pl.multiple_of(base + start, ROWS), ROWS), :]
                back, by_gain, by_bias = norm_back(resid[at, :], small[1:2], grad)
                back = back + grads[at, :]
                grad_resid[at, :] = back
                grad_branch[at, :] = back.astype(LOW)
                sums[0:8] += fold(by_gain)
                sums[8:16] += fold(by_bias)

    return kernel


def feed_back(grad_z, down, up, slope, resid, grads, small, tile=512):
    total, width = grad_z.shape
    ff = 2 * slope.shape[2]
    steps = ff // tile
    count = steps // 2
    clip = lambda j: jnp.minimum(j, steps - 1)
    wide_a, wide_b = column_halves(width // 2, tile, count)
    block = pl.BlockSpec((1, total, tile), lambda j: (clip(j) // count, 0, clip(j) % count))
    late = pl.BlockSpec((LATE, width), lambda j: (jnp.maximum(j - steps, 0), 0))
    return pl.pallas_call(
        feed_back_kernel(steps),
        name="feed_back",
        grid=(steps + total // LATE,),
        in_specs=[whole(total, width), wide_a, wide_a, wide_b, wide_b, wide_a, wide_a, wide_b, wide_b, block, late, late, whole(4, width)],
        out_specs=[block, late, late, whole(16, width)],
        out_shape=[
            jax.ShapeDtypeStruct((2, total, ff // 2), LOW),
            jax.ShapeDtypeStruct((total, width), jnp.float32),
            jax.ShapeDtypeStruct((total, width), LOW),
            jax.ShapeDtypeStruct((16, width), jnp.float32),
        ],
        scratch_shapes=[pltpu.VMEM((total, width), jnp.float32)],
        compiler_params=params(VM_BACK),
        cost_estimate=cost(4 * total * width * ff, 4 * (width * ff + total * ff) + 14 * total * width),
    )(grad_z, *down[0], *down[1], *up[0], *up[1], slope, resid, grads, small)


def backward_kernel(rows, steps, local_heads, factor):
    def kernel(before, own, after, top_a, bottom_a, top_b, bottom_b, column, row, saved,
               grad_projected, out, bias, grad_att):
        step, index = pl.program_id(0), pl.program_id(1)
        group = local_heads * HEAD_DIM
        wide = 3 * group
        half = top_a.shape[0]
        at_rows = pl.ds(pl.multiple_of(index * rows, rows), rows)

        @pl.when(step == 0)
        def _():
            bias[index] = window_bias(column[index], row[index])
            out[at_rows, :] = jnp.zeros((rows, 2 * half), jnp.float32)

        mine = slice(HALO, HALO + rows)

        def work(top, bottom):
            project((before, own, after), top[:, wide:], bottom[:, wide:], grad_att, index, rows)
            for h in range(local_heads):
                at = slice(h * HEAD_DIM, (h + 1) * HEAD_DIM)
                at_k = slice(group + h * HEAD_DIM, group + (h + 1) * HEAD_DIM)
                at_v = slice(2 * group + h * HEAD_DIM, 2 * group + (h + 1) * HEAD_DIM)
                q, k, v = saved[0, :, at], saved[0, :, at_k], saved[0, :, at_v]
                grad_mix = grad_att[:, at]
                p = attention_weights(q, k, bias[index], factor)
                grad_p = dot(grad_mix, v, (1, 1))
                weighted = jnp.sum(p * grad_p, axis=-1, keepdims=True)
                grad_s = (p * (grad_p - weighted)).astype(LOW)
                grad_projected[0, :, at] = (dot(grad_s[mine], k, (1, 0)) * factor).astype(LOW)
                grad_projected[0, :, at_k] = (dot(grad_s[:, mine], q, (0, 0)) * factor).astype(LOW)
                grad_projected[0, :, at_v] = dot(p[:, mine].astype(LOW), grad_mix, (0, 0)).astype(LOW)
            out[at_rows, :half] += dot(grad_projected[0], top[:, :wide], (1, 1))
            out[at_rows, half:] += dot(grad_projected[0], bottom[:, :wide], (1, 1))

        either(step, steps // 2, work, (top_a, bottom_a), (top_b, bottom_b))

    return kernel


def backward_block(window, weights, column, row, saved, steps, factor):
    before, own, after = window
    micro, rows, width = own.shape
    span = rows + 2 * HALO
    total = micro * rows
    half = steps // 2
    c = weights[0][0].shape[1] // half
    g = c // 4
    weight_a, weight_b = column_halves(width // 2, c, half)
    return pl.pallas_call(
        backward_kernel(rows, steps, g // HEAD_DIM, factor),
        name="attention_backward",
        grid=(steps, micro),
        in_specs=[
            whole(*before.shape), whole(*own.shape), whole(*after.shape),
            weight_a, weight_a, weight_b, weight_b,
            whole(*column.shape), whole(*row.shape),
            pl.BlockSpec((1, span, 3 * g), lambda k, i: (i, 0, k)),
        ],
        out_specs=[
            pl.BlockSpec((1, rows, 3 * g), lambda k, i: (k // half, i, k % half)),
            whole(total, width),
        ],
        scratch_shapes=[
            pltpu.VMEM((micro, span, span), jnp.float32),
            pltpu.VMEM((span, g), LOW),
        ],
        out_shape=[
            jax.ShapeDtypeStruct((2, total, 3 * g * half), LOW),
            jax.ShapeDtypeStruct((total, width), jnp.float32),
        ],
        compiler_params=params(VM_BWD),
        cost_estimate=cost(
            2 * micro * steps * g * (span * width + rows * width * 3 + 4 * span * span),
            35 * MEGA,
            micro * span * span * steps * g // HEAD_DIM,
        ),
    )(before, own, after, *weights[0], *weights[1], column, row, saved)


def leave_kernel(blocked):
    def kernel(table_ref, norm_one, entered, grad_resid, small, latents_grad, sums):
        @pl.when(pl.program_id(0) == 0)
        def _():
            sums[...] = jnp.zeros_like(sums)

        @pl.loop(0, entered.shape[0] // ROWS)
        def _(i):
            start = pl.multiple_of(i * ROWS, ROWS)
            at = pl.ds(start, ROWS)
            back, by_gain, by_bias = norm_back(entered[at, :], small[0:1], norm_one[at, :])
            store_blocks(latents_grad, start, back + grad_resid[at, :], table_ref if blocked else None)
            sums[0:8] += fold(by_gain)
            sums[8:16] += fold(by_bias)

    return kernel


def leave_norm(table, blocked, norm_one, entered, grad_resid, small):
    total, width = entered.shape
    rows = 128
    spec = pl.BlockSpec((rows, width), lambda i, *_: (i, 0))
    return pl.pallas_call(
        leave_kernel(blocked),
        name="leave",
        grid_spec=pltpu.PrefetchScalarGridSpec(
            num_scalar_prefetch=1,
            grid=(total // rows,),
            in_specs=[spec, spec, spec, whole(4, width)],
            out_specs=[spec, whole(16, width)],
        ),
        out_shape=[
            jax.ShapeDtypeStruct((total, width), jnp.float32),
            jax.ShapeDtypeStruct((16, width), jnp.float32),
        ],
        compiler_params=params(VM_ENTER),
        cost_estimate=cost(total * width * 30, total * width * 16),
    )(table, norm_one, entered, grad_resid, small)


def solution(mesh):
    plan = Plan(mesh)

    def body(latents, group_ids, pad_mask, w_qkv, w_out, w_up, w_down, norm_gain, norm_bias, out_grad):
        micro, rows, width = latents.shape
        total = micro * rows
        mp = plan.mp
        factor = HEAD_DIM ** (-0.5)
        links = Links(plan.dp, mp)
        small = jnp.concatenate([norm_gain, norm_bias], axis=0).T
        small = plan.gather_small(links, small).T.astype(jnp.float32)

        blocked = width // plan.dp % 128 == 0
        table = plan.own() ^ jnp.array(plan.relative, jnp.int32)
        rows_in = (latents.reshape(total, width), out_grad.reshape(total, width))
        if not blocked:
            rows_in = tuple(plan.enter(v) for v in rows_in)
        entered, grad_rows, grad_z, inputs_a = enter_norm(table, blocked, *rows_in, small)

        local = jnp.concatenate([w_qkv[0], w_qkv[1], w_qkv[2], w_out], axis=1)
        gather_attention = Gather(plan, links, plan.spread_columns(links, local))
        columns_up = lax.all_gather(w_up, "mp", axis=0)
        columns_down = lax.all_gather(w_down, "mp", axis=0)
        gather_up = Gather(plan, links, plan.halves([columns_up[k] for k in range(mp)]))
        gather_down = Gather(plan, links, plan.halves([columns_down[k] for k in range(mp)]))
        gather_attention.steps_but_last([small])
        window = links.halo(inputs_a.reshape(micro, rows, width))
        gather_attention.step([inputs_a])
        attention = gather_attention.finish()
        tokens = gather_up.steps_but_last([inputs_a])

        span = rows + 2 * HALO
        first = lax.axis_index("mp") * rows
        pads = ((0, 0), (HALO, HALO))
        groups = jnp.pad(group_ids[:, 0], pads, constant_values=-1)
        keys = jnp.where(jnp.pad(pad_mask[:, 0], pads) == 1, groups, -2)
        groups = lax.dynamic_slice_in_dim(groups, first, span, 1)
        keys = lax.dynamic_slice_in_dim(keys, first, span, 1)
        column, row = groups[:, :, None], keys[:, None, :]

        saved, attended, resid, inputs_c = forward_block(
            window, attention, after(column, *tokens, columns_down), row, entered, small, mp, factor
        )
        gather_up.step()
        tokens = gather_down.steps_but_last()
        gather_up.hold([inputs_c])
        up = gather_up.finish()
        gather_down.hold([inputs_c])
        hidden, slope = feed_up(after(inputs_c, *tokens), up)
        gather_down.step()
        gather_down.hold([hidden])
        down = gather_down.finish()
        grad_down = Scatter(plan, links, [(grad_z, [hidden[0], hidden[1]])])
        for i in range(2):
            grad_down.core(i)
        tokens = [grad_down.steps_but_last(i) for i in range(2)]
        upward, grad_resid, grad_branch, sums_two = feed_back(
            after(grad_z, *tokens), down, up, slope, resid, grad_rows, small
        )
        branch = links.halo(grad_branch.reshape(micro, rows, width))
        for i in range(2):
            grad_down.hold(i, [grad_branch])
        tokens = [grad_down.step(i) for i in range(2)]
        left = after(inputs_c, *tokens)
        grad_up = Scatter(
            plan, links, [(left, [upward[0], upward[1]]), (grad_branch, [attended[0], attended[1]])]
        )
        for i in range(2):
            grad_up.core(i)
        tokens = [grad_up.steps_but_last(i) for i in range(2)]
        grad_down = grad_down.reduce_columns()
        projected, norm_one = backward_block(
            branch, attention, after(column, *tokens), row, saved, mp, factor
        )
        for i in range(2):
            grad_up.hold(i, [norm_one])
        tokens = [grad_up.step(i) for i in range(2)]
        left = after(inputs_a, *tokens)
        grad_qkv = Scatter(plan, links, [(left, [projected[0], projected[1]])])
        for i in range(2):
            grad_qkv.core(i)
        tokens = [grad_qkv.steps_but_last(i) for i in range(2)]
        latents_grad, sums_one = leave_norm(
            table, blocked, after(norm_one, *tokens), entered, grad_resid, small
        )
        for i in range(2):
            grad_up.hold(i, [latents_grad])
        tokens = grad_up.shifts([True, False])
        latents_out = feed_down(table, blocked, after(hidden, sums_one, *tokens), down, resid)
        for i in range(2):
            grad_qkv.hold(i, [latents_out])
            grad_qkv.step(i)
        grad_qkv.shifts([False])
        grad_up, grad_out = grad_up.finish()
        grad_qkv = grad_qkv.finish()[0]
        grad_qkv = jnp.stack(jnp.split(grad_qkv, 3, axis=1))
        sums = jnp.stack([sums_one, sums_two], axis=0).reshape(2, 2, 8, width).sum(axis=2)
        sums = sums.transpose(1, 0, 2).reshape(4, width).T
        for bit in plan.major:
            middle = sums.shape[0] // 2
            sums = sums[:middle] + links.swap(sums[middle:], bit, 0)
        for bit in [1 << i for i in range(mp.bit_length() - 1)]:
            sums = sums + lax.ppermute(sums, "mp", [(i, i ^ bit) for i in range(mp)])
        sums = sums.T
        if not blocked:
            latents_out, latents_grad = plan.leave(latents_out), plan.leave(latents_grad)
        shape = latents.shape
        return (
            latents_out.reshape(shape),
            latents_grad.reshape(shape),
            grad_qkv,
            grad_out,
            grad_up,
            grad_down,
            sums[:2],
            sums[2:],
        )

    return jax.shard_map(
        body,
        mesh=mesh,
        in_specs=(
            P(None, ("dp", "mp"), None),
            P(None, "dp", None),
            P(None, "dp", None),
            P(None, "dp", "mp"),
            P("dp", "mp"),
            P("dp", "mp"),
            P("dp", "mp"),
            P(None, "dp"),
            P(None, "dp"),
            P(None, ("dp", "mp"), None),
        ),
        out_specs=(
            P(None, ("dp", "mp"), None),
            P(None, ("dp", "mp"), None),
            P(None, "dp", "mp"),
            P("dp", "mp"),
            P("dp", "mp"),
            P("dp", "mp"),
            P(None, "dp"),
            P(None, "dp"),
        ),
        check_vma=False,
    )
```

```python
import jax
import jax.numpy as jnp
from jax import lax
from jax.experimental import pallas as pl
from jax.experimental.pallas import tpu as pltpu
from jax.sharding import PartitionSpec as P

HEAD_DIM = 128
HALO = 128
EPSILON = 1e-05
LOW = jnp.bfloat16


def dot(left, right, dims, kind=jnp.float32):
    return lax.dot_general(
        left, right, ((dims[:1], dims[1:]), ((), ())), preferred_element_type=kind
    )


class Links:
    def __init__(self, dp, mp):
        self.dp, self.mp = dp, mp
        self.last = {}

    def send(self, value, axis, pairs, link, depth):
        before = self.last.setdefault(link, [])
        if depth and len(before) >= depth:
            value, _ = lax.optimization_barrier((value, before[-depth]))
        result = lax.ppermute(value, axis, pairs)
        before.append(result)
        return result

    def swap(self, value, bit, depth=0):
        return self.send(value, "dp", [(i, i ^ bit) for i in range(self.dp)], bit, depth)

    def shift(self, value, step, depth=3):
        pairs = [(i, (i + step) % self.mp) for i in range(self.mp)]
        return self.send(value, "mp", pairs, "z", depth)

    def halo(self, value, depth=0):
        count = self.mp
        before = self.send(value[:, -HALO:], "mp", [(i, i + 1) for i in range(count - 1)], "z", depth)
        after = self.send(value[:, :HALO], "mp", [(i + 1, i) for i in range(count - 1)], "z", depth)
        return before, value, after


class Plan:
    def __init__(self, mesh):
        self.dp = mesh.shape["dp"]
        self.mp = mesh.shape["mp"]
        bits = [1 << i for i in range(self.dp.bit_length() - 1)]
        core, others = bits[:1], bits[1:]
        self.orders = (others + core, others[::-1] + core)
        self.major = core + others[::-1]
        relative = [0]
        for bit in self.major[::-1]:
            relative = relative + [r ^ bit for r in relative]
        self.relative = relative

    def own(self):
        return lax.axis_index("dp")

    def enter(self, value):
        width = value.shape[-1] // self.dp
        axis = value.ndim - 1
        return jnp.concatenate(
            [
                lax.dynamic_slice_in_dim(value, (self.own() ^ r) * width, width, axis)
                for r in self.relative
            ],
            axis=axis,
        )

    def leave(self, value):
        width = value.shape[-1] // self.dp
        axis = value.ndim - 1
        inverse = {r: p for p, r in enumerate(self.relative)}
        table = jnp.array([inverse[r] for r in range(self.dp)], jnp.int32)
        return jnp.concatenate(
            [
                lax.dynamic_slice_in_dim(value, table[self.own() ^ n] * width, width, axis)
                for n in range(self.dp)
            ],
            axis=axis,
        )

    def gather_small(self, links, value):
        for bit in self.major[::-1]:
            value = jnp.concatenate([value, links.swap(value, bit, 0)], axis=0)
        return value

    def spread_columns(self, links, local):
        parts = [local] + [links.shift(local, -k, 0) for k in range(1, self.mp)]
        return self.halves(parts)

    def halves(self, parts):
        half = self.mp // 2
        return [jnp.concatenate(parts[i * half : (i + 1) * half], axis=1) for i in range(2)]


class Gather:
    def __init__(self, plan, links, held):
        self.plan, self.links = plan, links
        self.block = held[0].shape[0]
        self.held = [[h] for h in held]
        self.known = [[0], [0]]
        self.steps = [list(order[:-1]) for order in plan.orders]

    def pieces(self, i, order):
        span = self.held[i][0].shape[0] // self.block
        at = [self.known[i].index(r) for r in order]
        pieces = []
        while at:
            n = at.pop(0)
            count = 1
            while at and at[0] == n + count and (n + count) % span:
                at.pop(0)
                count += 1
            held = self.held[i][n // span]
            first = n % span * self.block
            pieces.append(held if count == span else held[first : first + count * self.block])
        return pieces

    def join(self, i, order):
        pieces = self.pieces(i, order)
        return pieces[0] if len(pieces) == 1 else jnp.concatenate(pieces, axis=0)

    def step(self, tokens=(), second=()):
        for i in range(2):
            bit = self.steps[i][0]
            value = self.join(i, self.known[i])
            value = after(value, *(second if i else tokens))
            self.held[i] = [value, self.links.swap(value, bit)]
            self.known[i] = self.known[i] + [r ^ bit for r in self.known[i]]
            self.steps[i] = self.steps[i][1:]
        return [h[1] for h in self.held]

    def steps_but_last(self, tokens=()):
        received = []
        while len(self.steps[0]) > 1:
            received = self.step(tokens, tokens)
        return received

    def hold(self, tokens):
        for i in range(2):
            self.held[i][1] = after(self.held[i][1], *tokens)

    def finish(self):
        order = self.plan.relative[: self.plan.dp // 2]
        mine = [self.join(i, order) for i in range(2)]
        return [(m, self.links.swap(m, self.plan.major[0])) for m in mine]


class Scatter:
    def __init__(self, plan, links, pairs):
        self.plan, self.links = plan, links
        self.pairs = pairs
        self.kept = [None, None]
        self.bits = [list(order[:-1][::-1]) for order in plan.orders]
        self.remain = [list(plan.major[1:]), list(plan.major[1:])]

    def core(self, i):
        self.kept[i] = []
        for left, rights in self.pairs:
            middle = left.shape[1] // 2
            sent = dot(left[:, middle:], rights[i], (0, 0)).astype(LOW)
            kept = dot(left[:, :middle], rights[i], (0, 0))
            self.kept[i].append((kept, self.links.swap(sent, self.plan.major[0])))

    def hold(self, i, tokens):
        self.kept[i] = [(k, after(r, *tokens)) for k, r in self.kept[i]]

    def add(self, i):
        self.kept[i] = [
            k[0] + k[1].astype(jnp.float32) if isinstance(k, tuple) else k for k in self.kept[i]
        ]
        return self.kept[i]

    def step(self, i, tokens=()):
        values = self.add(i)
        bit = self.bits[i].pop(0)
        block = values[0].shape[0] >> (self.remain[i].index(bit) + 1)
        shaped = [v.reshape(-1, 2, block, v.shape[1]) for v in values]
        out = [x[:, 1].reshape(-1, v.shape[1]).astype(LOW) for x, v in zip(shaped, values)]
        stay = [x[:, 0].reshape(-1, v.shape[1]) for x, v in zip(shaped, values)]
        out = out[0] if len(out) == 1 else jnp.concatenate(out, axis=1)
        received = self.links.swap(after(out, *tokens), bit)
        self.kept[i], at = [], 0
        for x in stay:
            self.kept[i].append((x, received[:, at : at + x.shape[1]]))
            at += x.shape[1]
        self.remain[i].remove(bit)
        return out

    def steps_but_last(self, i, tokens=()):
        out = None
        while len(self.bits[i]) > 1:
            out = self.step(i, tokens)
        return out

    def rows(self):
        half = self.plan.mp // 2
        result = []
        for pair in zip(*[self.add(i) for i in range(2)]):
            width = pair[0].shape[1] // half
            result.append([r[:, j * width : (j + 1) * width] for r in pair for j in range(half)])
        return result


def own_first(blocks):
    joined = jnp.stack(blocks)
    own = lax.axis_index("mp")
    return [
        lax.dynamic_index_in_dim(joined, lax.rem(own + k, len(blocks)), 0, keepdims=False)
        for k in range(len(blocks))
    ]


def shift_blocks(plan, links, products, tokens=()):
    received = []
    for k in range(1, plan.mp):
        out = [blocks[k].astype(LOW) for blocks in products]
        out = out[0] if len(out) == 1 else jnp.concatenate(out, axis=1)
        received.append(links.shift(after(out, *tokens), k, 0))
    result, at = [], 0
    for blocks in products:
        total = blocks[0]
        for part in received:
            total = total + part[:, at : at + total.shape[1]].astype(jnp.float32)
        result.append(total)
        at += total.shape[1]
    return result


def reduce_blocks(blocks):
    return lax.psum_scatter(jnp.stack(blocks), "mp", scatter_dimension=0, tiled=False)


def after(value, *tokens):
    if not tokens:
        return value
    return lax.optimization_barrier((value, *tokens))[0]


def split_dot(left, top, bottom):
    half = top.shape[0]
    return dot(left[:, :half], top, (1, 0)) + dot(left[:, half:], bottom, (1, 0))


C = {"z_up": 0, "z_down": 0, "g_zup": 0, "g_enter": 0, "g_x1": 1, "g_zdown": 0, "g_x2a": 2, "g_x2b": 1, "g_x1up": 1, "h_core": 4, "t_fwd": 2, "h_up": 1, "h_down": 1, "t_up": 1, "h_down2": 1, "t_back": 1, "h_d2": 1, "p_down": 1, "t_down0": 1, "g_u": 1, "g_o": 0, "merge": 1, "t_bwd": 1, "h_sd": 0, "h_u2": 1, "first_u2": 1, "g_q": 1, "t_leave": 1, "h_uz": 1, "z_u": 0, "t_down": 2, "h_q2": 1, "t_down2": 0, "g_sums": 0}
MEGA = 1 << 20
LOG2E = 1.4426950408889634
VM_FWD = 36
VM_UP = 20
VM_DOWN = 20
VM_BACK = 32
VM_BWD = 36
VM_ENTER = 20


def params(limit=56):
    return pltpu.CompilerParams(vmem_limit_bytes=limit * MEGA)


def cost(flops, bytes_accessed, transcendentals=0):
    return pl.CostEstimate(
        flops=int(flops), bytes_accessed=int(bytes_accessed), transcendentals=int(transcendentals)
    )


def whole(*shape):
    return pl.BlockSpec(shape, lambda *_: (0,) * len(shape), pipeline_mode=pl.Buffered(1))


def statistics(values):
    mean = jnp.mean(values, axis=-1, keepdims=True)
    centred = values - mean
    variance = jnp.mean(centred * centred, axis=-1, keepdims=True)
    return centred, lax.rsqrt(variance + EPSILON)


def norm_rows(values, gain, bias):
    centred, scale = statistics(values)
    return centred * scale * gain + bias


def norm_back(values, gain, grad):
    centred, scale = statistics(values)
    normed = centred * scale
    inner = grad * gain
    first = jnp.mean(inner, axis=-1, keepdims=True)
    second = jnp.mean(inner * normed, axis=-1, keepdims=True)
    return (inner - first - normed * second) * scale, grad * normed, grad


def fold(rows):
    total = rows[:8]
    for i in range(1, rows.shape[0] // 8):
        total = total + rows[i * 8 : i * 8 + 8]
    return total


ROWS = 64


def store_blocks(ref, start, value, table, inverse=None):
    if table is None:
        ref[pl.ds(start, value.shape[0]), :] = value
        return
    count = table.shape[0]
    block = value.shape[1] // count
    for p in range(count):
        at = pl.multiple_of(table[p] * block, block)
        ref[pl.ds(start, value.shape[0]), pl.ds(at, block)] = value[:, p * block : (p + 1) * block]


def load_blocks(ref, start, size, table):
    if table is None:
        return ref[pl.ds(start, size), :]
    count = table.shape[0]
    block = ref.shape[1] // count
    parts = []
    for p in range(count):
        at = pl.multiple_of(table[p] * block, block)
        parts.append(ref[pl.ds(start, size), pl.ds(at, block)])
    return jnp.concatenate(parts, axis=1)


def enter_kernel(blocked):
    def kernel(table_ref, latents, grads, small, entered, entered_grads, grad_z, inputs_a):
        table = table_ref if blocked else None

        @pl.loop(0, latents.shape[0] // ROWS)
        def _(i):
            start = pl.multiple_of(i * ROWS, ROWS)
            at = pl.ds(start, ROWS)
            values = load_blocks(latents, start, ROWS, table)
            entered[at, :] = values
            inputs_a[at, :] = norm_rows(values, small[0:1], small[2:3]).astype(LOW)
            values = load_blocks(grads, start, ROWS, table)
            entered_grads[at, :] = values
            grad_z[at, :] = values.astype(LOW)

    return kernel


def enter_norm(table, blocked, latents, grads, small):
    total, width = latents.shape
    rows = 256
    spec = pl.BlockSpec((rows, width), lambda i, *_: (i, 0))
    shape = lambda kind: jax.ShapeDtypeStruct((total, width), kind)
    return pl.pallas_call(
        enter_kernel(blocked),
        name="enter",
        grid_spec=pltpu.PrefetchScalarGridSpec(
            num_scalar_prefetch=1,
            grid=(total // rows,),
            in_specs=[spec, spec, whole(4, width)],
            out_specs=[spec] * 4,
        ),
        out_shape=[shape(jnp.float32), shape(jnp.float32), shape(LOW), shape(LOW)],
        compiler_params=params(VM_ENTER),
        cost_estimate=cost(total * width * 16, total * width * 20),
    )(table, latents, grads, small)


def attention_weights(q, k, bias, factor):
    scores = dot(q, k, (1, 1)) * (factor * LOG2E) + bias
    peak = jnp.max(scores, axis=-1, keepdims=True)
    weights = jnp.exp2(scores - peak)
    return weights * (1.0 / jnp.sum(weights, axis=-1, keepdims=True))


def window_bias(group_column, key_row):
    span = group_column.shape[0]
    place = lax.broadcasted_iota(jnp.int32, (span, span), 0)
    other = lax.broadcasted_iota(jnp.int32, (span, span), 1)
    allowed = (group_column == key_row) | (place == other)
    return jnp.where(allowed, 0.0, -1e30)


def column_halves(rows, tile, count):
    return (
        pl.BlockSpec((rows, tile), lambda k, *_: (0, jnp.minimum(k, count - 1))),
        pl.BlockSpec((rows, tile), lambda k, *_: (0, jnp.clip(k - count, 0, count - 1))),
    )


def either(step, count, work, first, second):
    @pl.when(step < count)
    def _():
        work(*first)

    @pl.when((step >= count) & (step < 2 * count))
    def _():
        work(*second)


def project(window, w_top, w_bottom, target, index, rows):
    before, own, after = window
    target[0:HALO] = split_dot(before[index], w_top, w_bottom).astype(LOW)
    target[HALO : HALO + rows] = split_dot(own[index], w_top, w_bottom).astype(LOW)
    target[HALO + rows :] = split_dot(after[index], w_top, w_bottom).astype(LOW)


def forward_kernel(rows, steps, local_heads, factor):
    def kernel(before, own, after, top_a, bottom_a, top_b, bottom_b, column, row, start, small,
               saved, attended, resid, inputs_c, bias, total):
        step, index = pl.program_id(0), pl.program_id(1)
        group = local_heads * HEAD_DIM
        wide = 3 * group
        half = top_a.shape[0]
        target = saved.at[0]

        @pl.when(step == 0)
        def _():
            bias[index] = window_bias(column[index], row[index])
            total[index] = jnp.zeros((rows, 2 * half), jnp.float32)

        mine = slice(HALO, HALO + rows)

        def work(top, bottom):
            project((before, own, after), top[:, :wide], bottom[:, :wide], target, index, rows)
            for h in range(local_heads):
                at = slice(h * HEAD_DIM, (h + 1) * HEAD_DIM)
                q = target[mine, at]
                k = target[:, group + h * HEAD_DIM : group + (h + 1) * HEAD_DIM]
                v = target[:, 2 * group + h * HEAD_DIM : 2 * group + (h + 1) * HEAD_DIM]
                p = attention_weights(q, k, bias[index, mine, :], factor).astype(LOW)
                attended[0, :, at] = dot(p, v, (1, 0)).astype(LOW)
            total[index, :, :half] += dot(attended[0], top[:, wide:], (1, 1))
            total[index, :, half:] += dot(attended[0], bottom[:, wide:], (1, 1))

        @pl.when(step < steps // 2)
        def _():
            work(top_a, bottom_a)

        @pl.when(step >= steps // 2)
        def _():
            work(top_b, bottom_b)

        @pl.when(step == steps - 1)
        def _():
            @pl.loop(0, rows // ROWS)
            def _(i):
                at = pl.ds(pl.multiple_of(i * ROWS, ROWS), ROWS)
                values = total[index, at, :] + start[at, :]
                resid[at, :] = values
                inputs_c[at, :] = norm_rows(values, small[1:2], small[3:4]).astype(LOW)

    return kernel


def forward_block(window, weights, column, row, start, small, steps, factor):
    before, own, after = window
    micro, rows, width = own.shape
    span = rows + 2 * HALO
    total = micro * rows
    half = steps // 2
    c = weights[0][0].shape[1] // half
    g = c // 4
    late = pl.BlockSpec((rows, width), lambda k, i: (jnp.where(k == steps - 1, i, 0), 0))
    weight_a, weight_b = column_halves(width // 2, c, half)
    return pl.pallas_call(
        forward_kernel(rows, steps, g // HEAD_DIM, factor),
        name="attention_forward",
        grid=(steps, micro),
        in_specs=[
            whole(*before.shape), whole(*own.shape), whole(*after.shape),
            weight_a, weight_a, weight_b, weight_b,
            whole(*column.shape), whole(*row.shape),
            late,
            whole(4, width),
        ],
        out_specs=[
            pl.BlockSpec((1, span, 3 * g), lambda k, i: (i, 0, k)),
            pl.BlockSpec((1, rows, g), lambda k, i: (k // half, i, k % half)),
            late,
            late,
        ],
        out_shape=[
            jax.ShapeDtypeStruct((micro, span, 3 * g * steps), LOW),
            jax.ShapeDtypeStruct((2, total, g * half), LOW),
            jax.ShapeDtypeStruct((total, width), jnp.float32),
            jax.ShapeDtypeStruct((total, width), LOW),
        ],
        scratch_shapes=[
            pltpu.VMEM((micro, span, span), jnp.float32),
            pltpu.VMEM((micro, rows, width), jnp.float32),
        ],
        compiler_params=params(VM_FWD),
        cost_estimate=cost(
            2 * micro * steps * g * (span * width * 3 + rows * width + 2 * rows * span),
            30 * MEGA,
            micro * rows * span * steps * g // HEAD_DIM,
        ),
    )(before, own, after, *weights[0], *weights[1], column, row, start, small)


def up_kernel(count):
    def kernel(inputs, top_a, bottom_a, top_b, bottom_b, hidden, slope):
        def work(top, bottom):
            u = split_dot(inputs[...], top[...], bottom[...])
            c = 0.7978845608028654
            square = u * u
            t = jnp.tanh(u * (c + c * 0.044715 * square))
            half = 0.5 + 0.5 * t
            hidden[0] = (u * half).astype(LOW)
            inner = 0.5 * c + 1.5 * c * 0.044715 * square
            slope[0] = (half + u * inner * (1.0 - t * t)).astype(LOW)

        either(pl.program_id(0), count, work, (top_a, bottom_a), (top_b, bottom_b))

    return kernel


def feed_up(inputs, weights, tile=512):
    total, width = inputs.shape
    ff = 2 * weights[0][0].shape[1]
    count = ff // 2 // tile
    block = pl.BlockSpec((1, total, tile), lambda j: (j // count, 0, j % count))
    weight_a, weight_b = column_halves(width // 2, tile, count)
    return pl.pallas_call(
        up_kernel(count),
        name="feed_up",
        grid=(ff // tile,),
        in_specs=[whole(total, width), weight_a, weight_a, weight_b, weight_b],
        out_specs=[block, block],
        out_shape=[jax.ShapeDtypeStruct((2, total, ff // 2), LOW)] * 2,
        compiler_params=params(VM_UP),
        cost_estimate=cost(2 * total * width * ff, 2 * (width * ff + 2 * total * ff), total * ff),
    )(inputs, *weights[0], *weights[1])


LATE = 256


def down_kernel(blocked, steps):
    def kernel(table_ref, hidden, top_a, bottom_a, top_b, bottom_b, start_rows, out, total):
        step = pl.program_id(0)
        half = top_a.shape[0]

        @pl.when(step == 0)
        def _():
            total[...] = jnp.zeros_like(total)

        def work(top, bottom):
            total[:, :half] += dot(hidden[0], top[...], (1, 1))
            total[:, half:] += dot(hidden[0], bottom[...], (1, 1))

        either(step, steps // 2, work, (top_a, bottom_a), (top_b, bottom_b))

        @pl.when(step >= steps)
        def _():
            base = (step - steps) * LATE

            @pl.loop(0, LATE // ROWS)
            def _(i):
                start = pl.multiple_of(i * ROWS, ROWS)
                at = pl.ds(pl.multiple_of(base + start, ROWS), ROWS)
                values = total[at, :] + start_rows[pl.ds(start, ROWS), :]
                store_blocks(out, start, values, table_ref if blocked else None)

    return kernel


def feed_down(table, blocked, hidden, weights, start, tile=512):
    total, width = start.shape
    ff = 2 * hidden.shape[2]
    steps = ff // tile
    count = steps // 2
    clip = lambda j: jnp.minimum(j, steps - 1)
    late = pl.BlockSpec((LATE, width), lambda j, *_: (jnp.maximum(j - steps, 0), 0))
    weight_a, weight_b = column_halves(width // 2, tile, count)
    return pl.pallas_call(
        down_kernel(blocked, steps),
        name="feed_down",
        grid_spec=pltpu.PrefetchScalarGridSpec(
            num_scalar_prefetch=1,
            grid=(steps + total // LATE,),
            in_specs=[
                pl.BlockSpec((1, total, tile), lambda j, *_: (clip(j) // count, 0, clip(j) % count)),
                weight_a, weight_a, weight_b, weight_b,
                late,
            ],
            out_specs=late,
            scratch_shapes=[pltpu.VMEM((total, width), jnp.float32)],
        ),
        out_shape=jax.ShapeDtypeStruct((total, width), jnp.float32),
        compiler_params=params(VM_DOWN),
        cost_estimate=cost(2 * total * width * ff, 2 * (width * ff + total * ff) + 8 * total * width),
    )(table, hidden, *weights[0], *weights[1], start)


def feed_back_kernel(steps):
    def kernel(grad_z, down_top_a, down_bottom_a, down_top_b, down_bottom_b,
               up_top_a, up_bottom_a, up_top_b, up_bottom_b, slope, resid, grads, small,
               grad_upward, grad_resid, grad_branch, sums, total):
        step = pl.program_id(0)
        half = up_top_a.shape[0]

        @pl.when(step == 0)
        def _():
            total[...] = jnp.zeros_like(total)
            sums[...] = jnp.zeros_like(sums)

        def work(down_top, down_bottom, up_top, up_bottom):
            grad = split_dot(grad_z[...], down_top[...], down_bottom[...]) * slope[0].astype(jnp.float32)
            grad_upward[0] = grad.astype(LOW)
            total[:, :half] += dot(grad_upward[0], up_top[...], (1, 1))
            total[:, half:] += dot(grad_upward[0], up_bottom[...], (1, 1))

        either(
            step, steps // 2, work,
            (down_top_a, down_bottom_a, up_top_a, up_bottom_a),
            (down_top_b, down_bottom_b, up_top_b, up_bottom_b),
        )

        @pl.when(step >= steps)
        def _():
            base = (step - steps) * LATE

            @pl.loop(0, LATE // ROWS)
            def _(i):
                start = pl.multiple_of(i * ROWS, ROWS)
                at = pl.ds(start, ROWS)
                grad = total[pl.ds(pl.multiple_of(base + start, ROWS), ROWS), :]
                back, by_gain, by_bias = norm_back(resid[at, :], small[1:2], grad)
                back = back + grads[at, :]
                grad_resid[at, :] = back
                grad_branch[at, :] = back.astype(LOW)
                sums[0:8] += fold(by_gain)
                sums[8:16] += fold(by_bias)

    return kernel


def feed_back(grad_z, down, up, slope, resid, grads, small, tile=512):
    total, width = grad_z.shape
    ff = 2 * slope.shape[2]
    steps = ff // tile
    count = steps // 2
    clip = lambda j: jnp.minimum(j, steps - 1)
    wide_a, wide_b = column_halves(width // 2, tile, count)
    block = pl.BlockSpec((1, total, tile), lambda j: (clip(j) // count, 0, clip(j) % count))
    late = pl.BlockSpec((LATE, width), lambda j: (jnp.maximum(j - steps, 0), 0))
    return pl.pallas_call(
        feed_back_kernel(steps),
        name="feed_back",
        grid=(steps + total // LATE,),
        in_specs=[whole(total, width), wide_a, wide_a, wide_b, wide_b, wide_a, wide_a, wide_b, wide_b, block, late, late, whole(4, width)],
        out_specs=[block, late, late, whole(16, width)],
        out_shape=[
            jax.ShapeDtypeStruct((2, total, ff // 2), LOW),
            jax.ShapeDtypeStruct((total, width), jnp.float32),
            jax.ShapeDtypeStruct((total, width), LOW),
            jax.ShapeDtypeStruct((16, width), jnp.float32),
        ],
        scratch_shapes=[pltpu.VMEM((total, width), jnp.float32)],
        compiler_params=params(VM_BACK),
        cost_estimate=cost(4 * total * width * ff, 4 * (width * ff + total * ff) + 14 * total * width),
    )(grad_z, *down[0], *down[1], *up[0], *up[1], slope, resid, grads, small)


def backward_kernel(rows, steps, local_heads, factor):
    def kernel(before, own, after, top_a, bottom_a, top_b, bottom_b, column, row, saved,
               grad_projected, out, bias, grad_att):
        step, index = pl.program_id(0), pl.program_id(1)
        group = local_heads * HEAD_DIM
        wide = 3 * group
        half = top_a.shape[0]
        at_rows = pl.ds(pl.multiple_of(index * rows, rows), rows)

        @pl.when(step == 0)
        def _():
            bias[index] = window_bias(column[index], row[index])
            out[at_rows, :] = jnp.zeros((rows, 2 * half), jnp.float32)

        mine = slice(HALO, HALO + rows)

        def work(top, bottom):
            project((before, own, after), top[:, wide:], bottom[:, wide:], grad_att, index, rows)
            for h in range(local_heads):
                at = slice(h * HEAD_DIM, (h + 1) * HEAD_DIM)
                at_k = slice(group + h * HEAD_DIM, group + (h + 1) * HEAD_DIM)
                at_v = slice(2 * group + h * HEAD_DIM, 2 * group + (h + 1) * HEAD_DIM)
                q, k, v = saved[0, :, at], saved[0, :, at_k], saved[0, :, at_v]
                grad_mix = grad_att[:, at]
                p = attention_weights(q, k, bias[index], factor)
                grad_p = dot(grad_mix, v, (1, 1))
                weighted = jnp.sum(p * grad_p, axis=-1, keepdims=True)
                grad_s = (p * (grad_p - weighted)).astype(LOW)
                grad_projected[0, :, at] = (dot(grad_s[mine], k, (1, 0)) * factor).astype(LOW)
                grad_projected[0, :, at_k] = (dot(grad_s[:, mine], q, (0, 0)) * factor).astype(LOW)
                grad_projected[0, :, at_v] = dot(p[:, mine].astype(LOW), grad_mix, (0, 0)).astype(LOW)
            out[at_rows, :half] += dot(grad_projected[0], top[:, :wide], (1, 1))
            out[at_rows, half:] += dot(grad_projected[0], bottom[:, :wide], (1, 1))

        either(step, steps // 2, work, (top_a, bottom_a), (top_b, bottom_b))

    return kernel


def backward_block(window, weights, column, row, saved, steps, factor):
    before, own, after = window
    micro, rows, width = own.shape
    span = rows + 2 * HALO
    total = micro * rows
    half = steps // 2
    c = weights[0][0].shape[1] // half
    g = c // 4
    weight_a, weight_b = column_halves(width // 2, c, half)
    return pl.pallas_call(
        backward_kernel(rows, steps, g // HEAD_DIM, factor),
        name="attention_backward",
        grid=(steps, micro),
        in_specs=[
            whole(*before.shape), whole(*own.shape), whole(*after.shape),
            weight_a, weight_a, weight_b, weight_b,
            whole(*column.shape), whole(*row.shape),
            pl.BlockSpec((1, span, 3 * g), lambda k, i: (i, 0, k)),
        ],
        out_specs=[
            pl.BlockSpec((1, rows, 3 * g), lambda k, i: (k // half, i, k % half)),
            whole(total, width),
        ],
        scratch_shapes=[
            pltpu.VMEM((micro, span, span), jnp.float32),
            pltpu.VMEM((span, g), LOW),
        ],
        out_shape=[
            jax.ShapeDtypeStruct((2, total, 3 * g * half), LOW),
            jax.ShapeDtypeStruct((total, width), jnp.float32),
        ],
        compiler_params=params(VM_BWD),
        cost_estimate=cost(
            2 * micro * steps * g * (span * width + rows * width * 3 + 4 * span * span),
            35 * MEGA,
            micro * span * span * steps * g // HEAD_DIM,
        ),
    )(before, own, after, *weights[0], *weights[1], column, row, saved)


def leave_kernel(blocked):
    def kernel(table_ref, norm_one, entered, grad_resid, small, latents_grad, sums):
        @pl.when(pl.program_id(0) == 0)
        def _():
            sums[...] = jnp.zeros_like(sums)

        @pl.loop(0, entered.shape[0] // ROWS)
        def _(i):
            start = pl.multiple_of(i * ROWS, ROWS)
            at = pl.ds(start, ROWS)
            back, by_gain, by_bias = norm_back(entered[at, :], small[0:1], norm_one[at, :])
            store_blocks(latents_grad, start, back + grad_resid[at, :], table_ref if blocked else None)
            sums[0:8] += fold(by_gain)
            sums[8:16] += fold(by_bias)

    return kernel


def leave_norm(table, blocked, norm_one, entered, grad_resid, small):
    total, width = entered.shape
    rows = 128
    spec = pl.BlockSpec((rows, width), lambda i, *_: (i, 0))
    return pl.pallas_call(
        leave_kernel(blocked),
        name="leave",
        grid_spec=pltpu.PrefetchScalarGridSpec(
            num_scalar_prefetch=1,
            grid=(total // rows,),
            in_specs=[spec, spec, spec, whole(4, width)],
            out_specs=[spec, whole(16, width)],
        ),
        out_shape=[
            jax.ShapeDtypeStruct((total, width), jnp.float32),
            jax.ShapeDtypeStruct((16, width), jnp.float32),
        ],
        compiler_params=params(VM_ENTER),
        cost_estimate=cost(total * width * 30, total * width * 16),
    )(table, norm_one, entered, grad_resid, small)


def solution(mesh):
    plan = Plan(mesh)

    def body(latents, group_ids, pad_mask, w_qkv, w_out, w_up, w_down, norm_gain, norm_bias, out_grad):
        micro, rows, width = latents.shape
        total = micro * rows
        mp = plan.mp
        factor = HEAD_DIM ** (-0.5)
        links = Links(plan.dp, mp)
        small = jnp.concatenate([norm_gain, norm_bias], axis=0).T
        small = plan.gather_small(links, small).T.astype(jnp.float32)

        blocked = width // plan.dp % 128 == 0
        table = plan.own() ^ jnp.array(plan.relative, jnp.int32)
        rows_in = (latents.reshape(total, width), out_grad.reshape(total, width))
        if not blocked:
            rows_in = tuple(plan.enter(v) for v in rows_in)
        local = jnp.concatenate([w_qkv[0], w_qkv[1], w_qkv[2], w_out], axis=1)

        def pick(name, *choices):
            chosen = choices[C[name]]
            return [t for t in chosen if t is not None]

        def columns_of(weight, name, tokens):
            if C[name]:
                return plan.spread_columns(links, after(weight, *tokens))
            columns = lax.all_gather(after(weight, *tokens), "mp", axis=0)
            return plan.halves([columns[k] for k in range(mp)])

        halves = plan.spread_columns(links, local)
        gather_attention = Gather(plan, links, halves)
        up_halves = columns_of(w_up, "z_up", pick("g_zup", [], halves))
        entered, grad_rows, grad_z, inputs_a = enter_norm(
            table, blocked, *rows_in, after(small, *pick("g_enter", [], halves))
        )
        gather_attention.steps_but_last(pick("g_x1", [], [small], [inputs_a]))
        window = links.halo(inputs_a.reshape(micro, rows, width))
        down_halves = columns_of(
            w_down, "z_down", pick("g_zdown", [], up_halves, [inputs_a], [window[0], window[2]])
        )
        halos = [window[0], window[2]]
        gather_attention.step(
            pick("g_x2a", [], [inputs_a], halos, up_halves, halos + up_halves),
            pick("g_x2b", [], [inputs_a], halos, up_halves),
        )
        gather_up = Gather(plan, links, up_halves)
        gather_down = Gather(plan, links, down_halves)
        tokens_up = gather_up.steps_but_last(pick("g_x1up", [], [inputs_a], halos))
        gather_attention.hold(
            pick("h_core", [], tokens_up, down_halves, tokens_up + down_halves, halos)
        )
        attention = gather_attention.finish()

        span = rows + 2 * HALO
        first = lax.axis_index("mp") * rows
        pads = ((0, 0), (HALO, HALO))
        groups = jnp.pad(group_ids[:, 0], pads, constant_values=-1)
        keys = jnp.where(jnp.pad(pad_mask[:, 0], pads) == 1, groups, -2)
        groups = lax.dynamic_slice_in_dim(groups, first, span, 1)
        keys = lax.dynamic_slice_in_dim(keys, first, span, 1)
        column, row = groups[:, :, None], keys[:, None, :]

        tokens_down = gather_down.steps_but_last()
        late_up = gather_up.step()
        saved, attended, resid, inputs_c = forward_block(
            window,
            attention,
            after(
                column,
                *pick(
                    "t_fwd",
                    [],
                    tokens_up,
                    tokens_up + down_halves,
                    tokens_down,
                    late_up,
                    late_up + tokens_down,
                ),
            ),
            row, entered, small, mp, factor,
        )
        gather_up.hold(pick("h_up", [], [inputs_c]))
        up = gather_up.finish()
        late_down = gather_down.step()
        gather_down.hold(pick("h_down", [], [inputs_c]))
        tokens = pick("t_up", [], tokens_down, late_down)
        hidden, slope = feed_up(after(inputs_c, *tokens), up)
        gather_down.hold(pick("h_down2", [], [hidden]))
        down = gather_down.finish()
        grad_down = Scatter(plan, links, [(grad_z, [hidden[0], hidden[1]])])
        for i in range(2):
            grad_down.core(i)
        tokens = [grad_down.steps_but_last(i) for i in range(2)]
        upward, grad_resid, grad_branch, sums_two = feed_back(
            after(grad_z, *pick("t_back", [], tokens)), down, up, slope, resid, grad_rows, small
        )
        branch = links.halo(grad_branch.reshape(micro, rows, width))
        halos = [branch[0], branch[2]]
        latents_out = None

        def put_down(*tokens):
            return feed_down(table, blocked, after(hidden, *tokens), down, resid)

        for i in range(2):
            grad_down.hold(i, pick("h_d2", [], [grad_branch]))
        tokens = [grad_down.step(i) for i in range(2)]
        if C["p_down"] == 0:
            latents_out = put_down(grad_branch, *pick("t_down0", [], tokens))
        middle = [latents_out]
        left = after(inputs_c, *pick("g_u", [], tokens, halos, middle))
        grad_up = Scatter(plan, links, [(left, [upward[0], upward[1]])])
        left = after(grad_branch, *pick("g_o", [], tokens, halos, middle))
        grad_out = Scatter(plan, links, [(left, [attended[0], attended[1]])])
        if C["merge"]:
            grad_up.pairs += grad_out.pairs
        parts = [grad_up] if C["merge"] else [grad_up, grad_out]
        for part in parts:
            for i in range(2):
                part.core(i)
        tokens = [part.steps_but_last(i) for part in parts for i in range(2)]
        down_rows = grad_down.rows()[0]
        projected, norm_one = backward_block(
            branch,
            attention,
            after(
                column,
                *pick("t_bwd", [], tokens, tokens + down_rows, down_rows, tokens[:2], middle, tokens + middle),
            ),
            row, saved, mp, factor,
        )
        grad_down = reduce_blocks([after(r, *pick("h_sd", [], [norm_one])) for r in down_rows])
        for part in parts:
            for i in range(2):
                part.hold(i, pick("h_u2", [], [norm_one]))
        outs = []

        def second(tokens):
            for part in parts:
                outs.extend(part.step(i, tokens) for i in range(2))

        if C["first_u2"]:
            second([])
        left = after(inputs_a, *pick("g_q", [], outs))
        grad_qkv = Scatter(plan, links, [(left, [projected[0], projected[1]])])
        for i in range(2):
            grad_qkv.core(i)
        tokens = [grad_qkv.steps_but_last(i) for i in range(2)]
        if not C["first_u2"]:
            second(tokens)
        latents_grad, sums_one = leave_norm(
            table, blocked, after(norm_one, *pick("t_leave", [], tokens)), entered, grad_resid, small
        )
        for part in parts:
            for i in range(2):
                part.hold(i, pick("h_uz", [], [latents_grad]))
        rows_uo = sum((part.rows() for part in parts), [])
        up_rows, out_rows = rows_uo
        if C["z_u"] == 0:
            grad_up = reduce_blocks(up_rows)
        elif C["z_u"] == 1:
            grad_up = shift_blocks(plan, links, [own_first(up_rows)])[0]
        else:
            grad_up, grad_out = shift_blocks(plan, links, [own_first(up_rows), out_rows])
        if C["p_down"] == 1:
            latents_out = put_down(*pick("t_down", [], [sums_one], [sums_one] + up_rows, tokens))
        for i in range(2):
            grad_qkv.hold(i, pick("h_q2", [], [latents_out], [latents_grad]))
            grad_qkv.step(i)
        qkv_rows = grad_qkv.rows()[0]
        if C["p_down"] == 2:
            latents_out = put_down(latents_grad, *pick("t_down2", [], up_rows, qkv_rows))
        if C["z_u"] == 2:
            grad_qkv = shift_blocks(plan, links, [qkv_rows])[0]
        else:
            grad_qkv, grad_out = shift_blocks(plan, links, [qkv_rows, out_rows])
        grad_qkv = jnp.stack(jnp.split(grad_qkv, 3, axis=1))
        sums = jnp.stack([sums_one, sums_two], axis=0).reshape(2, 2, 8, width).sum(axis=2)
        sums = sums.transpose(1, 0, 2).reshape(4, width).T
        sums = after(sums, *pick("g_sums", [], qkv_rows, [latents_grad]))
        for bit in plan.major:
            middle = sums.shape[0] // 2
            sums = sums[:middle] + links.swap(sums[middle:], bit, 0)
        for bit in [1 << i for i in range(mp.bit_length() - 1)]:
            sums = sums + lax.ppermute(sums, "mp", [(i, i ^ bit) for i in range(mp)])
        sums = sums.T
        if not blocked:
            latents_out, latents_grad = plan.leave(latents_out), plan.leave(latents_grad)
        shape = latents.shape
        return (
            latents_out.reshape(shape),
            latents_grad.reshape(shape),
            grad_qkv,
            grad_out,
            grad_up,
            grad_down,
            sums[:2],
            sums[2:],
        )

    return jax.shard_map(
        body,
        mesh=mesh,
        in_specs=(
            P(None, ("dp", "mp"), None),
            P(None, "dp", None),
            P(None, "dp", None),
            P(None, "dp", "mp"),
            P("dp", "mp"),
            P("dp", "mp"),
            P("dp", "mp"),
            P(None, "dp"),
            P(None, "dp"),
            P(None, ("dp", "mp"), None),
        ),
        out_specs=(
            P(None, ("dp", "mp"), None),
            P(None, ("dp", "mp"), None),
            P(None, "dp", "mp"),
            P("dp", "mp"),
            P("dp", "mp"),
            P("dp", "mp"),
            P(None, "dp"),
            P(None, "dp"),
        ),
        check_vma=False,
    )
```

```python
import jax
import jax.numpy as jnp
from jax import lax
from jax.experimental import pallas as pl
from jax.experimental.pallas import tpu as pltpu
from jax.sharding import PartitionSpec as P

HEAD_DIM = 128
HALO = 128
EPSILON = 1e-05
LOW = jnp.bfloat16


def dot(left, right, dims, kind=jnp.float32):
    return lax.dot_general(
        left, right, ((dims[:1], dims[1:]), ((), ())), preferred_element_type=kind
    )


class Links:
    def __init__(self, dp, mp):
        self.dp, self.mp = dp, mp
        self.last = {}

    def send(self, value, axis, pairs, link, depth):
        before = self.last.setdefault(link, [])
        if depth and len(before) >= depth:
            value, _ = lax.optimization_barrier((value, before[-depth]))
        result = lax.ppermute(value, axis, pairs)
        before.append(result)
        return result

    def swap(self, value, bit, depth=None):
        return self.send(value, "dp", [(i, i ^ bit) for i in range(self.dp)], bit, 0)

    def shift(self, value, step, depth=3):
        pairs = [(i, (i + step) % self.mp) for i in range(self.mp)]
        return self.send(value, "mp", pairs, "z", depth)

    def halo(self, value, depth=0):
        count = self.mp
        before = self.send(value[:, -HALO:], "mp", [(i, i + 1) for i in range(count - 1)], "z", depth)
        after = self.send(value[:, :HALO], "mp", [(i + 1, i) for i in range(count - 1)], "z", depth)
        return before, value, after


class Plan:
    def __init__(self, mesh):
        self.dp = mesh.shape["dp"]
        self.mp = mesh.shape["mp"]
        bits = [1 << i for i in range(self.dp.bit_length() - 1)]
        core, others = bits[:1], bits[1:]
        self.orders = (others + core, others[::-1] + core)
        self.major = core + others[::-1]
        relative = [0]
        for bit in self.major[::-1]:
            relative = relative + [r ^ bit for r in relative]
        self.relative = relative

    def own(self):
        return lax.axis_index("dp")

    def enter(self, value):
        width = value.shape[-1] // self.dp
        axis = value.ndim - 1
        return jnp.concatenate(
            [
                lax.dynamic_slice_in_dim(value, (self.own() ^ r) * width, width, axis)
                for r in self.relative
            ],
            axis=axis,
        )

    def leave(self, value):
        width = value.shape[-1] // self.dp
        axis = value.ndim - 1
        inverse = {r: p for p, r in enumerate(self.relative)}
        table = jnp.array([inverse[r] for r in range(self.dp)], jnp.int32)
        return jnp.concatenate(
            [
                lax.dynamic_slice_in_dim(value, table[self.own() ^ n] * width, width, axis)
                for n in range(self.dp)
            ],
            axis=axis,
        )

    def gather_small(self, links, value):
        for bit in self.major[::-1]:
            value = jnp.concatenate([value, links.swap(value, bit, 0)], axis=0)
        return value

    def spread_columns(self, links, local):
        parts = [local] + [links.shift(local, -k, 0) for k in range(1, self.mp)]
        return self.halves(parts)

    def halves(self, parts):
        half = self.mp // 2
        return [jnp.concatenate(parts[i * half : (i + 1) * half], axis=1) for i in range(2)]


class Gather:
    def __init__(self, plan, links, held):
        self.plan, self.links = plan, links
        self.block = held[0].shape[0]
        self.held = [[h] for h in held]
        self.known = [[0], [0]]
        self.steps = [list(order[:-1]) for order in plan.orders]

    def pieces(self, i, order):
        span = self.held[i][0].shape[0] // self.block
        at = [self.known[i].index(r) for r in order]
        pieces = []
        while at:
            n = at.pop(0)
            count = 1
            while at and at[0] == n + count and (n + count) % span:
                at.pop(0)
                count += 1
            held = self.held[i][n // span]
            first = n % span * self.block
            pieces.append(held if count == span else held[first : first + count * self.block])
        return pieces

    def join(self, i, order):
        pieces = self.pieces(i, order)
        return pieces[0] if len(pieces) == 1 else jnp.concatenate(pieces, axis=0)

    def step(self, tokens=(), second=()):
        for i in range(2):
            bit = self.steps[i][0]
            value = self.join(i, self.known[i])
            value = after(value, *(second if i else tokens))
            self.held[i] = [value, self.links.swap(value, bit)]
            self.known[i] = self.known[i] + [r ^ bit for r in self.known[i]]
            self.steps[i] = self.steps[i][1:]
        return [h[1] for h in self.held]

    def steps_but_last(self, tokens=()):
        received = []
        while len(self.steps[0]) > 1:
            received = self.step(tokens, tokens)
        return received

    def hold(self, tokens):
        for i in range(2):
            self.held[i][1] = after(self.held[i][1], *tokens)

    def finish(self):
        order = self.plan.relative[: self.plan.dp // 2]
        mine = [self.join(i, order) for i in range(2)]
        return [(m, self.links.swap(m, self.plan.major[0])) for m in mine]


class Scatter:
    def __init__(self, plan, links, pairs):
        self.plan, self.links = plan, links
        self.pairs = pairs
        self.kept = [None, None]
        self.bits = [list(order[:-1][::-1]) for order in plan.orders]
        self.remain = [list(plan.major[1:]), list(plan.major[1:])]

    def core(self, i):
        self.kept[i], outs = [], []
        for left, rights in self.pairs:
            middle = left.shape[1] // 2
            sent = dot(left[:, middle:], rights[i], (0, 0)).astype(LOW)
            kept = dot(left[:, :middle], rights[i], (0, 0))
            self.kept[i].append((kept, self.links.swap(sent, self.plan.major[0])))
            outs.append(sent)
        return outs

    def hold(self, i, tokens):
        self.kept[i] = [(k, after(r, *tokens)) for k, r in self.kept[i]]

    def add(self, i):
        self.kept[i] = [
            k[0] + k[1].astype(jnp.float32) if isinstance(k, tuple) else k for k in self.kept[i]
        ]
        return self.kept[i]

    def step(self, i, tokens=()):
        values = self.add(i)
        bit = self.bits[i].pop(0)
        block = values[0].shape[0] >> (self.remain[i].index(bit) + 1)
        shaped = [v.reshape(-1, 2, block, v.shape[1]) for v in values]
        out = [x[:, 1].reshape(-1, v.shape[1]).astype(LOW) for x, v in zip(shaped, values)]
        stay = [x[:, 0].reshape(-1, v.shape[1]) for x, v in zip(shaped, values)]
        out = out[0] if len(out) == 1 else jnp.concatenate(out, axis=1)
        received = self.links.swap(after(out, *tokens), bit)
        self.kept[i], at = [], 0
        for x in stay:
            self.kept[i].append((x, received[:, at : at + x.shape[1]]))
            at += x.shape[1]
        self.remain[i].remove(bit)
        return out

    def steps_but_last(self, i, tokens=()):
        out = None
        while len(self.bits[i]) > 1:
            out = self.step(i, tokens)
        return out

    def rows(self):
        half = self.plan.mp // 2
        result = []
        for pair in zip(*[self.add(i) for i in range(2)]):
            width = pair[0].shape[1] // half
            result.append([r[:, j * width : (j + 1) * width] for r in pair for j in range(half)])
        return result


def own_first(blocks):
    joined = jnp.stack(blocks)
    own = lax.axis_index("mp")
    return [
        lax.dynamic_index_in_dim(joined, lax.rem(own + k, len(blocks)), 0, keepdims=False)
        for k in range(len(blocks))
    ]


def shift_blocks(plan, links, products, tokens=()):
    outs, received = [], []
    for k in range(1, plan.mp):
        out = [blocks[k].astype(LOW) for blocks in products]
        out = out[0] if len(out) == 1 else jnp.concatenate(out, axis=1)
        outs.append(out)
        received.append(links.shift(after(out, *tokens), k, 0))
    result, at = [], 0
    for blocks in products:
        total = blocks[0]
        for part in received:
            total = total + part[:, at : at + total.shape[1]].astype(jnp.float32)
        result.append(total)
        at += total.shape[1]
    return result, outs


def reduce_blocks(blocks):
    return lax.psum_scatter(jnp.stack(blocks), "mp", scatter_dimension=0, tiled=False)


def after(value, *tokens):
    if not tokens:
        return value
    return lax.optimization_barrier((value, *tokens))[0]


def split_dot(left, top, bottom):
    half = top.shape[0]
    return dot(left[:, :half], top, (1, 0)) + dot(left[:, half:], bottom, (1, 0))


A_X2 = 1
A_CORE = 0
A_DOWN = 1
B_DOWN = 1
B_UADD = 1
Z_LAST = 1
D_SUMS = 1
MEGA = 1 << 20
LOG2E = 1.4426950408889634
VM_FWD = 36
VM_UP = 20
VM_DOWN = 20
VM_BACK = 32
VM_BWD = 36
VM_ENTER = 20


def params(limit=56):
    return pltpu.CompilerParams(vmem_limit_bytes=limit * MEGA)


def cost(flops, bytes_accessed, transcendentals=0):
    return pl.CostEstimate(
        flops=int(flops), bytes_accessed=int(bytes_accessed), transcendentals=int(transcendentals)
    )


def whole(*shape):
    return pl.BlockSpec(shape, lambda *_: (0,) * len(shape), pipeline_mode=pl.Buffered(1))


def statistics(values):
    mean = jnp.mean(values, axis=-1, keepdims=True)
    centred = values - mean
    variance = jnp.mean(centred * centred, axis=-1, keepdims=True)
    return centred, lax.rsqrt(variance + EPSILON)


def norm_rows(values, gain, bias):
    centred, scale = statistics(values)
    return centred * scale * gain + bias


def norm_back(values, gain, grad):
    centred, scale = statistics(values)
    normed = centred * scale
    inner = grad * gain
    first = jnp.mean(inner, axis=-1, keepdims=True)
    second = jnp.mean(inner * normed, axis=-1, keepdims=True)
    return (inner - first - normed * second) * scale, grad * normed, grad


def fold(rows):
    total = rows[:8]
    for i in range(1, rows.shape[0] // 8):
        total = total + rows[i * 8 : i * 8 + 8]
    return total


ROWS = 64


def store_blocks(ref, start, value, table, inverse=None):
    if table is None:
        ref[pl.ds(start, value.shape[0]), :] = value
        return
    count = table.shape[0]
    block = value.shape[1] // count
    for p in range(count):
        at = pl.multiple_of(table[p] * block, block)
        ref[pl.ds(start, value.shape[0]), pl.ds(at, block)] = value[:, p * block : (p + 1) * block]


def load_blocks(ref, start, size, table):
    if table is None:
        return ref[pl.ds(start, size), :]
    count = table.shape[0]
    block = ref.shape[1] // count
    parts = []
    for p in range(count):
        at = pl.multiple_of(table[p] * block, block)
        parts.append(ref[pl.ds(start, size), pl.ds(at, block)])
    return jnp.concatenate(parts, axis=1)


def enter_kernel(blocked):
    def kernel(table_ref, latents, grads, small, entered, entered_grads, grad_z, inputs_a):
        table = table_ref if blocked else None

        @pl.loop(0, latents.shape[0] // ROWS)
        def _(i):
            start = pl.multiple_of(i * ROWS, ROWS)
            at = pl.ds(start, ROWS)
            values = load_blocks(latents, start, ROWS, table)
            entered[at, :] = values
            inputs_a[at, :] = norm_rows(values, small[0:1], small[2:3]).astype(LOW)
            values = load_blocks(grads, start, ROWS, table)
            entered_grads[at, :] = values
            grad_z[at, :] = values.astype(LOW)

    return kernel


def enter_norm(table, blocked, latents, grads, small):
    total, width = latents.shape
    rows = 256
    spec = pl.BlockSpec((rows, width), lambda i, *_: (i, 0))
    shape = lambda kind: jax.ShapeDtypeStruct((total, width), kind)
    return pl.pallas_call(
        enter_kernel(blocked),
        name="enter",
        grid_spec=pltpu.PrefetchScalarGridSpec(
            num_scalar_prefetch=1,
            grid=(total // rows,),
            in_specs=[spec, spec, whole(4, width)],
            out_specs=[spec] * 4,
        ),
        out_shape=[shape(jnp.float32), shape(jnp.float32), shape(LOW), shape(LOW)],
        compiler_params=params(VM_ENTER),
        cost_estimate=cost(total * width * 16, total * width * 20),
    )(table, latents, grads, small)


def attention_weights(q, k, bias, factor):
    scores = dot(q, k, (1, 1)) * (factor * LOG2E) + bias
    peak = jnp.max(scores, axis=-1, keepdims=True)
    weights = jnp.exp2(scores - peak)
    return weights * (1.0 / jnp.sum(weights, axis=-1, keepdims=True))


def window_bias(group_column, key_row):
    span = group_column.shape[0]
    place = lax.broadcasted_iota(jnp.int32, (span, span), 0)
    other = lax.broadcasted_iota(jnp.int32, (span, span), 1)
    allowed = (group_column == key_row) | (place == other)
    return jnp.where(allowed, 0.0, -1e30)


def column_halves(rows, tile, count):
    return (
        pl.BlockSpec((rows, tile), lambda k, *_: (0, jnp.minimum(k, count - 1))),
        pl.BlockSpec((rows, tile), lambda k, *_: (0, jnp.clip(k - count, 0, count - 1))),
    )


def either(step, count, work, first, second):
    @pl.when(step < count)
    def _():
        work(*first)

    @pl.when((step >= count) & (step < 2 * count))
    def _():
        work(*second)


def project(window, w_top, w_bottom, target, index, rows):
    before, own, after = window
    target[0:HALO] = split_dot(before[index], w_top, w_bottom).astype(LOW)
    target[HALO : HALO + rows] = split_dot(own[index], w_top, w_bottom).astype(LOW)
    target[HALO + rows :] = split_dot(after[index], w_top, w_bottom).astype(LOW)


def forward_kernel(rows, steps, local_heads, factor):
    def kernel(before, own, after, top_a, bottom_a, top_b, bottom_b, column, row, start, small,
               saved, attended, resid, inputs_c, bias, total):
        step, index = pl.program_id(0), pl.program_id(1)
        group = local_heads * HEAD_DIM
        wide = 3 * group
        half = top_a.shape[0]
        target = saved.at[0]

        @pl.when(step == 0)
        def _():
            bias[index] = window_bias(column[index], row[index])
            total[index] = jnp.zeros((rows, 2 * half), jnp.float32)

        mine = slice(HALO, HALO + rows)

        def work(top, bottom):
            project((before, own, after), top[:, :wide], bottom[:, :wide], target, index, rows)
            for h in range(local_heads):
                at = slice(h * HEAD_DIM, (h + 1) * HEAD_DIM)
                q = target[mine, at]
                k = target[:, group + h * HEAD_DIM : group + (h + 1) * HEAD_DIM]
                v = target[:, 2 * group + h * HEAD_DIM : 2 * group + (h + 1) * HEAD_DIM]
                p = attention_weights(q, k, bias[index, mine, :], factor).astype(LOW)
                attended[0, :, at] = dot(p, v, (1, 0)).astype(LOW)
            total[index, :, :half] += dot(attended[0], top[:, wide:], (1, 1))
            total[index, :, half:] += dot(attended[0], bottom[:, wide:], (1, 1))

        @pl.when(step < steps // 2)
        def _():
            work(top_a, bottom_a)

        @pl.when(step >= steps // 2)
        def _():
            work(top_b, bottom_b)

        @pl.when(step == steps - 1)
        def _():
            @pl.loop(0, rows // ROWS)
            def _(i):
                at = pl.ds(pl.multiple_of(i * ROWS, ROWS), ROWS)
                values = total[index, at, :] + start[at, :]
                resid[at, :] = values
                inputs_c[at, :] = norm_rows(values, small[1:2], small[3:4]).astype(LOW)

    return kernel


def forward_block(window, weights, column, row, start, small, steps, factor):
    before, own, after = window
    micro, rows, width = own.shape
    span = rows + 2 * HALO
    total = micro * rows
    half = steps // 2
    c = weights[0][0].shape[1] // half
    g = c // 4
    late = pl.BlockSpec((rows, width), lambda k, i: (jnp.where(k == steps - 1, i, 0), 0))
    weight_a, weight_b = column_halves(width // 2, c, half)
    return pl.pallas_call(
        forward_kernel(rows, steps, g // HEAD_DIM, factor),
        name="attention_forward",
        grid=(steps, micro),
        in_specs=[
            whole(*before.shape), whole(*own.shape), whole(*after.shape),
            weight_a, weight_a, weight_b, weight_b,
            whole(*column.shape), whole(*row.shape),
            late,
            whole(4, width),
        ],
        out_specs=[
            pl.BlockSpec((1, span, 3 * g), lambda k, i: (i, 0, k)),
            pl.BlockSpec((1, rows, g), lambda k, i: (k // half, i, k % half)),
            late,
            late,
        ],
        out_shape=[
            jax.ShapeDtypeStruct((micro, span, 3 * g * steps), LOW),
            jax.ShapeDtypeStruct((2, total, g * half), LOW),
            jax.ShapeDtypeStruct((total, width), jnp.float32),
            jax.ShapeDtypeStruct((total, width), LOW),
        ],
        scratch_shapes=[
            pltpu.VMEM((micro, span, span), jnp.float32),
            pltpu.VMEM((micro, rows, width), jnp.float32),
        ],
        compiler_params=params(VM_FWD),
        cost_estimate=cost(
            2 * micro * steps * g * (span * width * 3 + rows * width + 2 * rows * span),
            30 * MEGA,
            micro * rows * span * steps * g // HEAD_DIM,
        ),
    )(before, own, after, *weights[0], *weights[1], column, row, start, small)


def up_kernel(count):
    def kernel(inputs, top_a, bottom_a, top_b, bottom_b, hidden, slope):
        def work(top, bottom):
            u = split_dot(inputs[...], top[...], bottom[...])
            c = 0.7978845608028654
            square = u * u
            t = jnp.tanh(u * (c + c * 0.044715 * square))
            half = 0.5 + 0.5 * t
            hidden[0] = (u * half).astype(LOW)
            inner = 0.5 * c + 1.5 * c * 0.044715 * square
            slope[0] = (half + u * inner * (1.0 - t * t)).astype(LOW)

        either(pl.program_id(0), count, work, (top_a, bottom_a), (top_b, bottom_b))

    return kernel


def feed_up(inputs, weights, tile=512):
    total, width = inputs.shape
    ff = 2 * weights[0][0].shape[1]
    count = ff // 2 // tile
    block = pl.BlockSpec((1, total, tile), lambda j: (j // count, 0, j % count))
    weight_a, weight_b = column_halves(width // 2, tile, count)
    return pl.pallas_call(
        up_kernel(count),
        name="feed_up",
        grid=(ff // tile,),
        in_specs=[whole(total, width), weight_a, weight_a, weight_b, weight_b],
        out_specs=[block, block],
        out_shape=[jax.ShapeDtypeStruct((2, total, ff // 2), LOW)] * 2,
        compiler_params=params(VM_UP),
        cost_estimate=cost(2 * total * width * ff, 2 * (width * ff + 2 * total * ff), total * ff),
    )(inputs, *weights[0], *weights[1])


LATE = 256


def down_kernel(blocked, steps):
    def kernel(table_ref, hidden, top_a, bottom_a, top_b, bottom_b, start_rows, out, total):
        step = pl.program_id(0)
        half = top_a.shape[0]

        @pl.when(step == 0)
        def _():
            total[...] = jnp.zeros_like(total)

        def work(top, bottom):
            total[:, :half] += dot(hidden[0], top[...], (1, 1))
            total[:, half:] += dot(hidden[0], bottom[...], (1, 1))

        either(step, steps // 2, work, (top_a, bottom_a), (top_b, bottom_b))

        @pl.when(step >= steps)
        def _():
            base = (step - steps) * LATE

            @pl.loop(0, LATE // ROWS)
            def _(i):
                start = pl.multiple_of(i * ROWS, ROWS)
                at = pl.ds(pl.multiple_of(base + start, ROWS), ROWS)
                values = total[at, :] + start_rows[pl.ds(start, ROWS), :]
                store_blocks(out, start, values, table_ref if blocked else None)

    return kernel


def feed_down(table, blocked, hidden, weights, start, tile=512):
    total, width = start.shape
    ff = 2 * hidden.shape[2]
    steps = ff // tile
    count = steps // 2
    clip = lambda j: jnp.minimum(j, steps - 1)
    late = pl.BlockSpec((LATE, width), lambda j, *_: (jnp.maximum(j - steps, 0), 0))
    weight_a, weight_b = column_halves(width // 2, tile, count)
    return pl.pallas_call(
        down_kernel(blocked, steps),
        name="feed_down",
        grid_spec=pltpu.PrefetchScalarGridSpec(
            num_scalar_prefetch=1,
            grid=(steps + total // LATE,),
            in_specs=[
                pl.BlockSpec((1, total, tile), lambda j, *_: (clip(j) // count, 0, clip(j) % count)),
                weight_a, weight_a, weight_b, weight_b,
                late,
            ],
            out_specs=late,
            scratch_shapes=[pltpu.VMEM((total, width), jnp.float32)],
        ),
        out_shape=jax.ShapeDtypeStruct((total, width), jnp.float32),
        compiler_params=params(VM_DOWN),
        cost_estimate=cost(2 * total * width * ff, 2 * (width * ff + total * ff) + 8 * total * width),
    )(table, hidden, *weights[0], *weights[1], start)


def slope_kernel(count):
    def kernel(grad_z, top_a, bottom_a, top_b, bottom_b, slope, grad_upward):
        def work(top, bottom):
            grad = split_dot(grad_z[...], top[...], bottom[...]) * slope[0].astype(jnp.float32)
            grad_upward[0] = grad.astype(LOW)

        either(pl.program_id(0), count, work, (top_a, bottom_a), (top_b, bottom_b))

    return kernel


def feed_slope(grad_z, down, slope, tile=512):
    total, width = grad_z.shape
    ff = 2 * slope.shape[2]
    count = ff // 2 // tile
    block = pl.BlockSpec((1, total, tile), lambda j: (j // count, 0, j % count))
    weight_a, weight_b = column_halves(width // 2, tile, count)
    return pl.pallas_call(
        slope_kernel(count),
        name="feed_slope",
        grid=(ff // tile,),
        in_specs=[whole(total, width), weight_a, weight_a, weight_b, weight_b, block],
        out_specs=block,
        out_shape=jax.ShapeDtypeStruct((2, total, ff // 2), LOW),
        compiler_params=params(VM_UP),
        cost_estimate=cost(2 * total * width * ff, 2 * (width * ff + 2 * total * ff)),
    )(grad_z, *down[0], *down[1], slope)


def feed_back_kernel(steps):
    def kernel(upward, top_a, bottom_a, top_b, bottom_b, resid, grads, small,
               grad_resid, grad_branch, sums, total):
        step = pl.program_id(0)
        half = top_a.shape[0]

        @pl.when(step == 0)
        def _():
            total[...] = jnp.zeros_like(total)
            sums[...] = jnp.zeros_like(sums)

        def work(top, bottom):
            total[:, :half] += dot(upward[0], top[...], (1, 1))
            total[:, half:] += dot(upward[0], bottom[...], (1, 1))

        either(step, steps // 2, work, (top_a, bottom_a), (top_b, bottom_b))

        @pl.when(step >= steps)
        def _():
            base = (step - steps) * LATE

            @pl.loop(0, LATE // ROWS)
            def _(i):
                start = pl.multiple_of(i * ROWS, ROWS)
                at = pl.ds(start, ROWS)
                grad = total[pl.ds(pl.multiple_of(base + start, ROWS), ROWS), :]
                back, by_gain, by_bias = norm_back(resid[at, :], small[1:2], grad)
                back = back + grads[at, :]
                grad_resid[at, :] = back
                grad_branch[at, :] = back.astype(LOW)
                sums[0:8] += fold(by_gain)
                sums[8:16] += fold(by_bias)

    return kernel


def feed_back(upward, up, resid, grads, small, tile=512):
    total, width = resid.shape
    ff = 2 * upward.shape[2]
    steps = ff // tile
    count = steps // 2
    clip = lambda j: jnp.minimum(j, steps - 1)
    weight_a, weight_b = column_halves(width // 2, tile, count)
    block = pl.BlockSpec((1, total, tile), lambda j: (clip(j) // count, 0, clip(j) % count))
    late = pl.BlockSpec((LATE, width), lambda j: (jnp.maximum(j - steps, 0), 0))
    return pl.pallas_call(
        feed_back_kernel(steps),
        name="feed_back",
        grid=(steps + total // LATE,),
        in_specs=[block, weight_a, weight_a, weight_b, weight_b, late, late, whole(4, width)],
        out_specs=[late, late, whole(16, width)],
        out_shape=[
            jax.ShapeDtypeStruct((total, width), jnp.float32),
            jax.ShapeDtypeStruct((total, width), LOW),
            jax.ShapeDtypeStruct((16, width), jnp.float32),
        ],
        scratch_shapes=[pltpu.VMEM((total, width), jnp.float32)],
        compiler_params=params(VM_DOWN),
        cost_estimate=cost(2 * total * width * ff, 2 * (width * ff + total * ff) + 14 * total * width),
    )(upward, *up[0], *up[1], resid, grads, small)


def backward_kernel(rows, steps, local_heads, factor):
    def kernel(before, own, after, top_a, bottom_a, top_b, bottom_b, column, row, saved,
               grad_projected, out, bias, grad_att):
        step, index = pl.program_id(0), pl.program_id(1)
        group = local_heads * HEAD_DIM
        wide = 3 * group
        half = top_a.shape[0]
        at_rows = pl.ds(pl.multiple_of(index * rows, rows), rows)

        @pl.when(step == 0)
        def _():
            bias[index] = window_bias(column[index], row[index])
            out[at_rows, :] = jnp.zeros((rows, 2 * half), jnp.float32)

        mine = slice(HALO, HALO + rows)

        def work(top, bottom):
            project((before, own, after), top[:, wide:], bottom[:, wide:], grad_att, index, rows)
            for h in range(local_heads):
                at = slice(h * HEAD_DIM, (h + 1) * HEAD_DIM)
                at_k = slice(group + h * HEAD_DIM, group + (h + 1) * HEAD_DIM)
                at_v = slice(2 * group + h * HEAD_DIM, 2 * group + (h + 1) * HEAD_DIM)
                q, k, v = saved[0, :, at], saved[0, :, at_k], saved[0, :, at_v]
                grad_mix = grad_att[:, at]
                p = attention_weights(q, k, bias[index], factor)
                grad_p = dot(grad_mix, v, (1, 1))
                weighted = jnp.sum(p * grad_p, axis=-1, keepdims=True)
                grad_s = (p * (grad_p - weighted)).astype(LOW)
                grad_projected[0, :, at] = (dot(grad_s[mine], k, (1, 0)) * factor).astype(LOW)
                grad_projected[0, :, at_k] = (dot(grad_s[:, mine], q, (0, 0)) * factor).astype(LOW)
                grad_projected[0, :, at_v] = dot(p[:, mine].astype(LOW), grad_mix, (0, 0)).astype(LOW)
            out[at_rows, :half] += dot(grad_projected[0], top[:, :wide], (1, 1))
            out[at_rows, half:] += dot(grad_projected[0], bottom[:, :wide], (1, 1))

        either(step, steps // 2, work, (top_a, bottom_a), (top_b, bottom_b))

    return kernel


def backward_block(window, weights, column, row, saved, steps, factor):
    before, own, after = window
    micro, rows, width = own.shape
    span = rows + 2 * HALO
    total = micro * rows
    half = steps // 2
    c = weights[0][0].shape[1] // half
    g = c // 4
    weight_a, weight_b = column_halves(width // 2, c, half)
    return pl.pallas_call(
        backward_kernel(rows, steps, g // HEAD_DIM, factor),
        name="attention_backward",
        grid=(steps, micro),
        in_specs=[
            whole(*before.shape), whole(*own.shape), whole(*after.shape),
            weight_a, weight_a, weight_b, weight_b,
            whole(*column.shape), whole(*row.shape),
            pl.BlockSpec((1, span, 3 * g), lambda k, i: (i, 0, k)),
        ],
        out_specs=[
            pl.BlockSpec((1, rows, 3 * g), lambda k, i: (k // half, i, k % half)),
            whole(total, width),
        ],
        scratch_shapes=[
            pltpu.VMEM((micro, span, span), jnp.float32),
            pltpu.VMEM((span, g), LOW),
        ],
        out_shape=[
            jax.ShapeDtypeStruct((2, total, 3 * g * half), LOW),
            jax.ShapeDtypeStruct((total, width), jnp.float32),
        ],
        compiler_params=params(VM_BWD),
        cost_estimate=cost(
            2 * micro * steps * g * (span * width + rows * width * 3 + 4 * span * span),
            35 * MEGA,
            micro * span * span * steps * g // HEAD_DIM,
        ),
    )(before, own, after, *weights[0], *weights[1], column, row, saved)


def leave_kernel(blocked):
    def kernel(table_ref, norm_one, entered, grad_resid, small, latents_grad, sums):
        @pl.when(pl.program_id(0) == 0)
        def _():
            sums[...] = jnp.zeros_like(sums)

        @pl.loop(0, entered.shape[0] // ROWS)
        def _(i):
            start = pl.multiple_of(i * ROWS, ROWS)
            at = pl.ds(start, ROWS)
            back, by_gain, by_bias = norm_back(entered[at, :], small[0:1], norm_one[at, :])
            store_blocks(latents_grad, start, back + grad_resid[at, :], table_ref if blocked else None)
            sums[0:8] += fold(by_gain)
            sums[8:16] += fold(by_bias)

    return kernel


def leave_norm(table, blocked, norm_one, entered, grad_resid, small):
    total, width = entered.shape
    rows = 128
    spec = pl.BlockSpec((rows, width), lambda i, *_: (i, 0))
    return pl.pallas_call(
        leave_kernel(blocked),
        name="leave",
        grid_spec=pltpu.PrefetchScalarGridSpec(
            num_scalar_prefetch=1,
            grid=(total // rows,),
            in_specs=[spec, spec, spec, whole(4, width)],
            out_specs=[spec, whole(16, width)],
        ),
        out_shape=[
            jax.ShapeDtypeStruct((total, width), jnp.float32),
            jax.ShapeDtypeStruct((16, width), jnp.float32),
        ],
        compiler_params=params(VM_ENTER),
        cost_estimate=cost(total * width * 30, total * width * 16),
    )(table, norm_one, entered, grad_resid, small)


def solution(mesh):
    plan = Plan(mesh)

    def body(latents, group_ids, pad_mask, w_qkv, w_out, w_up, w_down, norm_gain, norm_bias, out_grad):
        micro, rows, width = latents.shape
        total = micro * rows
        mp = plan.mp
        factor = HEAD_DIM ** (-0.5)
        links = Links(plan.dp, mp)
        small = jnp.concatenate([norm_gain, norm_bias], axis=0).T
        small = plan.gather_small(links, small).T.astype(jnp.float32)

        blocked = width // plan.dp % 128 == 0
        table = plan.own() ^ jnp.array(plan.relative, jnp.int32)
        rows_in = (latents.reshape(total, width), out_grad.reshape(total, width))
        if not blocked:
            rows_in = tuple(plan.enter(v) for v in rows_in)
        local = jnp.concatenate([w_qkv[0], w_qkv[1], w_qkv[2], w_out], axis=1)

        def columns_of(weight):
            columns = lax.all_gather(weight, "mp", axis=0)
            return plan.halves([columns[k] for k in range(mp)])

        halves = plan.spread_columns(links, local)
        gather_attention = Gather(plan, links, halves)
        up_halves = columns_of(w_up)
        entered, grad_rows, grad_z, inputs_a = enter_norm(table, blocked, *rows_in, small)
        gather_attention.steps_but_last([small])
        window = links.halo(inputs_a.reshape(micro, rows, width))
        down_halves = columns_of(w_down)
        halos = [window[0], window[2]]
        gather_attention.step(halos if A_X2 else [inputs_a], [inputs_a])
        gather_up = Gather(plan, links, up_halves)
        gather_down = Gather(plan, links, down_halves)
        tokens_up = gather_up.steps_but_last([inputs_a])
        gather_attention.hold(tokens_up + halos if A_CORE else halos)
        attention = gather_attention.finish()

        span = rows + 2 * HALO
        first = lax.axis_index("mp") * rows
        pads = ((0, 0), (HALO, HALO))
        groups = jnp.pad(group_ids[:, 0], pads, constant_values=-1)
        keys = jnp.where(jnp.pad(pad_mask[:, 0], pads) == 1, groups, -2)
        groups = lax.dynamic_slice_in_dim(groups, first, span, 1)
        keys = lax.dynamic_slice_in_dim(keys, first, span, 1)
        column, row = groups[:, :, None], keys[:, None, :]

        saved, attended, resid, inputs_c = forward_block(
            window, attention, after(column, *tokens_up, *down_halves), row, entered, small, mp, factor
        )
        early_down = gather_down.steps_but_last()
        gather_up.step()
        gather_up.hold([inputs_c] + early_down * A_DOWN)
        up = gather_up.finish()
        late_down = gather_down.step()
        hidden, slope = feed_up(after(inputs_c, *early_down), up)
        gather_down.hold([hidden])
        down = gather_down.finish()
        left = after(grad_z, *late_down) if B_DOWN else grad_z
        grad_down = Scatter(plan, links, [(left, [hidden[0], hidden[1]])])
        sent = grad_down.core(0) + grad_down.core(1)
        upward = feed_slope(after(grad_z, *sent), down, slope)
        for i in range(2):
            grad_down.hold(i, [upward])
        tokens = [grad_down.steps_but_last(i) for i in range(2)]
        left = after(inputs_c, *tokens)
        grad_up = Scatter(plan, links, [(left, [upward[0], upward[1]])])
        tokens = tokens + grad_up.core(0) + grad_up.core(1)
        if B_UADD:
            tokens += grad_up.add(0) + grad_up.add(1)
        grad_resid, grad_branch, sums_two = feed_back(
            upward, up, after(resid, *tokens), grad_rows, small
        )
        branch = links.halo(grad_branch.reshape(micro, rows, width))
        halos = [branch[0], branch[2]]
        for i in range(2):
            grad_down.hold(i, [grad_branch])
        tokens = [grad_down.step(i) for i in range(2)]
        latents_out = feed_down(table, blocked, after(hidden, *tokens), down, resid)
        for i in range(2):
            grad_down.hold(i, [latents_out])
        tokens = halos + [latents_out]
        left = after(grad_branch, *tokens)
        grad_out = Scatter(plan, links, [(left, [attended[0], attended[1]])])
        down_rows = grad_down.rows()[0]
        for i in range(2):
            if not B_UADD:
                grad_up.hold(i, [latents_out])
            grad_out.core(i)
            grad_up.kept[i] += grad_out.kept[i]
        tokens = [grad_up.steps_but_last(i) for i in range(2)]
        projected, norm_one = backward_block(
            branch, attention, after(column, *tokens, *down_rows), row, saved, mp, factor
        )
        grad_down = reduce_blocks(down_rows)
        for i in range(2):
            grad_up.hold(i, [norm_one])
        tokens = [grad_up.step(i) for i in range(2)]
        left = after(inputs_a, *tokens)
        grad_qkv = Scatter(plan, links, [(left, [projected[0], projected[1]])])
        grad_qkv.core(0)
        grad_qkv.core(1)
        tokens = [grad_qkv.steps_but_last(i) for i in range(2)]
        for i in range(2):
            grad_up.hold(i, tokens)
        up_rows, out_rows = grad_up.rows()
        (grad_up,), outs = shift_blocks(plan, links, [own_first(up_rows)])
        latents_grad, sums_one = leave_norm(
            table, blocked, after(norm_one, *outs), entered, grad_resid, small
        )
        for i in range(2):
            grad_qkv.hold(i, [latents_grad])
        tokens = [grad_qkv.step(i) for i in range(2)]
        qkv_rows = grad_qkv.rows()[0]
        (grad_qkv, grad_out), outs = shift_blocks(
            plan, links, [qkv_rows, out_rows], [grad_up] if Z_LAST else []
        )
        sums = jnp.stack([sums_one, sums_two], axis=0).reshape(2, 2, 8, width).sum(axis=2)
        sums = sums.transpose(1, 0, 2).reshape(4, width).T
        sums = after(sums, *(tokens if D_SUMS == 1 else outs if D_SUMS == 3 else [grad_up]))
        for bit in plan.major:
            middle = sums.shape[0] // 2
            sums = sums[:middle] + links.swap(sums[middle:], bit, 0)
        for bit in [1 << i for i in range(mp.bit_length() - 1)]:
            sums = sums + lax.ppermute(sums, "mp", [(i, i ^ bit) for i in range(mp)])
        grad_qkv = jnp.stack(jnp.split(grad_qkv, 3, axis=1))
        sums = sums.T
        if not blocked:
            latents_out, latents_grad = plan.leave(latents_out), plan.leave(latents_grad)
        shape = latents.shape
        return (
            latents_out.reshape(shape),
            latents_grad.reshape(shape),
            grad_qkv,
            grad_out,
            grad_up,
            grad_down,
            sums[:2],
            sums[2:],
        )

    return jax.shard_map(
        body,
        mesh=mesh,
        in_specs=(
            P(None, ("dp", "mp"), None),
            P(None, "dp", None),
            P(None, "dp", None),
            P(None, "dp", "mp"),
            P("dp", "mp"),
            P("dp", "mp"),
            P("dp", "mp"),
            P(None, "dp"),
            P(None, "dp"),
            P(None, ("dp", "mp"), None),
        ),
        out_specs=(
            P(None, ("dp", "mp"), None),
            P(None, ("dp", "mp"), None),
            P(None, "dp", "mp"),
            P("dp", "mp"),
            P("dp", "mp"),
            P("dp", "mp"),
            P(None, "dp"),
            P(None, "dp"),
        ),
        check_vma=False,
    )
```

```python
import jax
import jax.numpy as jnp
from jax import lax
from jax.experimental import pallas as pl
from jax.experimental.pallas import tpu as pltpu
from jax.sharding import PartitionSpec as P

HEAD_DIM = 128
HALO = 128
EPSILON = 1e-05
LOW = jnp.bfloat16


def dot(left, right, dims, kind=jnp.float32):
    return lax.dot_general(
        left, right, ((dims[:1], dims[1:]), ((), ())), preferred_element_type=kind
    )


class Links:
    def __init__(self, dp, mp):
        self.dp, self.mp = dp, mp
        self.last = {}

    def send(self, value, axis, pairs, link, depth):
        before = self.last.setdefault(link, [])
        if depth and len(before) >= depth:
            value, _ = lax.optimization_barrier((value, before[-depth]))
        result = lax.ppermute(value, axis, pairs)
        before.append(result)
        return result

    def swap(self, value, bit, depth=None):
        return self.send(value, "dp", [(i, i ^ bit) for i in range(self.dp)], bit, 0)

    def shift(self, value, step, depth=3):
        pairs = [(i, (i + step) % self.mp) for i in range(self.mp)]
        return self.send(value, "mp", pairs, "z", depth)

    def halo(self, value, depth=0):
        count = self.mp
        before = self.send(value[:, -HALO:], "mp", [(i, i + 1) for i in range(count - 1)], "z", depth)
        after = self.send(value[:, :HALO], "mp", [(i + 1, i) for i in range(count - 1)], "z", depth)
        return before, value, after


class Plan:
    def __init__(self, mesh):
        self.dp = mesh.shape["dp"]
        self.mp = mesh.shape["mp"]
        bits = [1 << i for i in range(self.dp.bit_length() - 1)]
        core, others = bits[:1], bits[1:]
        self.orders = (others + core, others[::-1] + core)
        self.major = core + others[::-1]
        relative = [0]
        for bit in self.major[::-1]:
            relative = relative + [r ^ bit for r in relative]
        self.relative = relative

    def own(self):
        return lax.axis_index("dp")

    def enter(self, value):
        width = value.shape[-1] // self.dp
        axis = value.ndim - 1
        return jnp.concatenate(
            [
                lax.dynamic_slice_in_dim(value, (self.own() ^ r) * width, width, axis)
                for r in self.relative
            ],
            axis=axis,
        )

    def leave(self, value):
        width = value.shape[-1] // self.dp
        axis = value.ndim - 1
        inverse = {r: p for p, r in enumerate(self.relative)}
        table = jnp.array([inverse[r] for r in range(self.dp)], jnp.int32)
        return jnp.concatenate(
            [
                lax.dynamic_slice_in_dim(value, table[self.own() ^ n] * width, width, axis)
                for n in range(self.dp)
            ],
            axis=axis,
        )

    def gather_small(self, links, value):
        for bit in self.major[::-1]:
            value = jnp.concatenate([value, links.swap(value, bit, 0)], axis=0)
        return value

    def spread_columns(self, links, local):
        parts = [local] + [links.shift(local, -k, 0) for k in range(1, self.mp)]
        return self.halves(parts)

    def halves(self, parts):
        half = self.mp // 2
        return [jnp.concatenate(parts[i * half : (i + 1) * half], axis=1) for i in range(2)]


class Gather:
    def __init__(self, plan, links, held):
        self.plan, self.links = plan, links
        self.block = held[0].shape[0]
        self.held = [[h] for h in held]
        self.known = [[0], [0]]
        self.steps = [list(order[:-1]) for order in plan.orders]

    def pieces(self, i, order):
        span = self.held[i][0].shape[0] // self.block
        at = [self.known[i].index(r) for r in order]
        pieces = []
        while at:
            n = at.pop(0)
            count = 1
            while at and at[0] == n + count and (n + count) % span:
                at.pop(0)
                count += 1
            held = self.held[i][n // span]
            first = n % span * self.block
            pieces.append(held if count == span else held[first : first + count * self.block])
        return pieces

    def join(self, i, order):
        pieces = self.pieces(i, order)
        return pieces[0] if len(pieces) == 1 else jnp.concatenate(pieces, axis=0)

    def step(self, tokens=(), second=()):
        for i in range(2):
            bit = self.steps[i][0]
            value = self.join(i, self.known[i])
            value = after(value, *(second if i else tokens))
            self.held[i] = [value, self.links.swap(value, bit)]
            self.known[i] = self.known[i] + [r ^ bit for r in self.known[i]]
            self.steps[i] = self.steps[i][1:]
        return [h[1] for h in self.held]

    def steps_but_last(self, tokens=()):
        received = []
        while len(self.steps[0]) > 1:
            received = self.step(tokens, tokens)
        return received

    def hold(self, tokens):
        for i in range(2):
            self.held[i][1] = after(self.held[i][1], *tokens)

    def finish(self):
        order = self.plan.relative[: self.plan.dp // 2]
        mine = [self.join(i, order) for i in range(2)]
        return [(m, self.links.swap(m, self.plan.major[0])) for m in mine]


class Scatter:
    def __init__(self, plan, links, pairs):
        self.plan, self.links = plan, links
        self.pairs = pairs
        self.kept = [None, None]
        self.bits = [list(order[:-1][::-1]) for order in plan.orders]
        self.remain = [list(plan.major[1:]), list(plan.major[1:])]

    def core(self, i):
        self.kept[i], outs = [], []
        for left, rights in self.pairs:
            middle = left.shape[1] // 2
            sent = dot(left[:, middle:], rights[i], (0, 0)).astype(LOW)
            kept = dot(left[:, :middle], rights[i], (0, 0))
            self.kept[i].append((kept, self.links.swap(sent, self.plan.major[0]), 0))
            outs.append(sent)
        return outs

    def hold(self, i, tokens):
        self.kept[i] = [(k, after(r, *tokens), at) for k, r, at in self.kept[i]]

    def add(self, i):
        self.kept[i] = [
            k[0] + k[1][:, k[2] : k[2] + k[0].shape[1]].astype(jnp.float32) if isinstance(k, tuple) else k
            for k in self.kept[i]
        ]
        return self.kept[i]

    def step(self, i, tokens=()):
        values = self.add(i)
        bit = self.bits[i].pop(0)
        block = values[0].shape[0] >> (self.remain[i].index(bit) + 1)
        shaped = [v.reshape(-1, 2, block, v.shape[1]) for v in values]
        out = [x[:, 1].reshape(-1, v.shape[1]).astype(LOW) for x, v in zip(shaped, values)]
        stay = [x[:, 0].reshape(-1, v.shape[1]) for x, v in zip(shaped, values)]
        out = out[0] if len(out) == 1 else jnp.concatenate(out, axis=1)
        received = self.links.swap(after(out, *tokens), bit)
        self.kept[i], at = [], 0
        for x in stay:
            self.kept[i].append((x, received, at))
            at += x.shape[1]
        self.remain[i].remove(bit)
        return out

    def steps_but_last(self, i, tokens=()):
        out = None
        while len(self.bits[i]) > 1:
            out = self.step(i, tokens)
        return out

    def rows(self):
        half = self.plan.mp // 2
        result = []
        for pair in zip(*[self.add(i) for i in range(2)]):
            width = pair[0].shape[1] // half
            result.append([r[:, j * width : (j + 1) * width] for r in pair for j in range(half)])
        return result


def own_first(blocks):
    joined = jnp.stack(blocks)
    own = lax.axis_index("mp")
    return [
        lax.dynamic_index_in_dim(joined, lax.rem(own + k, len(blocks)), 0, keepdims=False)
        for k in range(len(blocks))
    ]


def shift_blocks(plan, links, products, tokens=()):
    outs, received = [], []
    for k in range(1, plan.mp):
        out = [blocks[k].astype(LOW) for blocks in products]
        out = out[0] if len(out) == 1 else jnp.concatenate(out, axis=1)
        outs.append(out)
        received.append(links.shift(after(out, *tokens), k, 0))
    result, at = [], 0
    for blocks in products:
        total = blocks[0]
        for part in received:
            total = total + part[:, at : at + total.shape[1]].astype(jnp.float32)
        result.append(total)
        at += total.shape[1]
    return result, outs


def reduce_blocks(blocks):
    return lax.psum_scatter(jnp.stack(blocks), "mp", scatter_dimension=0, tiled=False)


def after(value, *tokens):
    if not tokens:
        return value
    return lax.optimization_barrier((value, *tokens))[0]


def split_dot(left, top, bottom):
    half = top.shape[0]
    return dot(left[:, :half], top, (1, 0)) + dot(left[:, half:], bottom, (1, 0))


A_X2 = 1
A_CORE = 0
A_DOWN = 1
B_DOWN = 1
B_UADD = 1
Z_LAST = 1
D_SUMS = 1
MEGA = 1 << 20
LOG2E = 1.4426950408889634
VM_FWD = 36
VM_UP = 20
VM_DOWN = 20
VM_BACK = 32
VM_BWD = 36
VM_ENTER = 20


def params(limit=56):
    return pltpu.CompilerParams(vmem_limit_bytes=limit * MEGA)


def cost(flops, bytes_accessed, transcendentals=0):
    return pl.CostEstimate(
        flops=int(flops), bytes_accessed=int(bytes_accessed), transcendentals=int(transcendentals)
    )


def whole(*shape):
    return pl.BlockSpec(shape, lambda *_: (0,) * len(shape), pipeline_mode=pl.Buffered(1))


def statistics(values):
    mean = jnp.mean(values, axis=-1, keepdims=True)
    centred = values - mean
    variance = jnp.mean(centred * centred, axis=-1, keepdims=True)
    return centred, lax.rsqrt(variance + EPSILON)


def norm_rows(values, gain, bias):
    centred, scale = statistics(values)
    return centred * scale * gain + bias


def norm_back(values, gain, grad):
    centred, scale = statistics(values)
    normed = centred * scale
    inner = grad * gain
    first = jnp.mean(inner, axis=-1, keepdims=True)
    second = jnp.mean(inner * normed, axis=-1, keepdims=True)
    return (inner - first - normed * second) * scale, grad * normed, grad


def fold(rows):
    total = rows[:8]
    for i in range(1, rows.shape[0] // 8):
        total = total + rows[i * 8 : i * 8 + 8]
    return total


ROWS = 64


def store_blocks(ref, start, value, table, inverse=None):
    if table is None:
        ref[pl.ds(start, value.shape[0]), :] = value
        return
    count = table.shape[0]
    block = value.shape[1] // count
    for p in range(count):
        at = pl.multiple_of(table[p] * block, block)
        ref[pl.ds(start, value.shape[0]), pl.ds(at, block)] = value[:, p * block : (p + 1) * block]


def load_blocks(ref, start, size, table):
    if table is None:
        return ref[pl.ds(start, size), :]
    count = table.shape[0]
    block = ref.shape[1] // count
    parts = []
    for p in range(count):
        at = pl.multiple_of(table[p] * block, block)
        parts.append(ref[pl.ds(start, size), pl.ds(at, block)])
    return jnp.concatenate(parts, axis=1)


def enter_kernel(blocked):
    def kernel(table_ref, latents, grads, small, entered, entered_grads, grad_z, inputs_a):
        table = table_ref if blocked else None

        @pl.loop(0, latents.shape[0] // ROWS)
        def _(i):
            start = pl.multiple_of(i * ROWS, ROWS)
            at = pl.ds(start, ROWS)
            values = load_blocks(latents, start, ROWS, table)
            entered[at, :] = values
            inputs_a[at, :] = norm_rows(values, small[0:1], small[2:3]).astype(LOW)
            values = load_blocks(grads, start, ROWS, table)
            entered_grads[at, :] = values
            grad_z[at, :] = values.astype(LOW)

    return kernel


def enter_norm(table, blocked, latents, grads, small):
    total, width = latents.shape
    rows = 256
    spec = pl.BlockSpec((rows, width), lambda i, *_: (i, 0))
    shape = lambda kind: jax.ShapeDtypeStruct((total, width), kind)
    return pl.pallas_call(
        enter_kernel(blocked),
        name="enter",
        grid_spec=pltpu.PrefetchScalarGridSpec(
            num_scalar_prefetch=1,
            grid=(total // rows,),
            in_specs=[spec, spec, whole(4, width)],
            out_specs=[spec] * 4,
        ),
        out_shape=[shape(jnp.float32), shape(jnp.float32), shape(LOW), shape(LOW)],
        compiler_params=params(VM_ENTER),
        cost_estimate=cost(total * width * 16, total * width * 20),
    )(table, latents, grads, small)


def attention_weights(q, k, bias, factor):
    scores = dot(q, k, (1, 1)) * (factor * LOG2E) + bias
    peak = jnp.max(scores, axis=-1, keepdims=True)
    weights = jnp.exp2(scores - peak)
    return weights * (1.0 / jnp.sum(weights, axis=-1, keepdims=True))


def window_bias(group_column, key_row):
    span = group_column.shape[0]
    place = lax.broadcasted_iota(jnp.int32, (span, span), 0)
    other = lax.broadcasted_iota(jnp.int32, (span, span), 1)
    allowed = (group_column == key_row) | (place == other)
    return jnp.where(allowed, 0.0, -1e30)


def column_halves(rows, tile, count):
    return (
        pl.BlockSpec((rows, tile), lambda k, *_: (0, jnp.minimum(k, count - 1))),
        pl.BlockSpec((rows, tile), lambda k, *_: (0, jnp.clip(k - count, 0, count - 1))),
    )


def either(step, count, work, first, second):
    @pl.when(step < count)
    def _():
        work(*first)

    @pl.when((step >= count) & (step < 2 * count))
    def _():
        work(*second)


def project(window, w_top, w_bottom, target, index, rows):
    before, own, after = window
    target[0:HALO] = split_dot(before[index], w_top, w_bottom).astype(LOW)
    target[HALO : HALO + rows] = split_dot(own[index], w_top, w_bottom).astype(LOW)
    target[HALO + rows :] = split_dot(after[index], w_top, w_bottom).astype(LOW)


def forward_kernel(rows, steps, local_heads, factor):
    def kernel(before, own, after, top_a, bottom_a, top_b, bottom_b, column, row, start, small,
               saved, attended, resid, inputs_c, bias, total):
        step, index = pl.program_id(0), pl.program_id(1)
        group = local_heads * HEAD_DIM
        wide = 3 * group
        half = top_a.shape[0]
        target = saved.at[0]

        @pl.when(step == 0)
        def _():
            bias[index] = window_bias(column[index], row[index])
            total[index] = jnp.zeros((rows, 2 * half), jnp.float32)

        mine = slice(HALO, HALO + rows)

        def work(top, bottom):
            project((before, own, after), top[:, :wide], bottom[:, :wide], target, index, rows)
            for h in range(local_heads):
                at = slice(h * HEAD_DIM, (h + 1) * HEAD_DIM)
                q = target[mine, at]
                k = target[:, group + h * HEAD_DIM : group + (h + 1) * HEAD_DIM]
                v = target[:, 2 * group + h * HEAD_DIM : 2 * group + (h + 1) * HEAD_DIM]
                p = attention_weights(q, k, bias[index, mine, :], factor).astype(LOW)
                attended[0, :, at] = dot(p, v, (1, 0)).astype(LOW)
            total[index, :, :half] += dot(attended[0], top[:, wide:], (1, 1))
            total[index, :, half:] += dot(attended[0], bottom[:, wide:], (1, 1))

        @pl.when(step < steps // 2)
        def _():
            work(top_a, bottom_a)

        @pl.when(step >= steps // 2)
        def _():
            work(top_b, bottom_b)

        @pl.when(step == steps - 1)
        def _():
            @pl.loop(0, rows // ROWS)
            def _(i):
                at = pl.ds(pl.multiple_of(i * ROWS, ROWS), ROWS)
                values = total[index, at, :] + start[at, :]
                resid[at, :] = values
                inputs_c[at, :] = norm_rows(values, small[1:2], small[3:4]).astype(LOW)

    return kernel


def forward_block(window, weights, column, row, start, small, steps, factor):
    before, own, after = window
    micro, rows, width = own.shape
    span = rows + 2 * HALO
    total = micro * rows
    half = steps // 2
    c = weights[0][0].shape[1] // half
    g = c // 4
    late = pl.BlockSpec((rows, width), lambda k, i: (jnp.where(k == steps - 1, i, 0), 0))
    weight_a, weight_b = column_halves(width // 2, c, half)
    return pl.pallas_call(
        forward_kernel(rows, steps, g // HEAD_DIM, factor),
        name="attention_forward",
        grid=(steps, micro),
        in_specs=[
            whole(*before.shape), whole(*own.shape), whole(*after.shape),
            weight_a, weight_a, weight_b, weight_b,
            whole(*column.shape), whole(*row.shape),
            late,
            whole(4, width),
        ],
        out_specs=[
            pl.BlockSpec((1, span, 3 * g), lambda k, i: (i, 0, k)),
            pl.BlockSpec((1, rows, g), lambda k, i: (k // half, i, k % half)),
            late,
            late,
        ],
        out_shape=[
            jax.ShapeDtypeStruct((micro, span, 3 * g * steps), LOW),
            jax.ShapeDtypeStruct((2, total, g * half), LOW),
            jax.ShapeDtypeStruct((total, width), jnp.float32),
            jax.ShapeDtypeStruct((total, width), LOW),
        ],
        scratch_shapes=[
            pltpu.VMEM((micro, span, span), jnp.float32),
            pltpu.VMEM((micro, rows, width), jnp.float32),
        ],
        compiler_params=params(VM_FWD),
        cost_estimate=cost(
            2 * micro * steps * g * (span * width * 3 + rows * width + 2 * rows * span),
            30 * MEGA,
            micro * rows * span * steps * g // HEAD_DIM,
        ),
    )(before, own, after, *weights[0], *weights[1], column, row, start, small)


def up_kernel(count):
    def kernel(inputs, top_a, bottom_a, top_b, bottom_b, hidden, slope):
        def work(top, bottom):
            u = split_dot(inputs[...], top[...], bottom[...])
            c = 0.7978845608028654
            square = u * u
            t = jnp.tanh(u * (c + c * 0.044715 * square))
            half = 0.5 + 0.5 * t
            hidden[0] = (u * half).astype(LOW)
            inner = 0.5 * c + 1.5 * c * 0.044715 * square
            slope[0] = (half + u * inner * (1.0 - t * t)).astype(LOW)

        either(pl.program_id(0), count, work, (top_a, bottom_a), (top_b, bottom_b))

    return kernel


def feed_up(inputs, weights, tile=512):
    total, width = inputs.shape
    ff = 2 * weights[0][0].shape[1]
    count = ff // 2 // tile
    block = pl.BlockSpec((1, total, tile), lambda j: (j // count, 0, j % count))
    weight_a, weight_b = column_halves(width // 2, tile, count)
    return pl.pallas_call(
        up_kernel(count),
        name="feed_up",
        grid=(ff // tile,),
        in_specs=[whole(total, width), weight_a, weight_a, weight_b, weight_b],
        out_specs=[block, block],
        out_shape=[jax.ShapeDtypeStruct((2, total, ff // 2), LOW)] * 2,
        compiler_params=params(VM_UP),
        cost_estimate=cost(2 * total * width * ff, 2 * (width * ff + 2 * total * ff), total * ff),
    )(inputs, *weights[0], *weights[1])


LATE = 256


def down_kernel(blocked, steps):
    def kernel(table_ref, hidden, top_a, bottom_a, top_b, bottom_b, start_rows, out, total):
        step = pl.program_id(0)
        half = top_a.shape[0]

        @pl.when(step == 0)
        def _():
            total[...] = jnp.zeros_like(total)

        def work(top, bottom):
            total[:, :half] += dot(hidden[0], top[...], (1, 1))
            total[:, half:] += dot(hidden[0], bottom[...], (1, 1))

        either(step, steps // 2, work, (top_a, bottom_a), (top_b, bottom_b))

        @pl.when(step >= steps)
        def _():
            base = (step - steps) * LATE

            @pl.loop(0, LATE // ROWS)
            def _(i):
                start = pl.multiple_of(i * ROWS, ROWS)
                at = pl.ds(pl.multiple_of(base + start, ROWS), ROWS)
                values = total[at, :] + start_rows[pl.ds(start, ROWS), :]
                store_blocks(out, start, values, table_ref if blocked else None)

    return kernel


def feed_down(table, blocked, hidden, weights, start, tile=512):
    total, width = start.shape
    ff = 2 * hidden.shape[2]
    steps = ff // tile
    count = steps // 2
    clip = lambda j: jnp.minimum(j, steps - 1)
    late = pl.BlockSpec((LATE, width), lambda j, *_: (jnp.maximum(j - steps, 0), 0))
    weight_a, weight_b = column_halves(width // 2, tile, count)
    return pl.pallas_call(
        down_kernel(blocked, steps),
        name="feed_down",
        grid_spec=pltpu.PrefetchScalarGridSpec(
            num_scalar_prefetch=1,
            grid=(steps + total // LATE,),
            in_specs=[
                pl.BlockSpec((1, total, tile), lambda j, *_: (clip(j) // count, 0, clip(j) % count)),
                weight_a, weight_a, weight_b, weight_b,
                late,
            ],
            out_specs=late,
            scratch_shapes=[pltpu.VMEM((total, width), jnp.float32)],
        ),
        out_shape=jax.ShapeDtypeStruct((total, width), jnp.float32),
        compiler_params=params(VM_DOWN),
        cost_estimate=cost(2 * total * width * ff, 2 * (width * ff + total * ff) + 8 * total * width),
    )(table, hidden, *weights[0], *weights[1], start)


def slope_kernel(count):
    def kernel(grad_z, top_a, bottom_a, top_b, bottom_b, slope, grad_upward):
        def work(top, bottom):
            grad = split_dot(grad_z[...], top[...], bottom[...]) * slope[0].astype(jnp.float32)
            grad_upward[0] = grad.astype(LOW)

        either(pl.program_id(0), count, work, (top_a, bottom_a), (top_b, bottom_b))

    return kernel


def feed_slope(grad_z, down, slope, tile=512):
    total, width = grad_z.shape
    ff = 2 * slope.shape[2]
    count = ff // 2 // tile
    block = pl.BlockSpec((1, total, tile), lambda j: (j // count, 0, j % count))
    weight_a, weight_b = column_halves(width // 2, tile, count)
    return pl.pallas_call(
        slope_kernel(count),
        name="feed_slope",
        grid=(ff // tile,),
        in_specs=[whole(total, width), weight_a, weight_a, weight_b, weight_b, block],
        out_specs=block,
        out_shape=jax.ShapeDtypeStruct((2, total, ff // 2), LOW),
        compiler_params=params(VM_UP),
        cost_estimate=cost(2 * total * width * ff, 2 * (width * ff + 2 * total * ff)),
    )(grad_z, *down[0], *down[1], slope)


def feed_back_kernel(steps):
    def kernel(upward, top_a, bottom_a, top_b, bottom_b, resid, grads, small,
               grad_resid, grad_branch, sums, total):
        step = pl.program_id(0)
        half = top_a.shape[0]

        @pl.when(step == 0)
        def _():
            total[...] = jnp.zeros_like(total)
            sums[...] = jnp.zeros_like(sums)

        def work(top, bottom):
            total[:, :half] += dot(upward[0], top[...], (1, 1))
            total[:, half:] += dot(upward[0], bottom[...], (1, 1))

        either(step, steps // 2, work, (top_a, bottom_a), (top_b, bottom_b))

        @pl.when(step >= steps)
        def _():
            base = (step - steps) * LATE

            @pl.loop(0, LATE // ROWS)
            def _(i):
                start = pl.multiple_of(i * ROWS, ROWS)
                at = pl.ds(start, ROWS)
                grad = total[pl.ds(pl.multiple_of(base + start, ROWS), ROWS), :]
                back, by_gain, by_bias = norm_back(resid[at, :], small[1:2], grad)
                back = back + grads[at, :]
                grad_resid[at, :] = back
                grad_branch[at, :] = back.astype(LOW)
                sums[0:8] += fold(by_gain)
                sums[8:16] += fold(by_bias)

    return kernel


def feed_back(upward, up, resid, grads, small, tile=512):
    total, width = resid.shape
    ff = 2 * upward.shape[2]
    steps = ff // tile
    count = steps // 2
    clip = lambda j: jnp.minimum(j, steps - 1)
    weight_a, weight_b = column_halves(width // 2, tile, count)
    block = pl.BlockSpec((1, total, tile), lambda j: (clip(j) // count, 0, clip(j) % count))
    late = pl.BlockSpec((LATE, width), lambda j: (jnp.maximum(j - steps, 0), 0))
    return pl.pallas_call(
        feed_back_kernel(steps),
        name="feed_back",
        grid=(steps + total // LATE,),
        in_specs=[block, weight_a, weight_a, weight_b, weight_b, late, late, whole(4, width)],
        out_specs=[late, late, whole(16, width)],
        out_shape=[
            jax.ShapeDtypeStruct((total, width), jnp.float32),
            jax.ShapeDtypeStruct((total, width), LOW),
            jax.ShapeDtypeStruct((16, width), jnp.float32),
        ],
        scratch_shapes=[pltpu.VMEM((total, width), jnp.float32)],
        compiler_params=params(VM_DOWN),
        cost_estimate=cost(2 * total * width * ff, 2 * (width * ff + total * ff) + 14 * total * width),
    )(upward, *up[0], *up[1], resid, grads, small)


def backward_kernel(rows, steps, local_heads, factor):
    def kernel(before, own, after, top_a, bottom_a, top_b, bottom_b, column, row, saved,
               grad_projected, out, bias, grad_att):
        step, index = pl.program_id(0), pl.program_id(1)
        group = local_heads * HEAD_DIM
        wide = 3 * group
        half = top_a.shape[0]
        at_rows = pl.ds(pl.multiple_of(index * rows, rows), rows)

        @pl.when(step == 0)
        def _():
            bias[index] = window_bias(column[index], row[index])
            out[at_rows, :] = jnp.zeros((rows, 2 * half), jnp.float32)

        mine = slice(HALO, HALO + rows)

        def work(top, bottom):
            project((before, own, after), top[:, wide:], bottom[:, wide:], grad_att, index, rows)
            for h in range(local_heads):
                at = slice(h * HEAD_DIM, (h + 1) * HEAD_DIM)
                at_k = slice(group + h * HEAD_DIM, group + (h + 1) * HEAD_DIM)
                at_v = slice(2 * group + h * HEAD_DIM, 2 * group + (h + 1) * HEAD_DIM)
                q, k, v = saved[0, :, at], saved[0, :, at_k], saved[0, :, at_v]
                grad_mix = grad_att[:, at]
                p = attention_weights(q, k, bias[index], factor)
                grad_p = dot(grad_mix, v, (1, 1))
                weighted = jnp.sum(p * grad_p, axis=-1, keepdims=True)
                grad_s = (p * (grad_p - weighted)).astype(LOW)
                grad_projected[0, :, at] = (dot(grad_s[mine], k, (1, 0)) * factor).astype(LOW)
                grad_projected[0, :, at_k] = (dot(grad_s[:, mine], q, (0, 0)) * factor).astype(LOW)
                grad_projected[0, :, at_v] = dot(p[:, mine].astype(LOW), grad_mix, (0, 0)).astype(LOW)
            out[at_rows, :half] += dot(grad_projected[0], top[:, :wide], (1, 1))
            out[at_rows, half:] += dot(grad_projected[0], bottom[:, :wide], (1, 1))

        either(step, steps // 2, work, (top_a, bottom_a), (top_b, bottom_b))

    return kernel


def backward_block(window, weights, column, row, saved, steps, factor):
    before, own, after = window
    micro, rows, width = own.shape
    span = rows + 2 * HALO
    total = micro * rows
    half = steps // 2
    c = weights[0][0].shape[1] // half
    g = c // 4
    weight_a, weight_b = column_halves(width // 2, c, half)
    return pl.pallas_call(
        backward_kernel(rows, steps, g // HEAD_DIM, factor),
        name="attention_backward",
        grid=(steps, micro),
        in_specs=[
            whole(*before.shape), whole(*own.shape), whole(*after.shape),
            weight_a, weight_a, weight_b, weight_b,
            whole(*column.shape), whole(*row.shape),
            pl.BlockSpec((1, span, 3 * g), lambda k, i: (i, 0, k)),
        ],
        out_specs=[
            pl.BlockSpec((1, rows, 3 * g), lambda k, i: (k // half, i, k % half)),
            whole(total, width),
        ],
        scratch_shapes=[
            pltpu.VMEM((micro, span, span), jnp.float32),
            pltpu.VMEM((span, g), LOW),
        ],
        out_shape=[
            jax.ShapeDtypeStruct((2, total, 3 * g * half), LOW),
            jax.ShapeDtypeStruct((total, width), jnp.float32),
        ],
        compiler_params=params(VM_BWD),
        cost_estimate=cost(
            2 * micro * steps * g * (span * width + rows * width * 3 + 4 * span * span),
            35 * MEGA,
            micro * span * span * steps * g // HEAD_DIM,
        ),
    )(before, own, after, *weights[0], *weights[1], column, row, saved)


def leave_kernel(blocked):
    def kernel(table_ref, norm_one, entered, grad_resid, small, latents_grad, sums):
        @pl.when(pl.program_id(0) == 0)
        def _():
            sums[...] = jnp.zeros_like(sums)

        @pl.loop(0, entered.shape[0] // ROWS)
        def _(i):
            start = pl.multiple_of(i * ROWS, ROWS)
            at = pl.ds(start, ROWS)
            back, by_gain, by_bias = norm_back(entered[at, :], small[0:1], norm_one[at, :])
            store_blocks(latents_grad, start, back + grad_resid[at, :], table_ref if blocked else None)
            sums[0:8] += fold(by_gain)
            sums[8:16] += fold(by_bias)

    return kernel


def leave_norm(table, blocked, norm_one, entered, grad_resid, small):
    total, width = entered.shape
    rows = 128
    spec = pl.BlockSpec((rows, width), lambda i, *_: (i, 0))
    return pl.pallas_call(
        leave_kernel(blocked),
        name="leave",
        grid_spec=pltpu.PrefetchScalarGridSpec(
            num_scalar_prefetch=1,
            grid=(total // rows,),
            in_specs=[spec, spec, spec, whole(4, width)],
            out_specs=[spec, whole(16, width)],
        ),
        out_shape=[
            jax.ShapeDtypeStruct((total, width), jnp.float32),
            jax.ShapeDtypeStruct((16, width), jnp.float32),
        ],
        compiler_params=params(VM_ENTER),
        cost_estimate=cost(total * width * 30, total * width * 16),
    )(table, norm_one, entered, grad_resid, small)


def solution(mesh):
    plan = Plan(mesh)

    def body(latents, group_ids, pad_mask, w_qkv, w_out, w_up, w_down, norm_gain, norm_bias, out_grad):
        micro, rows, width = latents.shape
        total = micro * rows
        mp = plan.mp
        factor = HEAD_DIM ** (-0.5)
        links = Links(plan.dp, mp)
        small = jnp.concatenate([norm_gain, norm_bias], axis=0).T
        small = plan.gather_small(links, small).T.astype(jnp.float32)

        blocked = width // plan.dp % 128 == 0
        table = plan.own() ^ jnp.array(plan.relative, jnp.int32)
        rows_in = (latents.reshape(total, width), out_grad.reshape(total, width))
        if not blocked:
            rows_in = tuple(plan.enter(v) for v in rows_in)
        local = jnp.concatenate([w_qkv[0], w_qkv[1], w_qkv[2], w_out], axis=1)

        def columns_of(weight):
            columns = lax.all_gather(weight, "mp", axis=0)
            return plan.halves([columns[k] for k in range(mp)])

        halves = plan.spread_columns(links, local)
        gather_attention = Gather(plan, links, halves)
        up_halves = columns_of(w_up)
        entered, grad_rows, grad_z, inputs_a = enter_norm(table, blocked, *rows_in, small)
        gather_attention.steps_but_last([small])
        window = links.halo(inputs_a.reshape(micro, rows, width))
        down_halves = columns_of(w_down)
        halos = [window[0], window[2]]
        gather_attention.step(halos if A_X2 else [inputs_a], [inputs_a])
        gather_up = Gather(plan, links, up_halves)
        gather_down = Gather(plan, links, down_halves)
        tokens_up = gather_up.steps_but_last([inputs_a])
        gather_attention.hold(tokens_up + halos if A_CORE else halos)
        attention = gather_attention.finish()

        span = rows + 2 * HALO
        first = lax.axis_index("mp") * rows
        pads = ((0, 0), (HALO, HALO))
        groups = jnp.pad(group_ids[:, 0], pads, constant_values=-1)
        keys = jnp.where(jnp.pad(pad_mask[:, 0], pads) == 1, groups, -2)
        groups = lax.dynamic_slice_in_dim(groups, first, span, 1)
        keys = lax.dynamic_slice_in_dim(keys, first, span, 1)
        column, row = groups[:, :, None], keys[:, None, :]

        saved, attended, resid, inputs_c = forward_block(
            window, attention, after(column, *tokens_up, *down_halves), row, entered, small, mp, factor
        )
        early_down = gather_down.steps_but_last()
        gather_up.step()
        gather_up.hold([inputs_c] + early_down * A_DOWN)
        up = gather_up.finish()
        late_down = gather_down.step()
        hidden, slope = feed_up(after(inputs_c, *early_down), up)
        gather_down.hold([hidden])
        down = gather_down.finish()
        left = after(grad_z, *late_down) if B_DOWN else grad_z
        grad_down = Scatter(plan, links, [(left, [hidden[0], hidden[1]])])
        sent = grad_down.core(0) + grad_down.core(1)
        upward = feed_slope(after(grad_z, *sent), down, slope)
        for i in range(2):
            grad_down.hold(i, [upward])
        tokens = [grad_down.steps_but_last(i) for i in range(2)]
        left = after(inputs_c, *tokens)
        grad_up = Scatter(plan, links, [(left, [upward[0], upward[1]])])
        tokens = tokens + grad_up.core(0) + grad_up.core(1)
        if B_UADD:
            tokens += grad_up.add(0) + grad_up.add(1)
        grad_resid, grad_branch, sums_two = feed_back(
            upward, up, after(resid, *tokens), grad_rows, small
        )
        branch = links.halo(grad_branch.reshape(micro, rows, width))
        halos = [branch[0], branch[2]]
        for i in range(2):
            grad_down.hold(i, [grad_branch])
        tokens = [grad_down.step(i) for i in range(2)]
        latents_out = feed_down(table, blocked, after(hidden, *tokens), down, resid)
        for i in range(2):
            grad_down.hold(i, [latents_out])
        tokens = halos + [latents_out]
        left = after(grad_branch, *tokens)
        grad_out = Scatter(plan, links, [(left, [attended[0], attended[1]])])
        down_rows = grad_down.rows()[0]
        for i in range(2):
            if not B_UADD:
                grad_up.hold(i, [latents_out])
            grad_out.core(i)
            grad_up.kept[i] += grad_out.kept[i]
        tokens = [grad_up.steps_but_last(i) for i in range(2)]
        projected, norm_one = backward_block(
            branch, attention, after(column, *tokens, *down_rows), row, saved, mp, factor
        )
        grad_down = reduce_blocks(down_rows)
        for i in range(2):
            grad_up.hold(i, [norm_one])
        tokens = [grad_up.step(i) for i in range(2)]
        left = after(inputs_a, *tokens)
        grad_qkv = Scatter(plan, links, [(left, [projected[0], projected[1]])])
        grad_qkv.core(0)
        grad_qkv.core(1)
        tokens += [grad_qkv.steps_but_last(i) for i in range(2)]
        latents_grad, sums_one = leave_norm(
            table, blocked, after(norm_one, *tokens), entered, grad_resid, small
        )
        for i in range(2):
            grad_up.hold(i, [latents_grad])
        up_rows, out_rows = grad_up.rows()
        (grad_up,), outs = shift_blocks(plan, links, [own_first(up_rows)])
        for i in range(2):
            grad_qkv.hold(i, outs)
        tokens = [grad_qkv.step(i) for i in range(2)]
        qkv_rows = grad_qkv.rows()[0]
        (grad_qkv, grad_out), outs = shift_blocks(
            plan, links, [qkv_rows, out_rows], [grad_up] if Z_LAST else []
        )
        sums = jnp.stack([sums_one, sums_two], axis=0).reshape(2, 2, 8, width).sum(axis=2)
        sums = sums.transpose(1, 0, 2).reshape(4, width).T
        sums = after(sums, *(tokens if D_SUMS == 1 else outs if D_SUMS == 3 else [grad_up]))
        for bit in plan.major:
            middle = sums.shape[0] // 2
            sums = sums[:middle] + links.swap(sums[middle:], bit, 0)
        for bit in [1 << i for i in range(mp.bit_length() - 1)]:
            sums = sums + lax.ppermute(sums, "mp", [(i, i ^ bit) for i in range(mp)])
        grad_qkv = jnp.stack(jnp.split(grad_qkv, 3, axis=1))
        sums = sums.T
        if not blocked:
            latents_out, latents_grad = plan.leave(latents_out), plan.leave(latents_grad)
        shape = latents.shape
        return (
            latents_out.reshape(shape),
            latents_grad.reshape(shape),
            grad_qkv,
            grad_out,
            grad_up,
            grad_down,
            sums[:2],
            sums[2:],
        )

    return jax.shard_map(
        body,
        mesh=mesh,
        in_specs=(
            P(None, ("dp", "mp"), None),
            P(None, "dp", None),
            P(None, "dp", None),
            P(None, "dp", "mp"),
            P("dp", "mp"),
            P("dp", "mp"),
            P("dp", "mp"),
            P(None, "dp"),
            P(None, "dp"),
            P(None, ("dp", "mp"), None),
        ),
        out_specs=(
            P(None, ("dp", "mp"), None),
            P(None, ("dp", "mp"), None),
            P(None, "dp", "mp"),
            P("dp", "mp"),
            P("dp", "mp"),
            P("dp", "mp"),
            P(None, "dp"),
            P(None, "dp"),
        ),
        check_vma=False,
    )
```

```python
import jax
import jax.numpy as jnp
from jax import lax
from jax.experimental import pallas as pl
from jax.experimental.pallas import tpu as pltpu
from jax.sharding import PartitionSpec as P

HEAD_DIM = 128
HALO = 128
EPSILON = 1e-05
LOW = jnp.bfloat16


def dot(left, right, dims, kind=jnp.float32):
    return lax.dot_general(
        left, right, ((dims[:1], dims[1:]), ((), ())), preferred_element_type=kind
    )


class Links:
    def __init__(self, dp, mp):
        self.dp, self.mp = dp, mp
        self.last = {}

    def send(self, value, axis, pairs, link, depth):
        before = self.last.setdefault(link, [])
        if depth and len(before) >= depth:
            value, _ = lax.optimization_barrier((value, before[-depth]))
        result = lax.ppermute(value, axis, pairs)
        before.append(result)
        return result

    def swap(self, value, bit, depth=None):
        return self.send(value, "dp", [(i, i ^ bit) for i in range(self.dp)], bit, 0)

    def shift(self, value, step, depth=3):
        pairs = [(i, (i + step) % self.mp) for i in range(self.mp)]
        return self.send(value, "mp", pairs, "z", depth)

    def halo(self, value, depth=0):
        count = self.mp
        before = self.send(value[:, -HALO:], "mp", [(i, i + 1) for i in range(count - 1)], "z", depth)
        after = self.send(value[:, :HALO], "mp", [(i + 1, i) for i in range(count - 1)], "z", depth)
        return before, value, after


class Plan:
    def __init__(self, mesh):
        self.dp = mesh.shape["dp"]
        self.mp = mesh.shape["mp"]
        bits = [1 << i for i in range(self.dp.bit_length() - 1)]
        core, others = bits[:1], bits[1:]
        self.orders = (others + core, others[::-1] + core)
        self.major = core + others[::-1]
        relative = [0]
        for bit in self.major[::-1]:
            relative = relative + [r ^ bit for r in relative]
        self.relative = relative

    def own(self):
        return lax.axis_index("dp")

    def enter(self, value):
        width = value.shape[-1] // self.dp
        axis = value.ndim - 1
        return jnp.concatenate(
            [
                lax.dynamic_slice_in_dim(value, (self.own() ^ r) * width, width, axis)
                for r in self.relative
            ],
            axis=axis,
        )

    def leave(self, value):
        width = value.shape[-1] // self.dp
        axis = value.ndim - 1
        inverse = {r: p for p, r in enumerate(self.relative)}
        table = jnp.array([inverse[r] for r in range(self.dp)], jnp.int32)
        return jnp.concatenate(
            [
                lax.dynamic_slice_in_dim(value, table[self.own() ^ n] * width, width, axis)
                for n in range(self.dp)
            ],
            axis=axis,
        )

    def gather_small(self, links, value):
        for bit in self.major[::-1]:
            value = jnp.concatenate([value, links.swap(value, bit, 0)], axis=0)
        return value

    def spread_columns(self, links, local):
        parts = [local] + [links.shift(local, -k, 0) for k in range(1, self.mp)]
        return self.halves(parts)

    def halves(self, parts):
        half = self.mp // 2
        return [jnp.concatenate(parts[i * half : (i + 1) * half], axis=1) for i in range(2)]


class Gather:
    def __init__(self, plan, links, held):
        self.plan, self.links = plan, links
        self.block = held[0].shape[0]
        self.held = [[h] for h in held]
        self.known = [[0], [0]]
        self.steps = [list(order[:-1]) for order in plan.orders]

    def pieces(self, i, order):
        span = self.held[i][0].shape[0] // self.block
        at = [self.known[i].index(r) for r in order]
        pieces = []
        while at:
            n = at.pop(0)
            count = 1
            while at and at[0] == n + count and (n + count) % span:
                at.pop(0)
                count += 1
            held = self.held[i][n // span]
            first = n % span * self.block
            pieces.append(held if count == span else held[first : first + count * self.block])
        return pieces

    def join(self, i, order):
        pieces = self.pieces(i, order)
        return pieces[0] if len(pieces) == 1 else jnp.concatenate(pieces, axis=0)

    def step(self, tokens=(), second=()):
        for i in range(2):
            bit = self.steps[i][0]
            value = self.join(i, self.known[i])
            value = after(value, *(second if i else tokens))
            self.held[i] = [value, self.links.swap(value, bit)]
            self.known[i] = self.known[i] + [r ^ bit for r in self.known[i]]
            self.steps[i] = self.steps[i][1:]
        return [h[1] for h in self.held]

    def steps_but_last(self, tokens=()):
        received = []
        while len(self.steps[0]) > 1:
            received = self.step(tokens, tokens)
        return received

    def hold(self, tokens):
        for i in range(2):
            self.held[i][1] = after(self.held[i][1], *tokens)

    def finish(self):
        order = self.plan.relative[: self.plan.dp // 2]
        mine = [self.join(i, order) for i in range(2)]
        return [(m, self.links.swap(m, self.plan.major[0])) for m in mine]


class Scatter:
    def __init__(self, plan, links, pairs):
        self.plan, self.links = plan, links
        self.pairs = pairs
        self.kept = [None, None]
        self.bits = [list(order[:-1][::-1]) for order in plan.orders]
        self.remain = [list(plan.major[1:]), list(plan.major[1:])]

    def core(self, i):
        self.kept[i], outs = [], []
        for left, rights in self.pairs:
            middle = left.shape[1] // 2
            sent = dot(left[:, middle:], rights[i], (0, 0)).astype(LOW)
            kept = dot(left[:, :middle], rights[i], (0, 0))
            self.kept[i].append((kept, self.links.swap(sent, self.plan.major[0]), 0))
            outs.append(sent)
        return outs

    def hold(self, i, tokens):
        self.kept[i] = [(k, after(r, *tokens), at) for k, r, at in self.kept[i]]

    def add(self, i):
        self.kept[i] = [
            k[0] + k[1][:, k[2] : k[2] + k[0].shape[1]].astype(jnp.float32) if isinstance(k, tuple) else k
            for k in self.kept[i]
        ]
        return self.kept[i]

    def step(self, i, tokens=()):
        values = self.add(i)
        bit = self.bits[i].pop(0)
        block = values[0].shape[0] >> (self.remain[i].index(bit) + 1)
        shaped = [v.reshape(-1, 2, block, v.shape[1]) for v in values]
        out = [x[:, 1].reshape(-1, v.shape[1]).astype(LOW) for x, v in zip(shaped, values)]
        stay = [x[:, 0].reshape(-1, v.shape[1]) for x, v in zip(shaped, values)]
        out = out[0] if len(out) == 1 else jnp.concatenate(out, axis=1)
        received = self.links.swap(after(out, *tokens), bit)
        self.kept[i], at = [], 0
        for x in stay:
            self.kept[i].append((x, received, at))
            at += x.shape[1]
        self.remain[i].remove(bit)
        return out

    def steps_but_last(self, i, tokens=()):
        out = None
        while len(self.bits[i]) > 1:
            out = self.step(i, tokens)
        return out

    def rows(self):
        half = self.plan.mp // 2
        result = []
        for pair in zip(*[self.add(i) for i in range(2)]):
            width = pair[0].shape[1] // half
            result.append([r[:, j * width : (j + 1) * width] for r in pair for j in range(half)])
        return result


def own_first(blocks):
    joined = jnp.stack(blocks)
    own = lax.axis_index("mp")
    return [
        lax.dynamic_index_in_dim(joined, lax.rem(own + k, len(blocks)), 0, keepdims=False)
        for k in range(len(blocks))
    ]


def shift_blocks(plan, links, products, tokens=()):
    outs, received = [], []
    for k in range(1, plan.mp):
        out = [blocks[k].astype(LOW) for blocks in products]
        out = out[0] if len(out) == 1 else jnp.concatenate(out, axis=1)
        outs.append(out)
        received.append(links.shift(after(out, *tokens), k, 0))
    result, at = [], 0
    for blocks in products:
        total = blocks[0]
        for part in received:
            total = total + part[:, at : at + total.shape[1]].astype(jnp.float32)
        result.append(total)
        at += total.shape[1]
    return result, outs


def reduce_blocks(blocks):
    return lax.psum_scatter(jnp.stack(blocks), "mp", scatter_dimension=0, tiled=False)


def after(value, *tokens):
    if not tokens:
        return value
    return lax.optimization_barrier((value, *tokens))[0]


def split_dot(left, top, bottom):
    half = top.shape[0]
    return dot(left[:, :half], top, (1, 0)) + dot(left[:, half:], bottom, (1, 0))


A_X2 = 2
A_CORE = 0
A_DOWN = 1
B_DOWN = 1
B_UADD = 1
Z_LAST = 1
D_SUMS = 1
MEGA = 1 << 20
LOG2E = 1.4426950408889634
VM_FWD = 36
VM_UP = 20
VM_DOWN = 20
VM_BACK = 32
VM_BWD = 36
VM_ENTER = 20


def params(limit=56):
    return pltpu.CompilerParams(vmem_limit_bytes=limit * MEGA)


def cost(flops, bytes_accessed, transcendentals=0):
    return pl.CostEstimate(
        flops=int(flops), bytes_accessed=int(bytes_accessed), transcendentals=int(transcendentals)
    )


def whole(*shape):
    return pl.BlockSpec(shape, lambda *_: (0,) * len(shape), pipeline_mode=pl.Buffered(1))


def statistics(values):
    mean = jnp.mean(values, axis=-1, keepdims=True)
    centred = values - mean
    variance = jnp.mean(centred * centred, axis=-1, keepdims=True)
    return centred, lax.rsqrt(variance + EPSILON)


def norm_rows(values, gain, bias):
    centred, scale = statistics(values)
    return centred * scale * gain + bias


def norm_back(values, gain, grad):
    centred, scale = statistics(values)
    normed = centred * scale
    inner = grad * gain
    first = jnp.mean(inner, axis=-1, keepdims=True)
    second = jnp.mean(inner * normed, axis=-1, keepdims=True)
    return (inner - first - normed * second) * scale, grad * normed, grad


def fold(rows):
    total = rows[:8]
    for i in range(1, rows.shape[0] // 8):
        total = total + rows[i * 8 : i * 8 + 8]
    return total


ROWS = 64


def store_blocks(ref, start, value, table, inverse=None):
    if table is None:
        ref[pl.ds(start, value.shape[0]), :] = value
        return
    count = table.shape[0]
    block = value.shape[1] // count
    for p in range(count):
        at = pl.multiple_of(table[p] * block, block)
        ref[pl.ds(start, value.shape[0]), pl.ds(at, block)] = value[:, p * block : (p + 1) * block]


def load_blocks(ref, start, size, table):
    if table is None:
        return ref[pl.ds(start, size), :]
    count = table.shape[0]
    block = ref.shape[1] // count
    parts = []
    for p in range(count):
        at = pl.multiple_of(table[p] * block, block)
        parts.append(ref[pl.ds(start, size), pl.ds(at, block)])
    return jnp.concatenate(parts, axis=1)


def enter_kernel(blocked):
    def kernel(table_ref, latents, grads, small, entered, entered_grads, grad_z, inputs_a):
        table = table_ref if blocked else None

        @pl.loop(0, latents.shape[0] // ROWS)
        def _(i):
            start = pl.multiple_of(i * ROWS, ROWS)
            at = pl.ds(start, ROWS)
            values = load_blocks(latents, start, ROWS, table)
            entered[at, :] = values
            inputs_a[at, :] = norm_rows(values, small[0:1], small[2:3]).astype(LOW)
            values = load_blocks(grads, start, ROWS, table)
            entered_grads[at, :] = values
            grad_z[at, :] = values.astype(LOW)

    return kernel


def enter_norm(table, blocked, latents, grads, small):
    total, width = latents.shape
    rows = 256
    spec = pl.BlockSpec((rows, width), lambda i, *_: (i, 0))
    shape = lambda kind: jax.ShapeDtypeStruct((total, width), kind)
    return pl.pallas_call(
        enter_kernel(blocked),
        name="enter",
        grid_spec=pltpu.PrefetchScalarGridSpec(
            num_scalar_prefetch=1,
            grid=(total // rows,),
            in_specs=[spec, spec, whole(4, width)],
            out_specs=[spec] * 4,
        ),
        out_shape=[shape(jnp.float32), shape(jnp.float32), shape(LOW), shape(LOW)],
        compiler_params=params(VM_ENTER),
        cost_estimate=cost(total * width * 16, total * width * 20),
    )(table, latents, grads, small)


def attention_weights(q, k, bias, factor):
    scores = dot(q, k, (1, 1)) * (factor * LOG2E) + bias
    peak = jnp.max(scores, axis=-1, keepdims=True)
    weights = jnp.exp2(scores - peak)
    return weights * (1.0 / jnp.sum(weights, axis=-1, keepdims=True))


def window_bias(group_column, key_row):
    span = group_column.shape[0]
    place = lax.broadcasted_iota(jnp.int32, (span, span), 0)
    other = lax.broadcasted_iota(jnp.int32, (span, span), 1)
    allowed = (group_column == key_row) | (place == other)
    return jnp.where(allowed, 0.0, -1e30)


def column_halves(rows, tile, count):
    return (
        pl.BlockSpec((rows, tile), lambda k, *_: (0, jnp.minimum(k, count - 1))),
        pl.BlockSpec((rows, tile), lambda k, *_: (0, jnp.clip(k - count, 0, count - 1))),
    )


def either(step, count, work, first, second):
    @pl.when(step < count)
    def _():
        work(*first)

    @pl.when((step >= count) & (step < 2 * count))
    def _():
        work(*second)


def project(window, w_top, w_bottom, target, index, rows):
    before, own, after = window
    target[0:HALO] = split_dot(before[index], w_top, w_bottom).astype(LOW)
    target[HALO : HALO + rows] = split_dot(own[index], w_top, w_bottom).astype(LOW)
    target[HALO + rows :] = split_dot(after[index], w_top, w_bottom).astype(LOW)


def forward_kernel(rows, steps, local_heads, factor):
    def kernel(before, own, after, top_a, bottom_a, top_b, bottom_b, column, row, start, small,
               saved, attended, resid, inputs_c, bias, total):
        step, index = pl.program_id(0), pl.program_id(1)
        group = local_heads * HEAD_DIM
        wide = 3 * group
        half = top_a.shape[0]
        target = saved.at[0]

        @pl.when(step == 0)
        def _():
            bias[index] = window_bias(column[index], row[index])
            total[index] = jnp.zeros((rows, 2 * half), jnp.float32)

        mine = slice(HALO, HALO + rows)

        def work(top, bottom):
            project((before, own, after), top[:, :wide], bottom[:, :wide], target, index, rows)
            for h in range(local_heads):
                at = slice(h * HEAD_DIM, (h + 1) * HEAD_DIM)
                q = target[mine, at]
                k = target[:, group + h * HEAD_DIM : group + (h + 1) * HEAD_DIM]
                v = target[:, 2 * group + h * HEAD_DIM : 2 * group + (h + 1) * HEAD_DIM]
                p = attention_weights(q, k, bias[index, mine, :], factor).astype(LOW)
                attended[0, :, at] = dot(p, v, (1, 0)).astype(LOW)
            total[index, :, :half] += dot(attended[0], top[:, wide:], (1, 1))
            total[index, :, half:] += dot(attended[0], bottom[:, wide:], (1, 1))

        @pl.when(step < steps // 2)
        def _():
            work(top_a, bottom_a)

        @pl.when(step >= steps // 2)
        def _():
            work(top_b, bottom_b)

        @pl.when(step == steps - 1)
        def _():
            @pl.loop(0, rows // ROWS)
            def _(i):
                at = pl.ds(pl.multiple_of(i * ROWS, ROWS), ROWS)
                values = total[index, at, :] + start[at, :]
                resid[at, :] = values
                inputs_c[at, :] = norm_rows(values, small[1:2], small[3:4]).astype(LOW)

    return kernel


def forward_block(window, weights, column, row, start, small, steps, factor):
    before, own, after = window
    micro, rows, width = own.shape
    span = rows + 2 * HALO
    total = micro * rows
    half = steps // 2
    c = weights[0][0].shape[1] // half
    g = c // 4
    late = pl.BlockSpec((rows, width), lambda k, i: (jnp.where(k == steps - 1, i, 0), 0))
    weight_a, weight_b = column_halves(width // 2, c, half)
    return pl.pallas_call(
        forward_kernel(rows, steps, g // HEAD_DIM, factor),
        name="attention_forward",
        grid=(steps, micro),
        in_specs=[
            whole(*before.shape), whole(*own.shape), whole(*after.shape),
            weight_a, weight_a, weight_b, weight_b,
            whole(*column.shape), whole(*row.shape),
            late,
            whole(4, width),
        ],
        out_specs=[
            pl.BlockSpec((1, span, 3 * g), lambda k, i: (i, 0, k)),
            pl.BlockSpec((1, rows, g), lambda k, i: (k // half, i, k % half)),
            late,
            late,
        ],
        out_shape=[
            jax.ShapeDtypeStruct((micro, span, 3 * g * steps), LOW),
            jax.ShapeDtypeStruct((2, total, g * half), LOW),
            jax.ShapeDtypeStruct((total, width), jnp.float32),
            jax.ShapeDtypeStruct((total, width), LOW),
        ],
        scratch_shapes=[
            pltpu.VMEM((micro, span, span), jnp.float32),
            pltpu.VMEM((micro, rows, width), jnp.float32),
        ],
        compiler_params=params(VM_FWD),
        cost_estimate=cost(
            2 * micro * steps * g * (span * width * 3 + rows * width + 2 * rows * span),
            30 * MEGA,
            micro * rows * span * steps * g // HEAD_DIM,
        ),
    )(before, own, after, *weights[0], *weights[1], column, row, start, small)


def up_kernel(count):
    def kernel(inputs, top_a, bottom_a, top_b, bottom_b, hidden, slope):
        def work(top, bottom):
            u = split_dot(inputs[...], top[...], bottom[...])
            c = 0.7978845608028654
            square = u * u
            t = jnp.tanh(u * (c + c * 0.044715 * square))
            half = 0.5 + 0.5 * t
            hidden[0] = (u * half).astype(LOW)
            inner = 0.5 * c + 1.5 * c * 0.044715 * square
            slope[0] = (half + u * inner * (1.0 - t * t)).astype(LOW)

        either(pl.program_id(0), count, work, (top_a, bottom_a), (top_b, bottom_b))

    return kernel


def feed_up(inputs, weights, tile=512):
    total, width = inputs.shape
    ff = 2 * weights[0][0].shape[1]
    count = ff // 2 // tile
    block = pl.BlockSpec((1, total, tile), lambda j: (j // count, 0, j % count))
    weight_a, weight_b = column_halves(width // 2, tile, count)
    return pl.pallas_call(
        up_kernel(count),
        name="feed_up",
        grid=(ff // tile,),
        in_specs=[whole(total, width), weight_a, weight_a, weight_b, weight_b],
        out_specs=[block, block],
        out_shape=[jax.ShapeDtypeStruct((2, total, ff // 2), LOW)] * 2,
        compiler_params=params(VM_UP),
        cost_estimate=cost(2 * total * width * ff, 2 * (width * ff + 2 * total * ff), total * ff),
    )(inputs, *weights[0], *weights[1])


LATE = 256


def down_kernel(blocked, steps):
    def kernel(table_ref, hidden, top_a, bottom_a, top_b, bottom_b, start_rows, out, total):
        step = pl.program_id(0)
        half = top_a.shape[0]

        @pl.when(step == 0)
        def _():
            total[...] = jnp.zeros_like(total)

        def work(top, bottom):
            total[:, :half] += dot(hidden[0], top[...], (1, 1))
            total[:, half:] += dot(hidden[0], bottom[...], (1, 1))

        either(step, steps // 2, work, (top_a, bottom_a), (top_b, bottom_b))

        @pl.when(step >= steps)
        def _():
            base = (step - steps) * LATE

            @pl.loop(0, LATE // ROWS)
            def _(i):
                start = pl.multiple_of(i * ROWS, ROWS)
                at = pl.ds(pl.multiple_of(base + start, ROWS), ROWS)
                values = total[at, :] + start_rows[pl.ds(start, ROWS), :]
                store_blocks(out, start, values, table_ref if blocked else None)

    return kernel


def feed_down(table, blocked, hidden, weights, start, tile=512):
    total, width = start.shape
    ff = 2 * hidden.shape[2]
    steps = ff // tile
    count = steps // 2
    clip = lambda j: jnp.minimum(j, steps - 1)
    late = pl.BlockSpec((LATE, width), lambda j, *_: (jnp.maximum(j - steps, 0), 0))
    weight_a, weight_b = column_halves(width // 2, tile, count)
    return pl.pallas_call(
        down_kernel(blocked, steps),
        name="feed_down",
        grid_spec=pltpu.PrefetchScalarGridSpec(
            num_scalar_prefetch=1,
            grid=(steps + total // LATE,),
            in_specs=[
                pl.BlockSpec((1, total, tile), lambda j, *_: (clip(j) // count, 0, clip(j) % count)),
                weight_a, weight_a, weight_b, weight_b,
                late,
            ],
            out_specs=late,
            scratch_shapes=[pltpu.VMEM((total, width), jnp.float32)],
        ),
        out_shape=jax.ShapeDtypeStruct((total, width), jnp.float32),
        compiler_params=params(VM_DOWN),
        cost_estimate=cost(2 * total * width * ff, 2 * (width * ff + total * ff) + 8 * total * width),
    )(table, hidden, *weights[0], *weights[1], start)


def slope_kernel(count):
    def kernel(grad_z, top_a, bottom_a, top_b, bottom_b, slope, grad_upward):
        def work(top, bottom):
            grad = split_dot(grad_z[...], top[...], bottom[...]) * slope[0].astype(jnp.float32)
            grad_upward[0] = grad.astype(LOW)

        either(pl.program_id(0), count, work, (top_a, bottom_a), (top_b, bottom_b))

    return kernel


def feed_slope(grad_z, down, slope, tile=512):
    total, width = grad_z.shape
    ff = 2 * slope.shape[2]
    count = ff // 2 // tile
    block = pl.BlockSpec((1, total, tile), lambda j: (j // count, 0, j % count))
    weight_a, weight_b = column_halves(width // 2, tile, count)
    return pl.pallas_call(
        slope_kernel(count),
        name="feed_slope",
        grid=(ff // tile,),
        in_specs=[whole(total, width), weight_a, weight_a, weight_b, weight_b, block],
        out_specs=block,
        out_shape=jax.ShapeDtypeStruct((2, total, ff // 2), LOW),
        compiler_params=params(VM_UP),
        cost_estimate=cost(2 * total * width * ff, 2 * (width * ff + 2 * total * ff)),
    )(grad_z, *down[0], *down[1], slope)


def feed_back_kernel(steps):
    def kernel(upward, top_a, bottom_a, top_b, bottom_b, resid, grads, small,
               grad_resid, grad_branch, sums, total):
        step = pl.program_id(0)
        half = top_a.shape[0]

        @pl.when(step == 0)
        def _():
            total[...] = jnp.zeros_like(total)
            sums[...] = jnp.zeros_like(sums)

        def work(top, bottom):
            total[:, :half] += dot(upward[0], top[...], (1, 1))
            total[:, half:] += dot(upward[0], bottom[...], (1, 1))

        either(step, steps // 2, work, (top_a, bottom_a), (top_b, bottom_b))

        @pl.when(step >= steps)
        def _():
            base = (step - steps) * LATE

            @pl.loop(0, LATE // ROWS)
            def _(i):
                start = pl.multiple_of(i * ROWS, ROWS)
                at = pl.ds(start, ROWS)
                grad = total[pl.ds(pl.multiple_of(base + start, ROWS), ROWS), :]
                back, by_gain, by_bias = norm_back(resid[at, :], small[1:2], grad)
                back = back + grads[at, :]
                grad_resid[at, :] = back
                grad_branch[at, :] = back.astype(LOW)
                sums[0:8] += fold(by_gain)
                sums[8:16] += fold(by_bias)

    return kernel


def feed_back(upward, up, resid, grads, small, tile=512):
    total, width = resid.shape
    ff = 2 * upward.shape[2]
    steps = ff // tile
    count = steps // 2
    clip = lambda j: jnp.minimum(j, steps - 1)
    weight_a, weight_b = column_halves(width // 2, tile, count)
    block = pl.BlockSpec((1, total, tile), lambda j: (clip(j) // count, 0, clip(j) % count))
    late = pl.BlockSpec((LATE, width), lambda j: (jnp.maximum(j - steps, 0), 0))
    return pl.pallas_call(
        feed_back_kernel(steps),
        name="feed_back",
        grid=(steps + total // LATE,),
        in_specs=[block, weight_a, weight_a, weight_b, weight_b, late, late, whole(4, width)],
        out_specs=[late, late, whole(16, width)],
        out_shape=[
            jax.ShapeDtypeStruct((total, width), jnp.float32),
            jax.ShapeDtypeStruct((total, width), LOW),
            jax.ShapeDtypeStruct((16, width), jnp.float32),
        ],
        scratch_shapes=[pltpu.VMEM((total, width), jnp.float32)],
        compiler_params=params(VM_DOWN),
        cost_estimate=cost(2 * total * width * ff, 2 * (width * ff + total * ff) + 14 * total * width),
    )(upward, *up[0], *up[1], resid, grads, small)


def backward_kernel(rows, steps, local_heads, factor):
    def kernel(before, own, after, top_a, bottom_a, top_b, bottom_b, column, row, saved,
               grad_projected, out, bias, grad_att):
        step, index = pl.program_id(0), pl.program_id(1)
        group = local_heads * HEAD_DIM
        wide = 3 * group
        half = top_a.shape[0]
        at_rows = pl.ds(pl.multiple_of(index * rows, rows), rows)

        @pl.when(step == 0)
        def _():
            bias[index] = window_bias(column[index], row[index])
            out[at_rows, :] = jnp.zeros((rows, 2 * half), jnp.float32)

        mine = slice(HALO, HALO + rows)

        def work(top, bottom):
            project((before, own, after), top[:, wide:], bottom[:, wide:], grad_att, index, rows)
            for h in range(local_heads):
                at = slice(h * HEAD_DIM, (h + 1) * HEAD_DIM)
                at_k = slice(group + h * HEAD_DIM, group + (h + 1) * HEAD_DIM)
                at_v = slice(2 * group + h * HEAD_DIM, 2 * group + (h + 1) * HEAD_DIM)
                q, k, v = saved[0, :, at], saved[0, :, at_k], saved[0, :, at_v]
                grad_mix = grad_att[:, at]
                p = attention_weights(q, k, bias[index], factor)
                grad_p = dot(grad_mix, v, (1, 1))
                weighted = jnp.sum(p * grad_p, axis=-1, keepdims=True)
                grad_s = (p * (grad_p - weighted)).astype(LOW)
                grad_projected[0, :, at] = (dot(grad_s[mine], k, (1, 0)) * factor).astype(LOW)
                grad_projected[0, :, at_k] = (dot(grad_s[:, mine], q, (0, 0)) * factor).astype(LOW)
                grad_projected[0, :, at_v] = dot(p[:, mine].astype(LOW), grad_mix, (0, 0)).astype(LOW)
            out[at_rows, :half] += dot(grad_projected[0], top[:, :wide], (1, 1))
            out[at_rows, half:] += dot(grad_projected[0], bottom[:, :wide], (1, 1))

        either(step, steps // 2, work, (top_a, bottom_a), (top_b, bottom_b))

    return kernel


def backward_block(window, weights, column, row, saved, steps, factor):
    before, own, after = window
    micro, rows, width = own.shape
    span = rows + 2 * HALO
    total = micro * rows
    half = steps // 2
    c = weights[0][0].shape[1] // half
    g = c // 4
    weight_a, weight_b = column_halves(width // 2, c, half)
    return pl.pallas_call(
        backward_kernel(rows, steps, g // HEAD_DIM, factor),
        name="attention_backward",
        grid=(steps, micro),
        in_specs=[
            whole(*before.shape), whole(*own.shape), whole(*after.shape),
            weight_a, weight_a, weight_b, weight_b,
            whole(*column.shape), whole(*row.shape),
            pl.BlockSpec((1, span, 3 * g), lambda k, i: (i, 0, k)),
        ],
        out_specs=[
            pl.BlockSpec((1, rows, 3 * g), lambda k, i: (k // half, i, k % half)),
            whole(total, width),
        ],
        scratch_shapes=[
            pltpu.VMEM((micro, span, span), jnp.float32),
            pltpu.VMEM((span, g), LOW),
        ],
        out_shape=[
            jax.ShapeDtypeStruct((2, total, 3 * g * half), LOW),
            jax.ShapeDtypeStruct((total, width), jnp.float32),
        ],
        compiler_params=params(VM_BWD),
        cost_estimate=cost(
            2 * micro * steps * g * (span * width + rows * width * 3 + 4 * span * span),
            35 * MEGA,
            micro * span * span * steps * g // HEAD_DIM,
        ),
    )(before, own, after, *weights[0], *weights[1], column, row, saved)


def leave_kernel(blocked):
    def kernel(table_ref, norm_one, entered, grad_resid, small, latents_grad, sums):
        @pl.when(pl.program_id(0) == 0)
        def _():
            sums[...] = jnp.zeros_like(sums)

        @pl.loop(0, entered.shape[0] // ROWS)
        def _(i):
            start = pl.multiple_of(i * ROWS, ROWS)
            at = pl.ds(start, ROWS)
            back, by_gain, by_bias = norm_back(entered[at, :], small[0:1], norm_one[at, :])
            store_blocks(latents_grad, start, back + grad_resid[at, :], table_ref if blocked else None)
            sums[0:8] += fold(by_gain)
            sums[8:16] += fold(by_bias)

    return kernel


def leave_norm(table, blocked, norm_one, entered, grad_resid, small):
    total, width = entered.shape
    rows = 128
    spec = pl.BlockSpec((rows, width), lambda i, *_: (i, 0))
    return pl.pallas_call(
        leave_kernel(blocked),
        name="leave",
        grid_spec=pltpu.PrefetchScalarGridSpec(
            num_scalar_prefetch=1,
            grid=(total // rows,),
            in_specs=[spec, spec, spec, whole(4, width)],
            out_specs=[spec, whole(16, width)],
        ),
        out_shape=[
            jax.ShapeDtypeStruct((total, width), jnp.float32),
            jax.ShapeDtypeStruct((16, width), jnp.float32),
        ],
        compiler_params=params(VM_ENTER),
        cost_estimate=cost(total * width * 30, total * width * 16),
    )(table, norm_one, entered, grad_resid, small)


def solution(mesh):
    plan = Plan(mesh)

    def body(latents, group_ids, pad_mask, w_qkv, w_out, w_up, w_down, norm_gain, norm_bias, out_grad):
        micro, rows, width = latents.shape
        total = micro * rows
        mp = plan.mp
        factor = HEAD_DIM ** (-0.5)
        links = Links(plan.dp, mp)
        small = jnp.concatenate([norm_gain, norm_bias], axis=0).T
        small = plan.gather_small(links, small).T.astype(jnp.float32)

        blocked = width // plan.dp % 128 == 0
        table = plan.own() ^ jnp.array(plan.relative, jnp.int32)
        rows_in = (latents.reshape(total, width), out_grad.reshape(total, width))
        if not blocked:
            rows_in = tuple(plan.enter(v) for v in rows_in)
        local = jnp.concatenate([w_qkv[0], w_qkv[1], w_qkv[2], w_out], axis=1)

        def columns_of(weight):
            columns = lax.all_gather(weight, "mp", axis=0)
            return plan.halves([columns[k] for k in range(mp)])

        halves = plan.spread_columns(links, local)
        gather_attention = Gather(plan, links, halves)
        up_halves = columns_of(w_up)
        entered, grad_rows, grad_z, inputs_a = enter_norm(table, blocked, *rows_in, small)
        gather_attention.steps_but_last([small])
        window = links.halo(inputs_a.reshape(micro, rows, width))
        down_halves = columns_of(w_down)
        halos = [window[0], window[2]]
        gather_attention.step([] if A_X2 == 2 else halos if A_X2 else [inputs_a], [inputs_a])
        gather_up = Gather(plan, links, up_halves)
        gather_down = Gather(plan, links, down_halves)
        tokens_up = gather_up.steps_but_last([inputs_a])
        gather_attention.hold(tokens_up + halos if A_CORE else halos)
        attention = gather_attention.finish()

        span = rows + 2 * HALO
        first = lax.axis_index("mp") * rows
        pads = ((0, 0), (HALO, HALO))
        groups = jnp.pad(group_ids[:, 0], pads, constant_values=-1)
        keys = jnp.where(jnp.pad(pad_mask[:, 0], pads) == 1, groups, -2)
        groups = lax.dynamic_slice_in_dim(groups, first, span, 1)
        keys = lax.dynamic_slice_in_dim(keys, first, span, 1)
        column, row = groups[:, :, None], keys[:, None, :]

        saved, attended, resid, inputs_c = forward_block(
            window, attention, after(column, *tokens_up, *down_halves), row, entered, small, mp, factor
        )
        early_down = gather_down.steps_but_last()
        gather_up.step()
        gather_up.hold([inputs_c] + early_down * A_DOWN)
        up = gather_up.finish()
        late_down = gather_down.step()
        hidden, slope = feed_up(after(inputs_c, *early_down), up)
        gather_down.hold([hidden])
        down = gather_down.finish()
        left = after(grad_z, *late_down) if B_DOWN else grad_z
        grad_down = Scatter(plan, links, [(left, [hidden[0], hidden[1]])])
        sent = grad_down.core(0) + grad_down.core(1)
        upward = feed_slope(after(grad_z, *sent), down, slope)
        for i in range(2):
            grad_down.hold(i, [upward])
        tokens = [grad_down.steps_but_last(i) for i in range(2)]
        left = after(inputs_c, *tokens)
        grad_up = Scatter(plan, links, [(left, [upward[0], upward[1]])])
        tokens = tokens + grad_up.core(0) + grad_up.core(1)
        if B_UADD:
            tokens += grad_up.add(0) + grad_up.add(1)
        grad_resid, grad_branch, sums_two = feed_back(
            upward, up, after(resid, *tokens), grad_rows, small
        )
        branch = links.halo(grad_branch.reshape(micro, rows, width))
        halos = [branch[0], branch[2]]
        for i in range(2):
            grad_down.hold(i, [grad_branch])
        tokens = [grad_down.step(i) for i in range(2)]
        latents_out = feed_down(table, blocked, after(hidden, *tokens), down, resid)
        for i in range(2):
            grad_down.hold(i, [latents_out])
        tokens = halos + [latents_out]
        left = after(grad_branch, *tokens)
        grad_out = Scatter(plan, links, [(left, [attended[0], attended[1]])])
        down_rows = grad_down.rows()[0]
        for i in range(2):
            if not B_UADD:
                grad_up.hold(i, [latents_out])
            grad_out.core(i)
            grad_up.kept[i] += grad_out.kept[i]
        tokens = [grad_up.steps_but_last(i) for i in range(2)]
        projected, norm_one = backward_block(
            branch, attention, after(column, *tokens, *down_rows), row, saved, mp, factor
        )
        grad_down = reduce_blocks(down_rows)
        for i in range(2):
            grad_up.hold(i, [norm_one])
        tokens = [grad_up.step(i) for i in range(2)]
        left = after(inputs_a, *tokens)
        grad_qkv = Scatter(plan, links, [(left, [projected[0], projected[1]])])
        grad_qkv.core(0)
        grad_qkv.core(1)
        tokens += [grad_qkv.steps_but_last(i) for i in range(2)]
        latents_grad, sums_one = leave_norm(
            table, blocked, after(norm_one, *tokens), entered, grad_resid, small
        )
        for i in range(2):
            grad_up.hold(i, [latents_grad])
        up_rows, out_rows = grad_up.rows()
        (grad_up,), outs = shift_blocks(plan, links, [own_first(up_rows)])
        for i in range(2):
            grad_qkv.hold(i, outs)
        tokens = [grad_qkv.step(i) for i in range(2)]
        qkv_rows = grad_qkv.rows()[0]
        (grad_qkv, grad_out), outs = shift_blocks(
            plan, links, [qkv_rows, out_rows], [grad_up] if Z_LAST else []
        )
        sums = jnp.stack([sums_one, sums_two], axis=0).reshape(2, 2, 8, width).sum(axis=2)
        sums = sums.transpose(1, 0, 2).reshape(4, width).T
        sums = after(sums, *(tokens if D_SUMS == 1 else outs if D_SUMS == 3 else [grad_up]))
        for bit in plan.major:
            middle = sums.shape[0] // 2
            sums = sums[:middle] + links.swap(sums[middle:], bit, 0)
        for bit in [1 << i for i in range(mp.bit_length() - 1)]:
            sums = sums + lax.ppermute(sums, "mp", [(i, i ^ bit) for i in range(mp)])
        grad_qkv = jnp.stack(jnp.split(grad_qkv, 3, axis=1))
        sums = sums.T
        if not blocked:
            latents_out, latents_grad = plan.leave(latents_out), plan.leave(latents_grad)
        shape = latents.shape
        return (
            latents_out.reshape(shape),
            latents_grad.reshape(shape),
            grad_qkv,
            grad_out,
            grad_up,
            grad_down,
            sums[:2],
            sums[2:],
        )

    return jax.shard_map(
        body,
        mesh=mesh,
        in_specs=(
            P(None, ("dp", "mp"), None),
            P(None, "dp", None),
            P(None, "dp", None),
            P(None, "dp", "mp"),
            P("dp", "mp"),
            P("dp", "mp"),
            P("dp", "mp"),
            P(None, "dp"),
            P(None, "dp"),
            P(None, ("dp", "mp"), None),
        ),
        out_specs=(
            P(None, ("dp", "mp"), None),
            P(None, ("dp", "mp"), None),
            P(None, "dp", "mp"),
            P("dp", "mp"),
            P("dp", "mp"),
            P("dp", "mp"),
            P(None, "dp"),
            P(None, "dp"),
        ),
        check_vma=False,
    )
```
